256 devices in a mesh: gx: 8 (over z), gy: 4 (over x), gz: 8 (over y, core).
Axes of the slice: x: 4, y: 4, z: 8, core: 2. Of those that a mesh axis runs over, the one named last changes fastest.
Arguments:
- rhs_boxes: float32 [8, 128, 32768], P('gz', ('gx', 'gy')), may hold values from -18 to 18
- a_boxes: float32 [8, 128, 32768], P('gz', ('gx', 'gy')), may hold values from 0.05 to 0.5
- b_boxes: float32 [8, 128, 32768], P('gz', ('gx', 'gy')), may hold values from 0.2 to 2
- new_place: int32 [8, 128], P('gz', ('gx', 'gy')), may hold values from 0 to 127, as said below
Outputs:
- solution: float32 [512, 128, 512], P('gx', 'gy', 'gz')
- residual: float32 [512, 128, 512], P('gx', 'gy', 'gz')
The draws below stay inside these ranges and needn't reach their ends.
Inputs may be any that keep to these rules, and one draw needn't show every extreme that they name: `new_place`: each entry is p = t * 4 + q: the box goes to device t of its layer (counted in the order of the gx+gy axes) at box position q. The entries of one layer are a permutation of its positions. The boxes of one device go to 4 different devices.
All inputs are finite; a program needn't handle non-finite values.
Results may differ from the reference program's by a relative error of at most 0.000079.
Values sent between devices are 32-bit elements; how exact they have to be, the bound alone decides.
No kernel may reach another device: no remote copies, remote signals or barrier semaphores. Data moves between devices by JAX's collectives and lax.ppermute only.
A program may use at most 192 MiB of HBM per device.

```python
import math
import jax
import jax.numpy as jnp
from jax import lax

BOX_EDGE = 32
BOXES_Z = 2
SWEEPS = 1
COARSE_SWEEPS = 4
BOX_CELLS = 32768
BOXES_DEV = 4
MEMBERS = 32
LAYERS = 8
NX = 512
NY = 128
NZ = 512
N_GX = 8
N_GY = 4


def layer_places(key):
    subkeys = jax.random.split(key, 4)
    offsets = jax.random.permutation(subkeys[0], MEMBERS)[:BOXES_DEV]
    relabel = jax.random.permutation(subkeys[1], MEMBERS)
    senders = jax.random.permutation(subkeys[2], MEMBERS)
    target = relabel[(senders[:, None] + offsets[None, :]) % MEMBERS]
    position_keys = jax.random.split(subkeys[3], MEMBERS)
    positions = jax.vmap(lambda one_key: jax.random.permutation(one_key, BOXES_DEV))(position_keys)
    landing = positions[target, jnp.arange(BOXES_DEV)[None, :]]
    return (target * BOXES_DEV + landing).reshape(MEMBERS * BOXES_DEV)


def draw_new_place(key, part):
    subkeys = jax.random.split(jax.random.fold_in(key, 11), LAYERS)
    return jax.vmap(layer_places)(subkeys).astype(jnp.int32)


def draw_rhs_boxes(key, part):
    extent = (LAYERS, MEMBERS * BOXES_DEV, BOX_CELLS)
    values = 3.0 * jax.random.normal(jax.random.fold_in(key, 3), extent, jnp.float32)
    return jnp.clip(values, -18.0, 18.0)


def block_levels(stream_key, shape, shards, smallest, largest):
    def one(dim, shards_of):
        heights = jax.random.uniform(jax.random.fold_in(jax.random.fold_in(stream_key, 6), dim), (shards_of,), jnp.float32, smallest / len(shards), largest / len(shards))
        return jnp.repeat(jnp.exp(heights), shape[dim] // shards_of).reshape((-1,) + (1,) * (len(shape) - dim - 1))

    gain = one(*shards[0])
    for cut in shards[1:]:
        gain = gain * one(*cut)
    return gain


def setup_inputs(seed: int = 0) -> dict:
    keys = jax.random.split(jax.random.key(seed), 5)
    rhs_boxes = draw_rhs_boxes(jax.random.fold_in(keys[4], 71), 0)
    a_boxes = jnp.clip(jnp.exp(math.log(0.5) - 2.3025851 * jax.random.uniform(keys[1], (LAYERS, MEMBERS * BOXES_DEV, BOX_CELLS), jnp.float32) ** block_levels(keys[1], (LAYERS, MEMBERS * BOXES_DEV, BOX_CELLS), ((0, 8), (1, 32)), -0.2, 0.2)), 0.05, 0.5)
    b_boxes = jnp.clip(jnp.exp(math.log(2.0) - 2.3025851 * jax.random.uniform(keys[2], (LAYERS, MEMBERS * BOXES_DEV, BOX_CELLS), jnp.float32) ** block_levels(keys[2], (LAYERS, MEMBERS * BOXES_DEV, BOX_CELLS), ((0, 8), (1, 32)), -0.2, 0.2)), 0.2, 2.0)
    new_place = draw_new_place(jax.random.fold_in(keys[4], 71), 0)
    return {"rhs_boxes": rhs_boxes, "a_boxes": a_boxes, "b_boxes": b_boxes, "new_place": new_place}


def stencil_sum(padded, across_x, across_y, across_z):
    summed = across_x[:-1] * padded[:-2, 1:-1, 1:-1] + across_x[1:] * padded[2:, 1:-1, 1:-1]
    summed = summed + across_y[:, :-1] * padded[1:-1, :-2, 1:-1] + across_y[:, 1:] * padded[1:-1, 2:, 1:-1]
    summed = summed + across_z[:, :, :-1] * padded[1:-1, 1:-1, :-2] + across_z[:, :, 1:] * padded[1:-1, 1:-1, 2:]
    return summed


def face_total(across_x, across_y, across_z):
    return across_x[:-1] + across_x[1:] + across_y[:, :-1] + across_y[:, 1:] + across_z[:, :, :-1] + across_z[:, :, 1:]


def checker(extent):
    return (lax.broadcasted_iota(jnp.int32, extent, 0) + lax.broadcasted_iota(jnp.int32, extent, 1) + lax.broadcasted_iota(jnp.int32, extent, 2)) % 2


def red_black(solution, source, coeffs, sweeps):
    diagonal, across_x, across_y, across_z, weight = coeffs
    colour = checker(solution.shape)
    for repeat in range(sweeps):
        for current in (0, 1):
            padded = jnp.pad(solution, 1)
            updated = (source + weight * stencil_sum(padded, across_x, across_y, across_z)) / diagonal
            solution = jnp.where(colour == current, updated, solution)
    return solution


def misfit(solution, source, coeffs):
    diagonal, across_x, across_y, across_z, weight = coeffs
    padded = jnp.pad(solution, 1)
    return source - (diagonal * solution - weight * stencil_sum(padded, across_x, across_y, across_z))


def restrict(values):
    size_x, size_y, size_z = values.shape
    return values.reshape(size_x // 2, 2, size_y // 2, 2, size_z // 2, 2).mean(axis=(1, 3, 5))


def coarse_faces(across_x, across_y, across_z):
    size_x, size_y, size_z = across_x.shape[0] - 1, across_x.shape[1], across_x.shape[2]
    coarse_x = across_x[0::2].reshape(size_x // 2 + 1, size_y // 2, 2, size_z // 2, 2).mean(axis=(2, 4))
    coarse_y = across_y[:, 0::2].reshape(size_x // 2, 2, size_y // 2 + 1, size_z // 2, 2).mean(axis=(1, 4))
    coarse_z = across_z[:, :, 0::2].reshape(size_x // 2, 2, size_y // 2, 2, size_z // 2 + 1).mean(axis=(1, 3))
    return coarse_x, coarse_y, coarse_z


def prolong(values):
    size_x, size_y, size_z = values.shape
    spread = jnp.broadcast_to(values[:, None, :, None, :, None], (size_x, 2, size_y, 2, size_z, 2))
    return spread.reshape(2 * size_x, 2 * size_y, 2 * size_z)


def place(values, new_place):
    layer_ids = jnp.arange(LAYERS, dtype=jnp.int32)[:, None]
    placed = jnp.zeros_like(values).at[layer_ids, new_place].set(values)
    shaped = placed.reshape(LAYERS, N_GX, N_GY, 2, BOXES_Z, BOX_EDGE, BOX_EDGE, BOX_EDGE)
    return shaped.transpose(1, 3, 5, 2, 6, 0, 4, 7).reshape(NX, NY, NZ)


def reference(rhs_boxes, a_boxes, b_boxes, new_place):
    rhs = place(rhs_boxes, new_place)
    acoef = place(a_boxes, new_place)
    bcoef = place(b_boxes, new_place)
    padded_b = jnp.pad(bcoef, 1)
    across_x = 0.5 * (padded_b[1:, 1:-1, 1:-1] + padded_b[:-1, 1:-1, 1:-1])
    across_y = 0.5 * (padded_b[1:-1, 1:, 1:-1] + padded_b[1:-1, :-1, 1:-1])
    across_z = 0.5 * (padded_b[1:-1, 1:-1, 1:] + padded_b[1:-1, 1:-1, :-1])
    fine_level = (acoef + 1.0 * face_total(across_x, across_y, across_z), across_x, across_y, across_z, 1.0)
    smoothed = red_black(jnp.zeros_like(rhs), rhs, fine_level, SWEEPS)
    coarse_rhs = restrict(misfit(smoothed, rhs, fine_level))
    coarse_x, coarse_y, coarse_z = coarse_faces(across_x, across_y, across_z)
    coarse = (restrict(acoef) + 0.25 * face_total(coarse_x, coarse_y, coarse_z), coarse_x, coarse_y, coarse_z, 0.25)
    correction = red_black(jnp.zeros_like(coarse_rhs), coarse_rhs, coarse, COARSE_SWEEPS)
    solution = red_black(smoothed + prolong(correction), rhs, fine_level, SWEEPS)
    return solution, misfit(solution, rhs, fine_level)
```

```python
import functools

import jax
import jax.numpy as jnp
from jax import lax
from jax.experimental import pallas as pl
from jax.experimental.pallas import tpu as pltpu
from jax.sharding import PartitionSpec as P

LAYER = ("gx", "gy")
F32 = jnp.float32
YR = 40
FXN = 70
CXN = 50
FY0 = 4
CY0 = 12
Z0 = 32


def lane_of(rows):
    return lax.broadcasted_iota(jnp.int32, (rows, 128), 1)


def rl(v, shift):
    shift = shift % 128
    return v if shift == 0 else pltpu.roll(v, shift, 1)


def ry(v, shift):
    return pltpu.roll(v, shift % v.shape[0], 0)


def plane(index, rows=YR):
    if isinstance(index, int):
        return pl.ds(index * rows, rows)
    return pl.ds(pl.multiple_of(index * rows, 8), rows)


def every(start, count, stride):
    return pl.ds(start, count, stride=stride)


def own_lanes(v):
    lane = lane_of(v.shape[0])
    return jnp.where((lane >= Z0) & (lane < Z0 + 64), v, 0.0)


def call(kernel, outs, scratch=(), limit=40, smem=0):
    def run(*args):
        return pl.pallas_call(
            kernel,
            out_shape=[jax.ShapeDtypeStruct(s, F32) for s in outs],
            in_specs=[pl.BlockSpec(memory_space=pltpu.SMEM)] * smem
            + [pl.BlockSpec(memory_space=pltpu.VMEM)] * (len(args) - smem),
            out_specs=[pl.BlockSpec(memory_space=pltpu.VMEM)] * len(outs),
            scratch_shapes=[pltpu.VMEM(s, F32) for s in scratch],
            compiler_params=pltpu.CompilerParams(vmem_limit_bytes=limit << 20),
        )(*args)

    return run


def spread_kernel(place, rhs, a, b, out):
    lane = lane_of(8)
    mark = jnp.zeros((8, 128), F32)
    for k in range(4):
        mark = jnp.where(lane == k, place[0, k].astype(F32), mark)

    @pl.loop(0, 32)
    def _(j):
        for f, src in enumerate((rhs, a, b)):
            for m in range(8):
                col = pl.ds(pl.multiple_of(j * 1024 + m * 128, 128), 128)
                out[j, f * 32 + m * 4 : f * 32 + m * 4 + 4, :] = src[0, :, col]
        out[j, 96:104, :] = mark


def route_kernel(place, got, out):
    @pl.loop(0, 32)
    def _(s):
        for k in range(4):
            p = place[s, k]
            t = lax.shift_right_logical(p, 2)
            q = lax.bitwise_and(p, 3)
            for f in range(3):
                out[t, f * 4 + q] = got[s, every(f * 32 + k, 8, 4), :]


def brick_kernel(got, rh, aa, bb, ylo, yhi, xlo, xhi):
    lane8 = lane_of(8)
    bricks = (rh, aa, bb)
    for br in bricks:
        br[...] = jnp.zeros_like(br)

    @pl.loop(0, 32)
    def _(j):
        for f, br in enumerate(bricks):
            for qx in range(2):
                low = got[j, f * 4 + qx * 2]
                high = got[j, f * 4 + qx * 2 + 1]
                for c in range(4):
                    both = jnp.where(lane8 < 64, rl(low, 32 - 32 * c), rl(high, 64 - 32 * c))
                    start = (j + (qx * 32 + 3)) * YR + (FY0 + c)
                    br[every(start, 8, 4), :] = own_lanes(both)

    lane = lane_of(32)
    for f, br in enumerate(bricks):
        for r in range(3):
            at = pl.ds((f * 3 + r) * 32, 32)
            for dst, y in ((ylo, r), (yhi, 29 + r)):
                first = br[every(3 * YR + FY0 + y, 32, YR), :]
                second = br[every(35 * YR + FY0 + y, 32, YR), :]
                dst[at, :] = jnp.where(lane < 64, rl(first, -32), rl(second, 32))
        xlo[pl.ds(f * 3 * YR, 3 * YR), :] = br[pl.ds(3 * YR, 3 * YR), :]
        xhi[pl.ds(f * 3 * YR, 3 * YR), :] = br[pl.ds(64 * YR, 3 * YR), :]


def fine_x_kernel(xlo, xhi, ylo, yhi, slo, shi, tlo, thi):
    lane = lane_of(YR)
    for own, out, tmp, base, shift in ((xlo, slo, tlo, 0, 32), (xhi, shi, thi, 29, -32)):
        tmp[...] = own[...]
        for f in range(3):
            for r in range(3):
                at = pl.ds((f * 3 + r) * 32 + base, 3)
                tmp[every(f * 3 * YR + FY0 - 3 + r, 3, YR), :] = own_lanes(rl(ylo[at, :], shift))
                tmp[every(f * 3 * YR + FY0 + 32 + r, 3, YR), :] = own_lanes(rl(yhi[at, :], shift))
        for m in range(5):
            v = rl(tmp[plane(2 * m), :], -32)
            w = rl(tmp[plane(2 * m + 1), :], 32) if m < 4 else jnp.zeros_like(v)
            out[plane(m), :] = jnp.where(lane < 64, v, w)


def fine_z_kernel(rh0, aa0, bb0, ylo, yhi, xlo, xhi, rh, aa, bb, zlo, zhi):
    lane = lane_of(YR)
    bricks = (rh, aa, bb)
    for f, (br0, br) in enumerate(zip((rh0, aa0, bb0), bricks)):
        br[...] = br0[...]
        for r in range(3):
            at = pl.ds((f * 3 + r) * 32, 32)
            for src, row in ((ylo, FY0 - 3 + r), (yhi, FY0 + 32 + r)):
                v = src[at, :]
                br[every(3 * YR + row, 32, YR), :] = own_lanes(rl(v, 32))
                br[every(35 * YR + row, 32, YR), :] = own_lanes(rl(v, -32))
        for i in range(3):
            n = f * 3 + i
            shift = 32 if n % 2 == 0 else -32
            br[plane(i), :] = own_lanes(rl(xlo[plane(n // 2), :], shift))
            br[plane(67 + i), :] = own_lanes(rl(xhi[plane(n // 2), :], shift))
    for group in range(5):
        lo = jnp.zeros((YR, 128), F32)
        hi = lo
        for slot in range(14):
            for f, br in enumerate(bricks):
                v = br[plane(group * 14 + slot), :]
                at = 9 * slot + 3 * f
                here = (lane >= at) & (lane < at + 3)
                lo = jnp.where(here, rl(v, at - Z0), lo)
                hi = jnp.where(here, rl(v, at - Z0 - 61), hi)
        zlo[plane(group), :] = lo
        zhi[plane(group), :] = hi


def nb_sum(fxp, fxm, fy, fz, vm, v, vp, step):
    total = fxp * vp + fxm * vm
    total = total + (fy * ry(v, -1) + ry(fy * v, 1))
    return total + (fz * rl(v, -step) + rl(fz * v, step))


def fine_nb(x, fx, fy, fz, v):
    return nb_sum(
        fx[plane(x), :],
        fx[plane(x - 1), :],
        fy[plane(x), :],
        fz[plane(x), :],
        v[plane(x - 1), :],
        v[plane(x), :],
        v[plane(x + 1), :],
        1,
    )


def fine_colour():
    return (lax.broadcasted_iota(jnp.int32, (YR, 128), 0) + lane_of(YR) + 1) % 2


def fine_update(x, colour, base, f, fx, fy, fz, inv, v):
    new = (f[plane(x), :] + fine_nb(x, fx, fy, fz, v)) * inv[plane(x), :]
    v[plane(x), :] = jnp.where((colour + x) % 2 == base, new, v[plane(x), :])


def presmooth_kernel(
    rh0, aa0, bb0, zlo, zhi, f, fx, fy, fz, inv, dg, v, c1, rc, slo, shi, a, b, tmp
):
    lane = lane_of(YR)
    even = lane % 2 == 0
    colour = fine_colour()
    for x in range(FXN):
        for n, (src, dst) in enumerate(((rh0, f), (aa0, a), (bb0, b))):
            at = 9 * (x % 14) + 3 * n
            w = src[plane(x), :]
            lo = rl(zlo[plane(x // 14), :], Z0 - 3 - at)
            hi = rl(zhi[plane(x // 14), :], Z0 + 64 - at)
            w = jnp.where((lane >= Z0 - 3) & (lane < Z0), lo, w)
            dst[plane(x), :] = jnp.where((lane >= Z0 + 64) & (lane < Z0 + 67), hi, w)

    @pl.loop(0, FXN - 1)
    def _(x):
        here = b[plane(x), :]
        fx[plane(x), :] = 0.5 * (here + b[plane(x + 1), :])
        fy[plane(x), :] = 0.5 * (here + ry(here, -1))
        fz[plane(x), :] = 0.5 * (here + rl(here, -1))

    for ref in (fx, fy, fz):
        ref[plane(FXN - 1), :] = jnp.zeros((YR, 128), F32)
    for ref in (inv, dg, v):
        ref[plane(0), :] = jnp.zeros((YR, 128), F32)
        ref[plane(FXN - 1), :] = jnp.zeros((YR, 128), F32)

    @pl.loop(1, FXN - 1)
    def _(x):
        py = fy[plane(x), :]
        pz = fz[plane(x), :]
        ax = a[plane(x), :]
        total = fx[plane(x), :] + fx[plane(x - 1), :] + py + ry(py, 1) + pz + rl(pz, 1)
        diag = ax + total
        inside = ax > 0.0
        one = jnp.where(inside, 1.0 / jnp.where(inside, diag, 1.0), 0.0)
        dg[plane(x), :] = diag
        inv[plane(x), :] = one
        v[plane(x), :] = jnp.where((colour + x) % 2 == 0, f[plane(x), :] * one, 0.0)

    @pl.loop(2, FXN - 2)
    def _(x):
        fine_update(x, colour, 1, f, fx, fy, fz, inv, v)

    even16 = lane_of(16) % 2 == 0
    lane16 = lane_of(16)

    def zpair(s):
        return s + jnp.where(even, rl(s, -1), rl(s, 1))

    def rows(slot, first):
        return tmp[every(slot * YR + first, 16, 2), :]

    def ypair(slot):
        return rows(slot, FY0) + rows(slot, FY0 + 1)

    def miss(x):
        return f[plane(x), :] - (dg[plane(x), :] * v[plane(x), :] - fine_nb(x, fx, fy, fz, v))

    @pl.loop(0, 32)
    def _(i):
        x0 = 2 * i + 3
        x1 = x0 + 1
        tmp[plane(0), :] = zpair(miss(x0) + miss(x1))
        tmp[plane(1), :] = zpair(a[plane(x0), :] + a[plane(x1), :])
        tmp[plane(2), :] = zpair(fx[plane(x1), :])
        tmp[plane(3), :] = zpair(fx[plane(x0 - 1), :])
        tmp[plane(4), :] = zpair(fy[plane(x0), :] + fy[plane(x1), :])
        tmp[plane(5), :] = fz[plane(x0), :] + fz[plane(x1), :]
        rhs = 0.125 * ypair(0)
        acoef = 0.125 * ypair(1)
        fxp = 0.25 * ypair(2)
        fxm = 0.25 * ypair(3)
        fyp = 0.25 * rows(4, FY0 + 1)
        fym = 0.25 * rows(4, FY0 - 1)
        s = 0.25 * ypair(5)
        fzp = jnp.where(even16, rl(s, -1), s)
        fzm = jnp.where(even16, rl(s, 1), rl(s, 2))
        diag = acoef + 0.25 * (fxp + fxm + fyp + fym + fzp + fzm)
        pa = jnp.where(even16, fxp, fyp)
        pb = jnp.where(even16, fzp, diag)
        c1[plane(i, 16), :] = jnp.where(lane16 < 64, rl(pa, -32), rl(pb, 32))
        rc[plane(i, 16), :] = jnp.where(lane16 < 64, rl(rhs, -32), 0.0)

    lane32 = lane_of(32)
    for dst, y0, fine0 in ((slo, 0, 0), (shi, 7, 29)):
        for r in range(9):
            dst[plane(r, 32), :] = c1[every(y0 + r, 32, 16), :]
            w = rc[every(y0 + r, 32, 16), :]
            if r < 6:
                start = (3 + 32 * (r // 3)) * YR + FY0 + fine0 + r % 3
                w = jnp.where(lane32 < 64, w, rl(v[every(start, 32, YR), :], 32))
            dst[plane(9 + r, 32), :] = w


def coarse_x_kernel(c1, rc, v, ylo, yhi, ec, er, vs, slo, shi):
    lane = lane_of(YR)
    ec[...] = jnp.zeros_like(ec)
    er[...] = jnp.zeros_like(er)
    vs[...] = v[...]
    for i in range(32):
        ec[pl.ds((i + 9) * YR + CY0, 16), :] = c1[plane(i, 16), :]
        er[pl.ds((i + 9) * YR + CY0, 16), :] = rc[plane(i, 16), :]
    for src, crow, frow in ((ylo, CY0 - 9, FY0 - 3), (yhi, CY0 + 16, FY0 + 32)):
        for r in range(9):
            ec[every(9 * YR + crow + r, 32, YR), :] = src[plane(r, 32), :]
            w = src[plane(9 + r, 32), :]
            er[every(9 * YR + crow + r, 32, YR), :] = w
            if r < 6:
                start = (3 + 32 * (r // 3)) * YR + frow + r % 3
                vs[every(start, 32, YR), :] = own_lanes(rl(w, -32))
    for dst, first, fine in ((slo, 9, 3), (shi, 32, 64)):
        for i in range(9):
            dst[plane(i), :] = ec[plane(first + i), :]
            w = er[plane(first + i), :]
            if i < 3:
                w = jnp.where(lane < 64, w, rl(own_lanes(vs[plane(fine + i), :]), 32))
            dst[plane(9 + i), :] = w


def slots():
    for n in range(150):
        yield n, n // 50, n % 50, n // 6, 21 * (n % 6)


def coarse_z_kernel(ec0, er0, vs0, xlo, xhi, ec, er, vs, zlo, zhi):
    lane = lane_of(YR)
    ec[...] = ec0[...]
    er[...] = er0[...]
    vs[...] = vs0[...]
    for src, first, fine in ((xlo, 0, 0), (xhi, 41, 67)):
        for i in range(9):
            ec[plane(first + i), :] = src[plane(i), :]
            w = src[plane(9 + i), :]
            er[plane(first + i), :] = w
            if i < 3:
                vs[plane(fine + i), :] = own_lanes(rl(w, -32))
    lo = hi = None
    for n, which, x, group, at in slots():
        if n % 6 == 0:
            lo = jnp.zeros((YR, 128), F32)
            hi = lo
        w = (ec, ec, er)[which][plane(x), :]
        base = 64 if which == 1 else 0
        here = (lane >= at) & (lane < at + 18)
        lo = jnp.where(here, rl(w, at - base), lo)
        hi = jnp.where(here, rl(w, at - base - 46), hi)
        if n < FXN:
            w = vs[plane(n), :]
            here = (lane >= at + 18) & (lane < at + 21)
            lo = jnp.where(here, rl(w, at + 18 - Z0), lo)
            hi = jnp.where(here, rl(w, at + 18 - Z0 - 61), hi)
        if n % 6 == 5:
            zlo[plane(group), :] = lo
            zhi[plane(group), :] = hi


def finish_kernel(
    ec, er, vs, zlo, zhi, f, fx, fy, fz, inv, dg, out, res, cx, cy, cz, ci, cf, cv, v, tmp
):
    lane = lane_of(YR)
    even = lane % 2 == 0
    own = (lane >= Z0) & (lane < Z0 + 64)
    below = (lane >= Z0 - 18) & (lane < Z0)
    above = (lane >= Z0 + 64) & (lane < Z0 + 82)
    for n, which, x, group, at in slots():
        w = (ec, ec, er)[which][plane(x), :]
        w = jnp.where(own, rl(w, -32 if which == 1 else 32), 0.0)
        w = jnp.where(below, rl(zlo[plane(group), :], Z0 - 18 - at), w)
        w = jnp.where(above, rl(zhi[plane(group), :], Z0 + 64 - at), w)
        if which == 0:
            cx[plane(x), :] = 0.25 * jnp.where(even, w, rl(w, 1))
            cy[plane(x), :] = 0.25 * jnp.where(even, rl(w, -1), w)
        elif which == 1:
            cz[plane(x), :] = 0.25 * jnp.where(even, w, rl(w, 1))
            diag = jnp.where(even, rl(w, -1), w)
            inside = diag > 0.0
            ci[plane(x), :] = jnp.where(inside, 1.0 / jnp.where(inside, diag, 1.0), 0.0)
        else:
            cf[plane(x), :] = w
        if n < FXN:
            w = own_lanes(vs[plane(n), :])
            low = rl(zlo[plane(group), :], Z0 - 3 - at - 18)
            high = rl(zhi[plane(group), :], Z0 + 64 - at - 18)
            w = jnp.where((lane >= Z0 - 3) & (lane < Z0), low, w)
            v[plane(n), :] = jnp.where((lane >= Z0 + 64) & (lane < Z0 + 67), high, w)

    row = lax.broadcasted_iota(jnp.int32, (YR, 128), 0)
    colour = (row + lane // 2 + 1) % 2

    @pl.loop(0, CXN)
    def _(x):
        cv[plane(x), :] = jnp.where((colour + x) % 2 == 0, cf[plane(x), :] * ci[plane(x), :], 0.0)

    for half in range(1, 8):

        @pl.loop(half, CXN - half)
        def _(x):
            nb = nb_sum(
                cx[plane(x), :],
                cx[plane(x - 1), :],
                cy[plane(x), :],
                cz[plane(x), :],
                cv[plane(x - 1), :],
                cv[plane(x), :],
                cv[plane(x + 1), :],
                2,
            )
            new = (cf[plane(x), :] + nb) * ci[plane(x), :]
            cv[plane(x), :] = jnp.where((colour + x) % 2 == half % 2, new, cv[plane(x), :])

    for i in range(-2, 34):
        c = cv[pl.ds((i + 9) * YR + CY0 - 2, 20), :]
        slot = (i % 2) * YR
        tmp[every(slot, 20, 2), :] = c
        tmp[every(slot + 1, 20, 2), :] = c
        spread = tmp[pl.ds(slot, YR), :]
        for x in (2 * i + 3, 2 * i + 4):
            if 0 <= x < FXN:
                v[plane(x), :] = v[plane(x), :] + spread

    shade = fine_colour()

    @pl.loop(1, FXN - 1)
    def _(x):
        fine_update(x, shade, 0, f, fx, fy, fz, inv, v)

    @pl.loop(2, FXN - 2)
    def _(x):
        fine_update(x, shade, 1, f, fx, fy, fz, inv, v)

    @pl.loop(0, 64)
    def _(i):
        x = i + 3
        w = v[plane(x), :]
        r = f[plane(x), :] - (dg[plane(x), :] * w - fine_nb(x, fx, fy, fz, v))
        out[i] = rl(w, -32)[FY0 : FY0 + 32, :64]
        res[i] = rl(r, -32)[FY0 : FY0 + 32, :64]


def swap(low, high, axis):
    count = lax.axis_size(axis)
    up = [(i, i + 1) for i in range(count - 1)]
    down = [(i + 1, i) for i in range(count - 1)]
    return lax.ppermute(high, axis, up), lax.ppermute(low, axis, down)


def body(rhs_boxes, a_boxes, b_boxes, new_place):
    exchange = functools.partial(
        lax.all_to_all, axis_name=LAYER, split_axis=0, concat_axis=0, tiled=True
    )
    (spread,) = call(spread_kernel, [(32, 104, 128)], smem=1)(
        new_place, rhs_boxes, a_boxes, b_boxes
    )
    got = exchange(spread)
    place = got[:, 96, :4].astype(jnp.int32)
    (routed,) = call(route_kernel, [(32, 12, 8, 128)], smem=1)(place, got)
    got = exchange(routed)

    fine = (FXN * YR, 128)
    coarse = (CXN * YR, 128)
    rh, aa, bb, ylo, yhi, xlo, xhi = call(
        brick_kernel, [fine] * 3 + [(288, 128)] * 2 + [(9 * YR, 128)] * 2
    )(got)
    ylo, yhi = swap(ylo, yhi, "gy")
    xlo, xhi = call(fine_x_kernel, [(5 * YR, 128)] * 2, [(9 * YR, 128)] * 2)(xlo, xhi, ylo, yhi)
    xlo, xhi = swap(xlo, xhi, "gx")
    rh, aa, bb, zlo, zhi = call(fine_z_kernel, [fine] * 3 + [(5 * YR, 128)] * 2)(
        rh, aa, bb, ylo, yhi, xlo, xhi
    )
    zlo, zhi = swap(zlo, zhi, "gz")
    f, fx, fy, fz, inv, dg, v, c1, rc, ylo, yhi = call(
        presmooth_kernel,
        [fine] * 7 + [(512, 128)] * 2 + [(18 * 32, 128)] * 2,
        [fine, fine, (6 * YR, 128)],
    )(rh, aa, bb, zlo, zhi)
    ylo, yhi = swap(ylo, yhi, "gy")
    ec, er, vs, xlo, xhi = call(coarse_x_kernel, [coarse, coarse, fine] + [(18 * YR, 128)] * 2)(
        c1, rc, v, ylo, yhi
    )
    xlo, xhi = swap(xlo, xhi, "gx")
    ec, er, vs, zlo, zhi = call(coarse_z_kernel, [coarse, coarse, fine] + [(25 * YR, 128)] * 2)(
        ec, er, vs, xlo, xhi
    )
    zlo, zhi = swap(zlo, zhi, "gz")
    return tuple(
        call(
            finish_kernel,
            [(64, 32, 64)] * 2,
            [coarse] * 6 + [fine, (2 * YR, 128)],
        )(ec, er, vs, zlo, zhi, f, fx, fy, fz, inv, dg)
    )


def solution(mesh):
    return jax.shard_map(
        body,
        mesh=mesh,
        in_specs=(
            P("gz", ("gx", "gy"), None),
            P("gz", ("gx", "gy"), None),
            P("gz", ("gx", "gy"), None),
            P("gz", ("gx", "gy")),
        ),
        out_specs=(P("gx", "gy", "gz"), P("gx", "gy", "gz")),
        check_vma=False,
    )
```

```python
import functools

import jax
import jax.numpy as jnp
from jax import lax
from jax.experimental import pallas as pl
from jax.experimental.pallas import tpu as pltpu
from jax.sharding import PartitionSpec as P

LAYER = ("gx", "gy")
F32 = jnp.float32
YR = 40
FXN = 70
CXN = 50
FY0 = 4
CY0 = 12
Z0 = 32


def lane_of(rows):
    return lax.broadcasted_iota(jnp.int32, (rows, 128), 1)


def rl(v, shift):
    shift = shift % 128
    return v if shift == 0 else pltpu.roll(v, shift, 1)


def ry(v, shift):
    return pltpu.roll(v, shift % v.shape[0], 0)


def plane(index, rows=YR):
    if isinstance(index, int):
        return pl.ds(index * rows, rows)
    return pl.ds(pl.multiple_of(index * rows, 8), rows)


def every(start, count, stride):
    return pl.ds(start, count, stride=stride)


def own_lanes(v):
    lane = lane_of(v.shape[0])
    return jnp.where((lane >= Z0) & (lane < Z0 + 64), v, 0.0)


def call(kernel, outs, scratch=(), limit=24, smem=0, us=2):
    def run(*args):
        return pl.pallas_call(
            kernel,
            out_shape=[jax.ShapeDtypeStruct(s, F32) for s in outs],
            in_specs=[pl.BlockSpec(memory_space=pltpu.SMEM)] * smem
            + [pl.BlockSpec(memory_space=pltpu.VMEM)] * (len(args) - smem),
            out_specs=[pl.BlockSpec(memory_space=pltpu.VMEM)] * len(outs),
            scratch_shapes=[pltpu.VMEM(s, F32) for s in scratch],
            cost_estimate=pl.CostEstimate(
                flops=0, transcendentals=0, bytes_accessed=us * 3_000_000
            ),
            compiler_params=pltpu.CompilerParams(vmem_limit_bytes=limit << 20),
        )(*args)

    return run


def spread_kernel(place, rhs, a, b, out):
    lane = lane_of(8)
    mark = jnp.zeros((8, 128), F32)
    for k in range(4):
        mark = jnp.where(lane == k, place[0, k].astype(F32), mark)

    @pl.loop(0, 32)
    def _(j):
        for f, src in enumerate((rhs, a, b)):
            for m in range(8):
                col = pl.ds(pl.multiple_of(j * 1024 + m * 128, 128), 128)
                out[j, f * 32 + m * 4 : f * 32 + m * 4 + 4, :] = src[0, :, col]
        out[j, 96:104, :] = mark


def route_kernel(place, got, out):
    @pl.loop(0, 32)
    def _(s):
        for k in range(4):
            p = place[s, k]
            t = lax.shift_right_logical(p, 2)
            q = lax.bitwise_and(p, 3)
            for f in range(3):
                out[t, f * 4 + q] = got[s, every(f * 32 + k, 8, 4), :]


def brick_kernel(got, rh, aa, bb, ylo, yhi, xlo, xhi):
    lane8 = lane_of(8)
    bricks = (rh, aa, bb)
    for br in bricks:
        br[...] = jnp.zeros_like(br)

    @pl.loop(0, 32)
    def _(j):
        for f, br in enumerate(bricks):
            for qx in range(2):
                low = got[j, f * 4 + qx * 2]
                high = got[j, f * 4 + qx * 2 + 1]
                for c in range(4):
                    both = jnp.where(lane8 < 64, rl(low, 32 - 32 * c), rl(high, 64 - 32 * c))
                    start = (j + (qx * 32 + 3)) * YR + (FY0 + c)
                    br[every(start, 8, 4), :] = own_lanes(both)

    lane = lane_of(32)
    for f, br in enumerate(bricks):
        for r in range(3):
            at = pl.ds((f * 3 + r) * 32, 32)
            for dst, y in ((ylo, r), (yhi, 29 + r)):
                first = br[every(3 * YR + FY0 + y, 32, YR), :]
                second = br[every(35 * YR + FY0 + y, 32, YR), :]
                dst[at, :] = jnp.where(lane < 64, rl(first, -32), rl(second, 32))
        xlo[pl.ds(f * 3 * YR, 3 * YR), :] = br[pl.ds(3 * YR, 3 * YR), :]
        xhi[pl.ds(f * 3 * YR, 3 * YR), :] = br[pl.ds(64 * YR, 3 * YR), :]


def fine_x_kernel(xlo, xhi, ylo, yhi, slo, shi, tlo, thi):
    lane = lane_of(YR)
    for own, out, tmp, base, shift in ((xlo, slo, tlo, 0, 32), (xhi, shi, thi, 29, -32)):
        tmp[...] = own[...]
        for f in range(3):
            for r in range(3):
                at = pl.ds((f * 3 + r) * 32 + base, 3)
                tmp[every(f * 3 * YR + FY0 - 3 + r, 3, YR), :] = own_lanes(rl(ylo[at, :], shift))
                tmp[every(f * 3 * YR + FY0 + 32 + r, 3, YR), :] = own_lanes(rl(yhi[at, :], shift))
        for m in range(5):
            v = rl(tmp[plane(2 * m), :], -32)
            w = rl(tmp[plane(2 * m + 1), :], 32) if m < 4 else jnp.zeros_like(v)
            out[plane(m), :] = jnp.where(lane < 64, v, w)


def fine_z_kernel(rh0, aa0, bb0, ylo, yhi, xlo, xhi, rh, aa, bb, zlo, zhi):
    lane = lane_of(YR)
    bricks = (rh, aa, bb)
    for f, (br0, br) in enumerate(zip((rh0, aa0, bb0), bricks)):
        br[...] = br0[...]
        for r in range(3):
            at = pl.ds((f * 3 + r) * 32, 32)
            for src, row in ((ylo, FY0 - 3 + r), (yhi, FY0 + 32 + r)):
                v = src[at, :]
                br[every(3 * YR + row, 32, YR), :] = own_lanes(rl(v, 32))
                br[every(35 * YR + row, 32, YR), :] = own_lanes(rl(v, -32))
        for i in range(3):
            n = f * 3 + i
            shift = 32 if n % 2 == 0 else -32
            br[plane(i), :] = own_lanes(rl(xlo[plane(n // 2), :], shift))
            br[plane(67 + i), :] = own_lanes(rl(xhi[plane(n // 2), :], shift))
    for group in range(5):
        lo = jnp.zeros((YR, 128), F32)
        hi = lo
        for slot in range(14):
            for f, br in enumerate(bricks):
                v = br[plane(group * 14 + slot), :]
                at = 9 * slot + 3 * f
                here = (lane >= at) & (lane < at + 3)
                lo = jnp.where(here, rl(v, at - Z0), lo)
                hi = jnp.where(here, rl(v, at - Z0 - 61), hi)
        zlo[plane(group), :] = lo
        zhi[plane(group), :] = hi


def span(x, count):
    if isinstance(x, int):
        return pl.ds(x * YR, count * YR)
    return pl.ds(pl.multiple_of(x * YR, 8), count * YR)


def nb_sum(x, count, cx, cy_ref, cz, v, step):
    at = span(x, count)
    here = v[at, :]
    cz = cz[span(x, count), :]
    total = cx[span(x, count), :] * v[span(x + 1, count), :]
    total = total + cx[span(x - 1, count), :] * v[span(x - 1, count), :]
    cy = cy_ref[at, :]
    total = total + (cy * ry(here, -1) + ry(cy * here, 1))
    return total + (cz * rl(here, -step) + rl(cz * here, step))


def steps(count):
    def run(step):
        for k in range(count):
            step(k)

    return run


def red_rows(rows, odd):
    row = lax.broadcasted_iota(jnp.int32, (rows, 128), 0)
    return (row + row // YR + lane_of(rows) + odd) % 2 == 0


FC = 4
FS = 4
STEPS = 68 // FS


def zpair(s):
    return s + jnp.where(lane_of(s.shape[0]) % 2 == 0, rl(s, -1), rl(s, 1))


def halves(w):
    w = w.reshape(FC // 2, 2, YR, 128)
    return w[:, 0].reshape(FC // 2 * YR, 128), w[:, 1].reshape(FC // 2 * YR, 128)


def both(w):
    first, second = halves(w)
    return first + second


def coefficient_kernel(
    rh0, aa0, bb0, zlo, zhi, f, fx, fy, fz, ir, ib, dg, v, c1, slo, shi, a, b, ta, tx, ty, tz
):
    lane = lane_of(YR)
    for x in range(FXN):
        for n, (src, dst) in enumerate(((rh0, f), (aa0, a), (bb0, b))):
            at = 9 * (x % 14) + 3 * n
            w = src[plane(x), :]
            lo = rl(zlo[plane(x // 14), :], Z0 - 3 - at)
            hi = rl(zhi[plane(x // 14), :], Z0 + 64 - at)
            w = jnp.where((lane >= Z0 - 3) & (lane < Z0), lo, w)
            dst[plane(x), :] = jnp.where((lane >= Z0 + 64) & (lane < Z0 + 67), hi, w)

    def faces(x, count):
        here = b[span(x, count), :]
        fx[span(x, count), :] = 0.5 * (here + b[span(x + 1, count), :])
        fy[span(x, count), :] = 0.5 * (here + ry(here, -1))
        fz[span(x, count), :] = 0.5 * (here + rl(here, -1))

    faces(0, 1)

    @steps(STEPS)
    def _(k):
        faces(1 + k * FS, FS)

    nothing = jnp.zeros((YR, 128), F32)
    for ref in (fx, fy, fz):
        ref[plane(FXN - 1), :] = nothing
    for ref in (ir, ib, dg, v):
        ref[plane(0), :] = nothing
        ref[plane(FXN - 1), :] = nothing

    @steps(STEPS)
    def _(k):
        x = 1 + k * FS
        at = span(x, FS)
        py = fy[at, :]
        pz = fz[at, :]
        ax = a[at, :]
        total = fx[at, :] + fx[span(x - 1, FS), :] + py + ry(py, 1) + pz + rl(pz, 1)
        diag = ax + total
        inside = ax > 0.0
        one = jnp.where(inside, 1.0 / jnp.where(inside, diag, 1.0), 0.0)
        red = red_rows(FS * YR, 0)
        dg[at, :] = diag
        ir[at, :] = jnp.where(red, one, 0.0)
        ib[at, :] = jnp.where(red, 0.0, one)
        v[at, :] = jnp.where(red, f[at, :] * one, 0.0)

    edge = fx[plane(2), :]
    edge = edge + jnp.where(lane % 2 == 0, rl(edge, -1), rl(edge, 1))
    tx[plane(0), :] = edge

    @steps(64 // FC)
    def _(k):
        at = span(3 + k * FC, FC)
        to = span(k * (FC // 2), FC // 2)
        ta[to, :] = zpair(both(a[at, :]))
        tx[span(k * (FC // 2) + 1, FC // 2), :] = zpair(halves(fx[at, :])[1])
        ty[to, :] = zpair(both(fy[at, :]))
        tz[to, :] = both(fz[at, :])

    @steps(8)
    def _(k):
        base = k * 4 * YR
        even = lane_of(80) % 2 == 0

        def rows(ref, first, planes=0):
            return ref[every(base + planes * YR + first, 80, 2), :]

        acoef = 0.125 * (rows(ta, 0) + rows(ta, 1))
        fxp = 0.25 * (rows(tx, 0, 1) + rows(tx, 1, 1))
        fxm = 0.25 * (rows(tx, 0) + rows(tx, 1))
        fyp = 0.25 * rows(ty, 1)
        s = 0.25 * (rows(tz, 0) + rows(tz, 1))
        fzp = jnp.where(even, rl(s, -1), s)
        diag = acoef + 0.25 * (fxp + fxm + fyp + ry(fyp, 1) + fzp + rl(fzp, 2))
        pa = jnp.where(even, fxp, fyp)
        pb = jnp.where(even, fzp, diag)
        c1[pl.ds(k * 80, 80), :] = jnp.where(lane_of(80) < 64, rl(pa, -32), rl(pb, 32))

    for dst, y0 in ((slo, 2), (shi, 9)):
        for r in range(9):
            dst[plane(r, 32), :] = c1[every(y0 + r, 32, 20), :]


def presmooth_kernel(f, fx, fy, fz, ib, dg, v0, v, rc, slo, shi, tr):
    for x in (0, FXN - 1):
        v[plane(x), :] = v0[plane(x), :]

    @steps(STEPS)
    def _(k):
        x = 1 + k * FS
        at = span(x, FS)
        new = (f[at, :] + nb_sum(x, FS, fx, fy, fz, v0, 1)) * ib[at, :]
        v[at, :] = v0[at, :] + new

    @steps(64 // FC)
    def _(k):
        x = 3 + k * FC
        at = span(x, FC)
        miss = f[at, :] - (dg[at, :] * v[at, :] - nb_sum(x, FC, fx, fy, fz, v, 1))
        tr[span(k * (FC // 2), FC // 2), :] = zpair(both(miss))

    @steps(8)
    def _(k):
        base = k * 4 * YR
        rhs = tr[every(base, 80, 2), :] + tr[every(base + 1, 80, 2), :]
        rc[pl.ds(k * 80, 80), :] = jnp.where(lane_of(80) < 64, rl(0.125 * rhs, -32), 0.0)

    lane32 = lane_of(32)
    for dst, y0, fine0 in ((slo, 2, 0), (shi, 9, 29)):
        for r in range(9):
            w = rc[every(y0 + r, 32, 20), :]
            if r < 6:
                start = (3 + 32 * (r // 3)) * YR + FY0 + fine0 + r % 3
                w = jnp.where(lane32 < 64, w, rl(v[every(start, 32, YR), :], 32))
            dst[plane(r, 32), :] = w


def coarse_own(dst, src):
    dst[...] = jnp.zeros_like(dst)
    for i in range(32):
        dst[pl.ds((i + 9) * YR + CY0, 16), :] = src[pl.ds(i * 20 + 2, 16), :]


def coef_x_kernel(c1, ylo, yhi, ec, slo, shi):
    coarse_own(ec, c1)
    for src, crow in ((ylo, CY0 - 9), (yhi, CY0 + 16)):
        for r in range(9):
            ec[every(9 * YR + crow + r, 32, YR), :] = src[plane(r, 32), :]
    slo[...] = ec[pl.ds(9 * YR, 9 * YR), :]
    shi[...] = ec[pl.ds(32 * YR, 9 * YR), :]


def rhs_x_kernel(rc, v, ylo, yhi, er, vs, slo, shi):
    lane = lane_of(YR)
    coarse_own(er, rc)
    vs[...] = v[...]
    for src, crow, frow in ((ylo, CY0 - 9, FY0 - 3), (yhi, CY0 + 16, FY0 + 32)):
        for r in range(9):
            w = src[plane(r, 32), :]
            er[every(9 * YR + crow + r, 32, YR), :] = w
            if r < 6:
                start = (3 + 32 * (r // 3)) * YR + frow + r % 3
                vs[every(start, 32, YR), :] = own_lanes(rl(w, -32))
    for dst, first, fine in ((slo, 9, 3), (shi, 32, 64)):
        for i in range(9):
            w = er[plane(first + i), :]
            if i < 3:
                w = jnp.where(lane < 64, w, rl(own_lanes(vs[plane(fine + i), :]), 32))
            dst[plane(i), :] = w


def coef_slot(which, x):
    n = which * 50 + x
    return plane(n // 7), 18 * (n % 7)


def coef_z_kernel(ec0, xlo, xhi, ec, zlo, zhi):
    lane = lane_of(YR)
    ec[...] = ec0[...]
    ec[pl.ds(0, 9 * YR), :] = xlo[...]
    ec[pl.ds(41 * YR, 9 * YR), :] = xhi[...]
    lo = hi = None
    for n in range(100):
        at = 18 * (n % 7)
        if at == 0:
            lo = jnp.zeros((YR, 128), F32)
            hi = lo
        w = ec[plane(n % 50), :]
        base = 64 * (n // 50)
        here = (lane >= at) & (lane < at + 18)
        lo = jnp.where(here, rl(w, at - base), lo)
        hi = jnp.where(here, rl(w, at - base - 46), hi)
        if at == 108 or n == 99:
            zlo[plane(n // 7), :] = lo
            zhi[plane(n // 7), :] = hi


def rhs_z_kernel(er, vs0, xlo, xhi, rm, vs, zlo, zhi):
    lane = lane_of(YR)
    even = lane % 2 == 0
    own = (lane >= Z0) & (lane < Z0 + 64)
    vs[...] = vs0[...]
    for src, fine in ((xlo, 0), (xhi, 67)):
        for i in range(3):
            vs[plane(fine + i), :] = own_lanes(rl(src[plane(i), :], -32))
    lo = hi = None
    for n in range(25):
        at = 27 * (n % 4)
        if at == 0:
            lo = jnp.zeros((YR, 128), F32)
            hi = lo
        first = xlo[plane(n), :] if n < 9 else er[plane(n), :]
        second = xhi[plane(n - 16), :] if n >= 16 else er[plane(n + 25), :]
        w = rl(jnp.where(even, first, second), 32)
        rm[plane(n), :] = jnp.where(own, w, 0.0)
        here = (lane >= at) & (lane < at + 18)
        lo = jnp.where(here, rl(w, at - Z0), lo)
        hi = jnp.where(here, rl(w, at - Z0 - 46), hi)
        for i in range(3):
            if 3 * n + i < FXN:
                w = vs[plane(3 * n + i), :]
                to = at + 18 + 3 * i
                here = (lane >= to) & (lane < to + 3)
                lo = jnp.where(here, rl(w, to - Z0), lo)
                hi = jnp.where(here, rl(w, to - Z0 - 61), hi)
        if at == 81 or n == 24:
            zlo[plane(n // 4), :] = lo
            zhi[plane(n // 4), :] = hi


MXN = 28
CC = 1


def merge_kernel(ec, zlo, zhi, cx, cy, cz, jr, jb):
    lane = lane_of(YR)
    even = lane % 2 == 0
    own = (lane >= Z0) & (lane < Z0 + 64)
    below = (lane >= Z0 - 18) & (lane < Z0)
    above = (lane >= Z0 + 64) & (lane < Z0 + 82)
    nothing = jnp.zeros((YR, 128), F32)
    row = lax.broadcasted_iota(jnp.int32, (YR, 128), 0)
    colour = (row + lane // 2 + 1) % 2

    def load(which, x):
        if not 0 <= x < CXN:
            return nothing
        group, at = coef_slot(which, x)
        w = jnp.where(own, rl(ec[plane(x), :], 32 - 64 * which), 0.0)
        w = jnp.where(below, rl(zlo[group, :], Z0 - 18 - at), w)
        return jnp.where(above, rl(zhi[group, :], Z0 + 64 - at), w)

    for p in range(27):
        first, second = load(0, p - 1), load(0, p + 24)
        cx[plane(p), :] = 0.25 * jnp.where(even, first, rl(second, 1))
        cy[plane(p), :] = 0.25 * jnp.where(even, rl(first, -1), second)
        first, second = load(1, p - 1), load(1, p + 24)
        cz[plane(p), :] = 0.25 * jnp.where(even, first, rl(second, 1))
        diag = jnp.where(even, rl(first, -1), second)
        inside = diag > 0.0
        one = jnp.where(inside, 1.0 / jnp.where(inside, diag, 1.0), 0.0)
        isred = jnp.where(even, colour + p - 1, colour + p + 24) % 2 == 0
        jr[plane(p), :] = jnp.where(isred, one, 0.0)
        jb[plane(p), :] = jnp.where(isred, 0.0, one)
    for ref in (cx, cy, cz, jr, jb):
        ref[plane(27), :] = nothing


def finish_kernel(
    rm, vs, zlo, zhi, cx, cy, cz, jr, jb, f, fx, fy, fz, ir, ib, dg, out, res, cf, red, blk, v, w0, tmp
):
    lane = lane_of(YR)
    even = lane % 2 == 0
    below = (lane >= Z0 - 18) & (lane < Z0)
    above = (lane >= Z0 + 64) & (lane < Z0 + 82)
    nothing = jnp.zeros((YR, 128), F32)
    for ref in (cf, red, blk):
        for p in (0, 26, 27):
            ref[plane(p), :] = nothing
    for n in range(25):
        at = 27 * (n % 4)
        w = jnp.where(below, rl(zlo[plane(n // 4), :], Z0 - 18 - at), rm[plane(n), :])
        w = jnp.where(above, rl(zhi[plane(n // 4), :], Z0 + 64 - at), w)
        cf[plane(n + 1), :] = w
        red[plane(n + 1), :] = w * jr[plane(n + 1), :]
    for n in range(FXN):
        at = 27 * (n // 3 % 4) + 18 + 3 * (n % 3)
        group = plane(n // 12)
        w = own_lanes(vs[plane(n), :])
        low = rl(zlo[group, :], Z0 - 3 - at)
        high = rl(zhi[group, :], Z0 + 64 - at)
        w = jnp.where((lane >= Z0 - 3) & (lane < Z0), low, w)
        v[plane(n), :] = jnp.where((lane >= Z0 + 64) & (lane < Z0 + 67), high, w)

    def seam(ref):
        ref[plane(26), :] = jnp.where(even, rl(ref[plane(1), :], -1), 0.0)
        ref[plane(0), :] = jnp.where(even, 0.0, rl(ref[plane(25), :], 1))

    seam(red)

    for half in range(1, 8):
        src, dst, inv = (red, blk, jb) if half % 2 else (blk, red, jr)

        @steps(26 // CC)
        def _(k):
            x = 1 + k * CC
            at = span(x, CC)
            dst[at, :] = (cf[at, :] + nb_sum(x, CC, cx, cy, cz, src, 2)) * inv[at, :]

        seam(dst)

    for i in range(-2, 34):
        p = i + 10 if i + 9 < 25 else i + 9 - 24
        c = red[plane(p), :] + blk[plane(p), :]
        c = jnp.where(even, c, rl(c, 1)) if i + 9 < 25 else jnp.where(even, rl(c, -1), c)
        c = c[CY0 - 2 : CY0 + 18]
        slot = (i % 8) * YR
        tmp[every(slot, 20, 2), :] = c
        tmp[every(slot + 1, 20, 2), :] = c
        spread = tmp[pl.ds(slot, YR), :]
        for x in (2 * i + 3, 2 * i + 4):
            if 0 <= x < FXN:
                v[plane(x), :] = v[plane(x), :] + spread

    w0[plane(0), :] = nothing
    w0[plane(FXN - 1), :] = nothing

    @steps(STEPS)
    def _(k):
        x = 1 + k * FS
        at = span(x, FS)
        w0[at, :] = (f[at, :] + nb_sum(x, FS, fx, fy, fz, v, 1)) * ir[at, :]

    @steps(STEPS)
    def _(k):
        x = 1 + k * FS
        at = span(x, FS)
        new = (f[at, :] + nb_sum(x, FS, fx, fy, fz, w0, 1)) * ib[at, :]
        v[at, :] = new + w0[at, :]

    def crop(w):
        return rl(w, -32).reshape(FC, YR, 128)[:, FY0 : FY0 + 32, :64]

    @steps(64 // FC)
    def _(k):
        x = 3 + k * FC
        at = span(x, FC)
        w = v[at, :]
        r = f[at, :] - (dg[at, :] * w - nb_sum(x, FC, fx, fy, fz, v, 1))
        out[pl.ds(k * FC, FC)] = crop(w)
        res[pl.ds(k * FC, FC)] = crop(r)


def swap(low, high, axis):
    count = lax.axis_size(axis)
    up = [(i, i + 1) for i in range(count - 1)]
    down = [(i + 1, i) for i in range(count - 1)]
    return lax.ppermute(high, axis, up), lax.ppermute(low, axis, down)


def body(rhs_boxes, a_boxes, b_boxes, new_place):
    exchange = functools.partial(
        lax.all_to_all, axis_name=LAYER, split_axis=0, concat_axis=0, tiled=True
    )
    (spread,) = call(spread_kernel, [(32, 104, 128)], smem=1)(
        new_place, rhs_boxes, a_boxes, b_boxes
    )
    got = exchange(spread)
    place = got[:, 96, :4].astype(jnp.int32)
    (routed,) = call(route_kernel, [(32, 12, 8, 128)], smem=1)(place, got)
    got = exchange(routed)

    fine = (FXN * YR, 128)
    coarse = (CXN * YR, 128)
    rh, aa, bb, ylo, yhi, xlo, xhi = call(
        brick_kernel, [fine] * 3 + [(288, 128)] * 2 + [(9 * YR, 128)] * 2
    )(got)
    ylo, yhi = swap(ylo, yhi, "gy")
    xlo, xhi = call(fine_x_kernel, [(5 * YR, 128)] * 2, [(9 * YR, 128)] * 2)(xlo, xhi, ylo, yhi)
    xlo, xhi = swap(xlo, xhi, "gx")
    rh, aa, bb, zlo, zhi = call(fine_z_kernel, [fine] * 3 + [(5 * YR, 128)] * 2)(
        rh, aa, bb, ylo, yhi, xlo, xhi
    )
    zlo, zhi = swap(zlo, zhi, "gz")
    f, fx, fy, fz, ir, ib, dg, v, c1, cylo, cyhi = call(
        coefficient_kernel,
        [fine] * 8 + [(640, 128)] + [(9 * 32, 128)] * 2,
        [fine, fine] + [(33 * YR, 128)] * 4,
        us=8,
    )(rh, aa, bb, zlo, zhi)
    cylo, cyhi = swap(cylo, cyhi, "gy")
    v, rc, ylo, yhi = call(
        presmooth_kernel,
        [fine, (640, 128)] + [(9 * 32, 128)] * 2,
        [(32 * YR, 128)],
        us=6,
    )(f, fx, fy, fz, ib, dg, v)
    cylo, cyhi, rc = lax.optimization_barrier((cylo, cyhi, rc))
    ylo, yhi = swap(ylo, yhi, "gy")
    ec, cxlo, cxhi = call(coef_x_kernel, [coarse] + [(9 * YR, 128)] * 2, us=1)(c1, cylo, cyhi)
    cxlo, cxhi = swap(cxlo, cxhi, "gx")
    er, vs, xlo, xhi = call(rhs_x_kernel, [coarse, fine] + [(9 * YR, 128)] * 2, us=1)(
        rc, v, ylo, yhi
    )
    xlo, xhi = swap(xlo, xhi, "gx")
    ec, czlo, czhi = call(coef_z_kernel, [coarse] + [(15 * YR, 128)] * 2)(ec, cxlo, cxhi)
    czlo, czhi = swap(czlo, czhi, "gz")
    rm, vs, zlo, zhi = call(
        rhs_z_kernel, [(25 * YR, 128), fine] + [(7 * YR, 128)] * 2
    )(er, vs, xlo, xhi)
    zlo, zhi = swap(zlo, zhi, "gz")
    merged = (MXN * YR, 128)
    coefs = call(merge_kernel, [merged] * 5, us=5)(ec, czlo, czhi)
    return tuple(
        call(
            finish_kernel,
            [(64, 32, 64)] * 2,
            [merged] * 3 + [fine, fine, (8 * YR, 128)],
            us=8,
        )(rm, vs, zlo, zhi, *coefs, f, fx, fy, fz, ir, ib, dg)
    )


def solution(mesh):
    return jax.shard_map(
        body,
        mesh=mesh,
        in_specs=(
            P("gz", ("gx", "gy"), None),
            P("gz", ("gx", "gy"), None),
            P("gz", ("gx", "gy"), None),
            P("gz", ("gx", "gy")),
        ),
        out_specs=(P("gx", "gy", "gz"), P("gx", "gy", "gz")),
        check_vma=False,
    )
```

```python
import functools

import jax
import jax.numpy as jnp
from jax import lax
from jax.experimental import pallas as pl
from jax.experimental.pallas import tpu as pltpu
from jax.sharding import PartitionSpec as P

LAYER = ("gx", "gy")
F32 = jnp.float32
YR = 40
FXN = 70
CXN = 50
FY0 = 4
CY0 = 12
Z0 = 32


def lane_of(rows):
    return lax.broadcasted_iota(jnp.int32, (rows, 128), 1)


def rl(v, shift):
    shift = shift % 128
    return v if shift == 0 else pltpu.roll(v, shift, 1)


def ry(v, shift):
    return pltpu.roll(v, shift % v.shape[0], 0)


def plane(index, rows=YR):
    if isinstance(index, int):
        return pl.ds(index * rows, rows)
    return pl.ds(pl.multiple_of(index * rows, 8), rows)


def every(start, count, stride):
    return pl.ds(start, count, stride=stride)


def own_lanes(v):
    lane = lane_of(v.shape[0])
    return jnp.where((lane >= Z0) & (lane < Z0 + 64), v, 0.0)


def call(kernel, outs, scratch=(), limit=24, smem=0, us=2):
    def run(*args):
        return pl.pallas_call(
            kernel,
            out_shape=[jax.ShapeDtypeStruct(s, F32) for s in outs],
            in_specs=[pl.BlockSpec(memory_space=pltpu.SMEM)] * smem
            + [pl.BlockSpec(memory_space=pltpu.VMEM)] * (len(args) - smem),
            out_specs=[pl.BlockSpec(memory_space=pltpu.VMEM)] * len(outs),
            scratch_shapes=[pltpu.VMEM(s, F32) for s in scratch],
            cost_estimate=pl.CostEstimate(
                flops=0, transcendentals=0, bytes_accessed=us * 3_000_000
            ),
            compiler_params=pltpu.CompilerParams(vmem_limit_bytes=limit << 20),
        )(*args)

    return run


def spread_kernel(place_hbm, rhs, a, b, out, buf, place, sem):
    first = pltpu.make_async_copy(place_hbm, place, sem.at[12])
    first.start()
    copies = []
    for f, src in enumerate((rhs, a, b)):
        for part in range(4):
            at = pl.ds(part * 8192, 8192)
            copy = pltpu.make_async_copy(
                src.at[0, :, at], buf.at[f, :, at], sem.at[f * 4 + part]
            )
            copy.start()
            copies.append(copy)
    first.wait()
    lane = lane_of(8)
    mark = jnp.zeros((8, 128), F32)
    for k in range(4):
        mark = jnp.where(lane == k, place[0, k].astype(F32), mark)
    for j in range(32):
        out[j, 96:104, :] = mark
    for f in range(3):
        for part in range(4):
            copies[f * 4 + part].wait()
            for j in range(part * 8, part * 8 + 8):
                for m in range(8):
                    at = f * 32 + m * 4
                    out[j, at : at + 4, :] = buf[f, :, j * 1024 + m * 128 : j * 1024 + m * 128 + 128]


def route_kernel(place, got, out):
    @pl.loop(0, 32)
    def _(s):
        for k in range(4):
            p = place[s, k]
            t = lax.shift_right_logical(p, 2)
            q = lax.bitwise_and(p, 3)
            for f in range(3):
                out[t, f * 4 + q] = got[s, every(f * 32 + k, 8, 4), :]


DEPTH = (2, 2, 3)
FIRST = (0, 2, 4)
ITEMS = tuple((f, r) for f in range(3) for r in range(DEPTH[f]))


def strip_kernel(got, ylo, yhi):
    quarter = lane_of(32) // 32
    for f in range(3):
        for dst, row, first in ((ylo, 0, 0), (yhi, 7, 4 - DEPTH[f])):
            parts = [got[every((f * 4 + q) * 8 + row, 32, 96), :] for q in range(4)]
            for r in range(DEPTH[f]):
                w = rl(parts[0], -32 * (first + r))
                for q in range(1, 4):
                    w = jnp.where(quarter == q, rl(parts[q], 32 * (q - first - r)), w)
                dst[plane(FIRST[f] + r, 32), :] = w


def brick_kernel(got, rh, aa, bb, xlo, xhi):
    lane8 = lane_of(8)
    bricks = (rh, aa, bb)
    for br in bricks:
        br[...] = jnp.zeros_like(br)

    @pl.loop(0, 16)
    def _(k):
        for half in range(2):
            j = 2 * k + half
            for f, br in enumerate(bricks):
                for qx in range(2):
                    low = got[j, f * 4 + qx * 2]
                    high = got[j, f * 4 + qx * 2 + 1]
                    for c in range(4):
                        w = jnp.where(lane8 < 64, rl(low, 32 - 32 * c), rl(high, 64 - 32 * c))
                        start = (j + (qx * 32 + 3)) * YR + (FY0 + c)
                        br[every(start, 8, 4), :] = own_lanes(w)

    for f, br in enumerate(bricks):
        size = DEPTH[f] * YR
        xlo[pl.ds(FIRST[f] * YR, size), :] = br[pl.ds(3 * YR, size), :]
        xhi[pl.ds(FIRST[f] * YR, size), :] = br[pl.ds(67 * YR - size, size), :]


def fine_x_kernel(xlo, xhi, ylo, yhi, slo, shi, tlo, thi):
    lane = lane_of(YR)
    for own, out, tmp, upper in ((xlo, slo, tlo, False), (xhi, shi, thi, True)):
        tmp[...] = own[...]
        for n, (f, r) in enumerate(ITEMS):
            d = DEPTH[f]
            at = pl.ds(n * 32 + (32 - d if upper else 0), d)
            shift = -32 if upper else 32
            for src, row in ((ylo, FY0 - d + r), (yhi, FY0 + 32 + r)):
                tmp[every(FIRST[f] * YR + row, d, YR), :] = own_lanes(rl(src[at, :], shift))
        for m in range(4):
            v = rl(tmp[plane(2 * m), :], -32)
            w = rl(tmp[plane(2 * m + 1), :], 32) if m < 3 else jnp.zeros_like(v)
            out[plane(m), :] = jnp.where(lane < 64, v, w)


def z_slot(n):
    return plane(n // 18), 7 * (n % 18)


def fine_y_kernel(rh0, aa0, bb0, ylo, yhi, rh, aa, bb, zlo, zhi):
    lane = lane_of(YR)
    bricks = (rh, aa, bb)
    for br0, br in zip((rh0, aa0, bb0), bricks):
        br[...] = br0[...]
    for n, (f, r) in enumerate(ITEMS):
        for src, row in ((ylo, FY0 - DEPTH[f] + r), (yhi, FY0 + 32 + r)):
            v = src[plane(n, 32), :]
            bricks[f][every(3 * YR + row, 32, YR), :] = own_lanes(rl(v, 32))
            bricks[f][every(35 * YR + row, 32, YR), :] = own_lanes(rl(v, -32))
    lo = hi = None
    for n in range(64):
        group, base = z_slot(n)
        if base == 0:
            lo = jnp.zeros((YR, 128), F32)
            hi = lo
        for f, br in enumerate(bricks):
            v = br[plane(n + 3), :]
            at = base + FIRST[f]
            here = (lane >= at) & (lane < at + DEPTH[f])
            lo = jnp.where(here, rl(v, at - Z0), lo)
            hi = jnp.where(here, rl(v, at - Z0 - 64 + DEPTH[f]), hi)
        if n % 18 == 17 or n == 63:
            zlo[group, :] = lo
            zhi[group, :] = hi


def x_plane(f, r, src):
    n = FIRST[f] + r
    return own_lanes(rl(src[plane(n // 2), :], -32 if n % 2 else 32))


def fine_z_kernel(zlo0, zhi0, xlo, xhi, zlo, zhi):
    lane = lane_of(YR)
    zlo[...] = zlo0[...]
    zhi[...] = zhi0[...]
    lo = zlo0[plane(3), :]
    hi = zhi0[plane(3), :]
    for f, r in ITEMS:
        for src, n in ((xlo, 64 + 3 - DEPTH[f] + r), (xhi, 67 + r)):
            v = x_plane(f, r, src)
            at = z_slot(n)[1] + FIRST[f]
            here = (lane >= at) & (lane < at + DEPTH[f])
            lo = jnp.where(here, rl(v, at - Z0), lo)
            hi = jnp.where(here, rl(v, at - Z0 - 64 + DEPTH[f]), hi)
    zlo[plane(3), :] = lo
    zhi[plane(3), :] = hi


def span(x, count):
    if isinstance(x, int):
        return pl.ds(x * YR, count * YR)
    return pl.ds(pl.multiple_of(x * YR, 8), count * YR)


def nb_sum(x, count, cx, cy_ref, cz, v, step):
    at = span(x, count)
    here = v[at, :]
    cz = cz[span(x, count), :]
    total = cx[span(x, count), :] * v[span(x + 1, count), :]
    total = total + cx[span(x - 1, count), :] * v[span(x - 1, count), :]
    cy = cy_ref[at, :]
    total = total + (cy * ry(here, -1) + ry(cy * here, 1))
    return total + (cz * rl(here, -step) + rl(cz * here, step))


def steps(count):
    def run(step):
        for k in range(count):
            step(k)

    return run


def red_rows(rows, odd):
    row = lax.broadcasted_iota(jnp.int32, (rows, 128), 0)
    return (row + row // YR + lane_of(rows) + odd) % 2 == 0


FC = 4
FS = 4
STEPS = 68 // FS


def zpair(s):
    return s + jnp.where(lane_of(s.shape[0]) % 2 == 0, rl(s, -1), rl(s, 1))


def halves(w):
    w = w.reshape(FC // 2, 2, YR, 128)
    return w[:, 0].reshape(FC // 2 * YR, 128), w[:, 1].reshape(FC // 2 * YR, 128)


def both(w):
    first, second = halves(w)
    return first + second


def coefficient_kernel(
    rh0, aa0, bb0, xlo, xhi, zlo, zhi, f, fx, fy, fz, ir, ib, dg, v, c1, slo, shi, a, b, ta, tx, ty, tz
):
    lane = lane_of(YR)
    for x in range(FXN):
        group, base = z_slot(x - 3 if 3 <= x < 67 else (64 + x if x < 3 else x))
        for n, (src, dst) in enumerate(((rh0, f), (aa0, a), (bb0, b))):
            d = DEPTH[n]
            if 3 <= x < 67:
                w = src[plane(x), :]
            elif 3 - d <= x < 3:
                w = x_plane(n, x - 3 + d, xlo)
            elif 67 <= x < 67 + d:
                w = x_plane(n, x - 67, xhi)
            else:
                dst[plane(x), :] = jnp.zeros((YR, 128), F32)
                continue
            at = base + FIRST[n]
            w = jnp.where((lane >= Z0 - d) & (lane < Z0), rl(zlo[group, :], Z0 - d - at), w)
            above = (lane >= Z0 + 64) & (lane < Z0 + 64 + d)
            dst[plane(x), :] = jnp.where(above, rl(zhi[group, :], Z0 + 64 - at), w)

    def faces(x, count):
        here = b[span(x, count), :]
        fx[span(x, count), :] = 0.5 * (here + b[span(x + 1, count), :])
        fy[span(x, count), :] = 0.5 * (here + ry(here, -1))
        fz[span(x, count), :] = 0.5 * (here + rl(here, -1))

    faces(0, 1)

    @steps(STEPS)
    def _(k):
        faces(1 + k * FS, FS)

    nothing = jnp.zeros((YR, 128), F32)
    for ref in (fx, fy, fz):
        ref[plane(FXN - 1), :] = nothing
    for ref in (ir, ib, dg, v):
        ref[plane(0), :] = nothing
        ref[plane(FXN - 1), :] = nothing

    @steps(STEPS)
    def _(k):
        x = 1 + k * FS
        at = span(x, FS)
        py = fy[at, :]
        pz = fz[at, :]
        ax = a[at, :]
        total = fx[at, :] + fx[span(x - 1, FS), :] + py + ry(py, 1) + pz + rl(pz, 1)
        diag = ax + total
        inside = ax > 0.0
        one = jnp.where(inside, 1.0 / jnp.where(inside, diag, 1.0), 0.0)
        red = red_rows(FS * YR, 0)
        dg[at, :] = diag
        ir[at, :] = jnp.where(red, one, 0.0)
        ib[at, :] = jnp.where(red, 0.0, one)
        v[at, :] = jnp.where(red, f[at, :] * one, 0.0)

    edge = fx[plane(2), :]
    edge = edge + jnp.where(lane % 2 == 0, rl(edge, -1), rl(edge, 1))
    tx[plane(0), :] = edge

    @steps(64 // FC)
    def _(k):
        at = span(3 + k * FC, FC)
        to = span(k * (FC // 2), FC // 2)
        ta[to, :] = zpair(both(a[at, :]))
        tx[span(k * (FC // 2) + 1, FC // 2), :] = zpair(halves(fx[at, :])[1])
        ty[to, :] = zpair(both(fy[at, :]))
        tz[to, :] = both(fz[at, :])

    @steps(8)
    def _(k):
        base = k * 4 * YR
        even = lane_of(80) % 2 == 0

        def rows(ref, first, planes=0):
            return ref[every(base + planes * YR + first, 80, 2), :]

        acoef = 0.125 * (rows(ta, 0) + rows(ta, 1))
        fxp = 0.25 * (rows(tx, 0, 1) + rows(tx, 1, 1))
        fxm = 0.25 * (rows(tx, 0) + rows(tx, 1))
        fyp = 0.25 * rows(ty, 1)
        s = 0.25 * (rows(tz, 0) + rows(tz, 1))
        fzp = jnp.where(even, rl(s, -1), s)
        diag = acoef + 0.25 * (fxp + fxm + fyp + ry(fyp, 1) + fzp + rl(fzp, 2))
        pa = jnp.where(even, fxp, fyp)
        pb = jnp.where(even, fzp, diag)
        c1[pl.ds(k * 80, 80), :] = jnp.where(lane_of(80) < 64, rl(pa, -32), rl(pb, 32))

    for dst, y0 in ((slo, 2), (shi, 9)):
        for r in range(9):
            dst[plane(r, 32), :] = c1[every(y0 + r, 32, 20), :]


def presmooth_kernel(f, fx, fy, fz, ib, dg, v0, v, rc, slo, shi, tr):
    for x in (0, FXN - 1):
        v[plane(x), :] = v0[plane(x), :]

    @steps(STEPS)
    def _(k):
        x = 1 + k * FS
        at = span(x, FS)
        new = (f[at, :] + nb_sum(x, FS, fx, fy, fz, v0, 1)) * ib[at, :]
        v[at, :] = v0[at, :] + new

    @steps(64 // FC)
    def _(k):
        x = 3 + k * FC
        at = span(x, FC)
        miss = f[at, :] - (dg[at, :] * v[at, :] - nb_sum(x, FC, fx, fy, fz, v, 1))
        tr[span(k * (FC // 2), FC // 2), :] = zpair(both(miss))

    @steps(8)
    def _(k):
        base = k * 4 * YR
        rhs = tr[every(base, 80, 2), :] + tr[every(base + 1, 80, 2), :]
        rc[pl.ds(k * 80, 80), :] = jnp.where(lane_of(80) < 64, rl(0.125 * rhs, -32), 0.0)

    lane32 = lane_of(32)
    for dst, y0, fine0 in ((slo, 2, 0), (shi, 9, 29)):
        for r in range(9):
            w = rc[every(y0 + r, 32, 20), :]
            if r < 6:
                start = (3 + 32 * (r // 3)) * YR + FY0 + fine0 + r % 3
                w = jnp.where(lane32 < 64, w, rl(v[every(start, 32, YR), :], 32))
            dst[plane(r, 32), :] = w


def coarse_own(dst, src):
    dst[...] = jnp.zeros_like(dst)
    for i in range(32):
        dst[pl.ds((i + 9) * YR + CY0, 16), :] = src[pl.ds(i * 20 + 2, 16), :]


def coef_x_kernel(c1, ylo, yhi, ec, slo, shi):
    coarse_own(ec, c1)
    for src, crow in ((ylo, CY0 - 9), (yhi, CY0 + 16)):
        for r in range(9):
            ec[every(9 * YR + crow + r, 32, YR), :] = src[plane(r, 32), :]
    slo[...] = ec[pl.ds(9 * YR, 9 * YR), :]
    shi[...] = ec[pl.ds(32 * YR, 9 * YR), :]


def rhs_x_kernel(rc, v, ylo, yhi, er, vs, slo, shi):
    lane = lane_of(YR)
    coarse_own(er, rc)
    vs[...] = v[...]
    for src, crow, frow in ((ylo, CY0 - 9, FY0 - 3), (yhi, CY0 + 16, FY0 + 32)):
        for r in range(9):
            w = src[plane(r, 32), :]
            er[every(9 * YR + crow + r, 32, YR), :] = w
            if r < 6:
                start = (3 + 32 * (r // 3)) * YR + frow + r % 3
                vs[every(start, 32, YR), :] = own_lanes(rl(w, -32))
    for dst, first, fine in ((slo, 9, 3), (shi, 32, 64)):
        for i in range(9):
            w = er[plane(first + i), :]
            if i < 3:
                w = jnp.where(lane < 64, w, rl(own_lanes(vs[plane(fine + i), :]), 32))
            dst[plane(i), :] = w


def coef_slot(which, x):
    n = which * 50 + x
    return plane(n // 7), 18 * (n % 7)


def coef_z_kernel(ec0, xlo, xhi, ec, zlo, zhi):
    lane = lane_of(YR)
    ec[...] = ec0[...]
    ec[pl.ds(0, 9 * YR), :] = xlo[...]
    ec[pl.ds(41 * YR, 9 * YR), :] = xhi[...]
    lo = hi = None
    for n in range(100):
        at = 18 * (n % 7)
        if at == 0:
            lo = jnp.zeros((YR, 128), F32)
            hi = lo
        w = ec[plane(n % 50), :]
        base = 64 * (n // 50)
        here = (lane >= at) & (lane < at + 18)
        lo = jnp.where(here, rl(w, at - base), lo)
        hi = jnp.where(here, rl(w, at - base - 46), hi)
        if at == 108 or n == 99:
            zlo[plane(n // 7), :] = lo
            zhi[plane(n // 7), :] = hi


def rhs_z_kernel(er, vs0, xlo, xhi, rm, vs, zlo, zhi):
    lane = lane_of(YR)
    even = lane % 2 == 0
    own = (lane >= Z0) & (lane < Z0 + 64)
    vs[...] = vs0[...]
    for src, fine in ((xlo, 0), (xhi, 67)):
        for i in range(3):
            vs[plane(fine + i), :] = own_lanes(rl(src[plane(i), :], -32))
    lo = hi = None
    for n in range(25):
        at = 27 * (n % 4)
        if at == 0:
            lo = jnp.zeros((YR, 128), F32)
            hi = lo
        first = xlo[plane(n), :] if n < 9 else er[plane(n), :]
        second = xhi[plane(n - 16), :] if n >= 16 else er[plane(n + 25), :]
        w = rl(jnp.where(even, first, second), 32)
        rm[plane(n), :] = jnp.where(own, w, 0.0)
        here = (lane >= at) & (lane < at + 18)
        lo = jnp.where(here, rl(w, at - Z0), lo)
        hi = jnp.where(here, rl(w, at - Z0 - 46), hi)
        for i in range(3):
            if 3 * n + i < FXN:
                w = vs[plane(3 * n + i), :]
                to = at + 18 + 3 * i
                here = (lane >= to) & (lane < to + 3)
                lo = jnp.where(here, rl(w, to - Z0), lo)
                hi = jnp.where(here, rl(w, to - Z0 - 61), hi)
        if at == 81 or n == 24:
            zlo[plane(n // 4), :] = lo
            zhi[plane(n // 4), :] = hi


MXN = 28
CC = 1


def merge_kernel(ec, zlo, zhi, cx, cy, cz, jr, jb):
    lane = lane_of(YR)
    even = lane % 2 == 0
    own = (lane >= Z0) & (lane < Z0 + 64)
    below = (lane >= Z0 - 18) & (lane < Z0)
    above = (lane >= Z0 + 64) & (lane < Z0 + 82)
    nothing = jnp.zeros((YR, 128), F32)
    row = lax.broadcasted_iota(jnp.int32, (YR, 128), 0)
    colour = (row + lane // 2 + 1) % 2

    def load(which, x):
        if not 0 <= x < CXN:
            return nothing
        group, at = coef_slot(which, x)
        w = jnp.where(own, rl(ec[plane(x), :], 32 - 64 * which), 0.0)
        w = jnp.where(below, rl(zlo[group, :], Z0 - 18 - at), w)
        return jnp.where(above, rl(zhi[group, :], Z0 + 64 - at), w)

    for p in range(27):
        first, second = load(0, p - 1), load(0, p + 24)
        cx[plane(p), :] = 0.25 * jnp.where(even, first, rl(second, 1))
        cy[plane(p), :] = 0.25 * jnp.where(even, rl(first, -1), second)
        first, second = load(1, p - 1), load(1, p + 24)
        cz[plane(p), :] = 0.25 * jnp.where(even, first, rl(second, 1))
        diag = jnp.where(even, rl(first, -1), second)
        inside = diag > 0.0
        one = jnp.where(inside, 1.0 / jnp.where(inside, diag, 1.0), 0.0)
        isred = jnp.where(even, colour + p - 1, colour + p + 24) % 2 == 0
        jr[plane(p), :] = jnp.where(isred, one, 0.0)
        jb[plane(p), :] = jnp.where(isred, 0.0, one)
    for ref in (cx, cy, cz, jr, jb):
        ref[plane(27), :] = nothing


def finish_kernel(
    rm, vs, zlo, zhi, cx, cy, cz, jr, jb, f, fx, fy, fz, ir, ib, dg, out, res, cf, red, blk, v, w0, tmp
):
    lane = lane_of(YR)
    even = lane % 2 == 0
    below = (lane >= Z0 - 18) & (lane < Z0)
    above = (lane >= Z0 + 64) & (lane < Z0 + 82)
    nothing = jnp.zeros((YR, 128), F32)
    for ref in (cf, red, blk):
        for p in (0, 26, 27):
            ref[plane(p), :] = nothing
    for n in range(25):
        at = 27 * (n % 4)
        w = jnp.where(below, rl(zlo[plane(n // 4), :], Z0 - 18 - at), rm[plane(n), :])
        w = jnp.where(above, rl(zhi[plane(n // 4), :], Z0 + 64 - at), w)
        cf[plane(n + 1), :] = w
        red[plane(n + 1), :] = w * jr[plane(n + 1), :]
    for n in range(FXN):
        at = 27 * (n // 3 % 4) + 18 + 3 * (n % 3)
        group = plane(n // 12)
        w = own_lanes(vs[plane(n), :])
        low = rl(zlo[group, :], Z0 - 3 - at)
        high = rl(zhi[group, :], Z0 + 64 - at)
        w = jnp.where((lane >= Z0 - 3) & (lane < Z0), low, w)
        v[plane(n), :] = jnp.where((lane >= Z0 + 64) & (lane < Z0 + 67), high, w)

    def seam(ref):
        ref[plane(26), :] = jnp.where(even, rl(ref[plane(1), :], -1), 0.0)
        ref[plane(0), :] = jnp.where(even, 0.0, rl(ref[plane(25), :], 1))

    seam(red)

    for half in range(1, 8):
        src, dst, inv = (red, blk, jb) if half % 2 else (blk, red, jr)

        @steps(26 // CC)
        def _(k):
            x = 1 + k * CC
            at = span(x, CC)
            dst[at, :] = (cf[at, :] + nb_sum(x, CC, cx, cy, cz, src, 2)) * inv[at, :]

        seam(dst)

    for i in range(-2, 34):
        p = i + 10 if i + 9 < 25 else i + 9 - 24
        c = red[plane(p), :] + blk[plane(p), :]
        c = jnp.where(even, c, rl(c, 1)) if i + 9 < 25 else jnp.where(even, rl(c, -1), c)
        c = c[CY0 - 2 : CY0 + 18]
        slot = (i % 8) * YR
        tmp[every(slot, 20, 2), :] = c
        tmp[every(slot + 1, 20, 2), :] = c
        spread = tmp[pl.ds(slot, YR), :]
        for x in (2 * i + 3, 2 * i + 4):
            if 0 <= x < FXN:
                v[plane(x), :] = v[plane(x), :] + spread

    w0[plane(0), :] = nothing
    w0[plane(FXN - 1), :] = nothing

    @steps(STEPS)
    def _(k):
        x = 1 + k * FS
        at = span(x, FS)
        w0[at, :] = (f[at, :] + nb_sum(x, FS, fx, fy, fz, v, 1)) * ir[at, :]

    @steps(STEPS)
    def _(k):
        x = 1 + k * FS
        at = span(x, FS)
        new = (f[at, :] + nb_sum(x, FS, fx, fy, fz, w0, 1)) * ib[at, :]
        v[at, :] = new + w0[at, :]

    def crop(w):
        return rl(w, -32).reshape(FC, YR, 128)[:, FY0 : FY0 + 32, :64]

    @steps(64 // FC)
    def _(k):
        x = 3 + k * FC
        at = span(x, FC)
        w = v[at, :]
        r = f[at, :] - (dg[at, :] * w - nb_sum(x, FC, fx, fy, fz, v, 1))
        out[pl.ds(k * FC, FC)] = crop(w)
        res[pl.ds(k * FC, FC)] = crop(r)


def swap(low, high, axis):
    count = lax.axis_size(axis)
    up = [(i, i + 1) for i in range(count - 1)]
    down = [(i + 1, i) for i in range(count - 1)]
    return lax.ppermute(high, axis, up), lax.ppermute(low, axis, down)


def body(rhs_boxes, a_boxes, b_boxes, new_place):
    exchange = functools.partial(
        lax.all_to_all, axis_name=LAYER, split_axis=0, concat_axis=0, tiled=True
    )
    hbm = pl.BlockSpec(memory_space=pltpu.HBM)
    spread = pl.pallas_call(
        spread_kernel,
        out_shape=jax.ShapeDtypeStruct((32, 104, 128), F32),
        in_specs=[hbm] * 4,
        out_specs=pl.BlockSpec(memory_space=pltpu.VMEM),
        scratch_shapes=[
            pltpu.VMEM((3, 4, 32768), F32),
            pltpu.SMEM((1, 4), jnp.int32),
            pltpu.SemaphoreType.DMA((13,)),
        ],
        compiler_params=pltpu.CompilerParams(vmem_limit_bytes=8 << 20),
    )(
        *(
            pltpu.with_memory_space_constraint(w, pltpu.HBM)
            for w in (new_place, rhs_boxes, a_boxes, b_boxes)
        )
    )
    got = exchange(spread)
    place = got[:, 96, :4].astype(jnp.int32)
    (routed,) = call(route_kernel, [(32, 12, 8, 128)], smem=1)(place, got)
    got = exchange(routed)

    fine = (FXN * YR, 128)
    coarse = (CXN * YR, 128)
    ylo, yhi = call(strip_kernel, [(7 * 32, 128)] * 2, us=1)(got.reshape(3072, 128))
    ylo, yhi = swap(ylo, yhi, "gy")
    rh, aa, bb, xlo, xhi = call(brick_kernel, [fine] * 3 + [(7 * YR, 128)] * 2, us=4)(got)
    xlo, xhi = call(fine_x_kernel, [(4 * YR, 128)] * 2, [(7 * YR, 128)] * 2, us=1)(
        xlo, xhi, ylo, yhi
    )
    xlo, xhi = swap(xlo, xhi, "gx")
    rh, aa, bb, zlo, zhi = call(fine_y_kernel, [fine] * 3 + [(4 * YR, 128)] * 2)(
        rh, aa, bb, ylo, yhi
    )
    zlo, zhi = call(fine_z_kernel, [(4 * YR, 128)] * 2, us=1)(zlo, zhi, xlo, xhi)
    zlo, zhi = swap(zlo, zhi, "gz")
    f, fx, fy, fz, ir, ib, dg, v, c1, cylo, cyhi = call(
        coefficient_kernel,
        [fine] * 8 + [(640, 128)] + [(9 * 32, 128)] * 2,
        [fine, fine] + [(33 * YR, 128)] * 4,
        us=8,
    )(rh, aa, bb, xlo, xhi, zlo, zhi)
    cylo, cyhi = swap(cylo, cyhi, "gy")
    v, rc, ylo, yhi = call(
        presmooth_kernel,
        [fine, (640, 128)] + [(9 * 32, 128)] * 2,
        [(32 * YR, 128)],
        us=6,
    )(f, fx, fy, fz, ib, dg, v)
    cylo, cyhi, rc = lax.optimization_barrier((cylo, cyhi, rc))
    ylo, yhi = swap(ylo, yhi, "gy")
    ec, cxlo, cxhi = call(coef_x_kernel, [coarse] + [(9 * YR, 128)] * 2, us=1)(c1, cylo, cyhi)
    cxlo, cxhi = swap(cxlo, cxhi, "gx")
    er, vs, xlo, xhi = call(rhs_x_kernel, [coarse, fine] + [(9 * YR, 128)] * 2, us=1)(
        rc, v, ylo, yhi
    )
    xlo, xhi = swap(xlo, xhi, "gx")
    ec, czlo, czhi = call(coef_z_kernel, [coarse] + [(15 * YR, 128)] * 2)(ec, cxlo, cxhi)
    czlo, czhi = swap(czlo, czhi, "gz")
    rm, vs, zlo, zhi = call(
        rhs_z_kernel, [(25 * YR, 128), fine] + [(7 * YR, 128)] * 2
    )(er, vs, xlo, xhi)
    zlo, zhi = swap(zlo, zhi, "gz")
    merged = (MXN * YR, 128)
    coefs = call(merge_kernel, [merged] * 5, us=5)(ec, czlo, czhi)
    return tuple(
        call(
            finish_kernel,
            [(64, 32, 64)] * 2,
            [merged] * 3 + [fine, fine, (8 * YR, 128)],
            us=8,
        )(rm, vs, zlo, zhi, *coefs, f, fx, fy, fz, ir, ib, dg)
    )


def solution(mesh):
    return jax.shard_map(
        body,
        mesh=mesh,
        in_specs=(
            P("gz", ("gx", "gy"), None),
            P("gz", ("gx", "gy"), None),
            P("gz", ("gx", "gy"), None),
            P("gz", ("gx", "gy")),
        ),
        out_specs=(P("gx", "gy", "gz"), P("gx", "gy", "gz")),
        check_vma=False,
    )
```

```python
import functools

import jax
import jax.numpy as jnp
from jax import lax
from jax.experimental import pallas as pl
from jax.experimental.pallas import tpu as pltpu
from jax.sharding import PartitionSpec as P

LAYER = ("gx", "gy")
F32 = jnp.float32
YR = 40
FXN = 70
CXN = 50
FY0 = 4
CY0 = 12


def lane_of(rows):
    return lax.broadcasted_iota(jnp.int32, (rows, 128), 1)


def rl(v, shift):
    shift = shift % 128
    return v if shift == 0 else pltpu.roll(v, shift, 1)


def ry(v, shift):
    return pltpu.roll(v, shift % v.shape[0], 0)


def plane(index, rows=YR):
    if isinstance(index, int):
        return pl.ds(index * rows, rows)
    return pl.ds(pl.multiple_of(index * rows, 8), rows)


def every(start, count, stride):
    return pl.ds(start, count, stride=stride)


def own_lanes(v):
    lane = lane_of(v.shape[0])
    return jnp.where(lane < 64, v, 0.0)


def call(kernel, outs, scratch=(), limit=24, smem=0, us=2):
    def run(*args):
        return pl.pallas_call(
            kernel,
            out_shape=[jax.ShapeDtypeStruct(s, F32) for s in outs],
            in_specs=[pl.BlockSpec(memory_space=pltpu.SMEM)] * smem
            + [pl.BlockSpec(memory_space=pltpu.VMEM)] * (len(args) - smem),
            out_specs=[pl.BlockSpec(memory_space=pltpu.VMEM)] * len(outs),
            scratch_shapes=[pltpu.VMEM(s, F32) for s in scratch],
            cost_estimate=pl.CostEstimate(
                flops=0, transcendentals=0, bytes_accessed=us * 3_000_000
            ),
            compiler_params=pltpu.CompilerParams(vmem_limit_bytes=limit << 20),
        )(*args)

    return run


def spread_kernel(place_hbm, rhs, a, b, out, buf, place, sem):
    first = pltpu.make_async_copy(place_hbm, place, sem.at[12])
    first.start()
    copies = []
    for f, src in enumerate((rhs, a, b)):
        for part in range(4):
            at = pl.ds(part * 8192, 8192)
            copy = pltpu.make_async_copy(
                src.at[0, :, at], buf.at[f, :, at], sem.at[f * 4 + part]
            )
            copy.start()
            copies.append(copy)
    first.wait()
    lane = lane_of(8)
    mark = jnp.zeros((8, 128), F32)
    for k in range(4):
        mark = jnp.where(lane == k, place[0, k].astype(F32), mark)
    for j in range(32):
        out[j, 96:104, :] = mark
    for f in range(3):
        for part in range(4):
            copies[f * 4 + part].wait()
            for j in range(part * 8, part * 8 + 8):
                for m in range(8):
                    at = f * 32 + m * 4
                    out[j, at : at + 4, :] = buf[f, :, j * 1024 + m * 128 : j * 1024 + m * 128 + 128]


def route_kernel(place, got, out):
    @pl.loop(0, 32)
    def _(s):
        for k in range(4):
            p = place[s, k]
            t = lax.shift_right_logical(p, 2)
            q = lax.bitwise_and(p, 3)
            for f in range(3):
                out[t, f * 4 + q] = got[s, every(f * 32 + k, 8, 4), :]


DEPTH = (2, 2, 3)
FIRST = (0, 2, 4)
ITEMS = tuple((f, r) for f in range(3) for r in range(DEPTH[f]))


def strip_kernel(got, ylo, yhi):
    quarter = lane_of(32) // 32
    for f in range(3):
        for dst, row, first in ((ylo, 0, 0), (yhi, 7, 4 - DEPTH[f])):
            parts = [got[every((f * 4 + q) * 8 + row, 32, 96), :] for q in range(4)]
            for r in range(DEPTH[f]):
                w = rl(parts[0], -32 * (first + r))
                for q in range(1, 4):
                    w = jnp.where(quarter == q, rl(parts[q], 32 * (q - first - r)), w)
                dst[plane(FIRST[f] + r, 32), :] = w


def brick_kernel(got, rh, aa, bb, xlo, xhi):
    lane8 = lane_of(8)
    bricks = (rh, aa, bb)
    for br in bricks:
        br[...] = jnp.zeros_like(br)

    @pl.loop(0, 16)
    def _(k):
        for half in range(2):
            j = 2 * k + half
            for f, br in enumerate(bricks):
                for qx in range(2):
                    low = got[j, f * 4 + qx * 2]
                    high = got[j, f * 4 + qx * 2 + 1]
                    for c in range(4):
                        w = jnp.where(lane8 < 32, rl(low, -32 * c), rl(high, 32 - 32 * c))
                        start = (j + (qx * 32 + 3)) * YR + (FY0 + c)
                        br[every(start, 8, 4), :] = own_lanes(w)

    for f, br in enumerate(bricks):
        size = DEPTH[f] * YR
        xlo[pl.ds(FIRST[f] * YR, size), :] = br[pl.ds(3 * YR, size), :]
        xhi[pl.ds(FIRST[f] * YR, size), :] = br[pl.ds(67 * YR - size, size), :]


def fine_x_kernel(xlo, xhi, ylo, yhi, slo, shi, tlo, thi):
    lane = lane_of(YR)
    for own, out, tmp, upper in ((xlo, slo, tlo, False), (xhi, shi, thi, True)):
        tmp[...] = own[...]
        for n, (f, r) in enumerate(ITEMS):
            d = DEPTH[f]
            at = pl.ds(n * 32 + (32 - d if upper else 0), d)
            shift = 64 if upper else 0
            for src, row in ((ylo, FY0 - d + r), (yhi, FY0 + 32 + r)):
                tmp[every(FIRST[f] * YR + row, d, YR), :] = own_lanes(rl(src[at, :], shift))
        for m in range(4):
            v = tmp[plane(2 * m), :]
            w = rl(tmp[plane(2 * m + 1), :], 64) if m < 3 else jnp.zeros_like(v)
            out[plane(m), :] = jnp.where(lane < 64, v, w)


def z_slot(n):
    return plane(n // 18), 7 * (n % 18)


def fine_y_kernel(rh0, aa0, bb0, ylo, yhi, rh, aa, bb, zlo, zhi):
    lane = lane_of(YR)
    bricks = (rh, aa, bb)
    for br0, br in zip((rh0, aa0, bb0), bricks):
        br[...] = br0[...]
    for n, (f, r) in enumerate(ITEMS):
        for src, row in ((ylo, FY0 - DEPTH[f] + r), (yhi, FY0 + 32 + r)):
            v = src[plane(n, 32), :]
            bricks[f][every(3 * YR + row, 32, YR), :] = own_lanes(v)
            bricks[f][every(35 * YR + row, 32, YR), :] = own_lanes(rl(v, 64))
    lo = hi = None
    for n in range(64):
        group, base = z_slot(n)
        if base == 0:
            lo = jnp.zeros((YR, 128), F32)
            hi = lo
        for f, br in enumerate(bricks):
            v = br[plane(n + 3), :]
            at = base + FIRST[f]
            here = (lane >= at) & (lane < at + DEPTH[f])
            lo = jnp.where(here, rl(v, at), lo)
            hi = jnp.where(here, rl(v, at - 64 + DEPTH[f]), hi)
        if n % 18 == 17 or n == 63:
            zlo[group, :] = lo
            zhi[group, :] = hi


def x_plane(f, r, src):
    n = FIRST[f] + r
    return own_lanes(rl(src[plane(n // 2), :], 64 * (n % 2)))


def fine_z_kernel(zlo0, zhi0, xlo, xhi, zlo, zhi):
    lane = lane_of(YR)
    zlo[...] = zlo0[...]
    zhi[...] = zhi0[...]
    lo = zlo0[plane(3), :]
    hi = zhi0[plane(3), :]
    for f, r in ITEMS:
        for src, n in ((xlo, 64 + 3 - DEPTH[f] + r), (xhi, 67 + r)):
            v = x_plane(f, r, src)
            at = z_slot(n)[1] + FIRST[f]
            here = (lane >= at) & (lane < at + DEPTH[f])
            lo = jnp.where(here, rl(v, at), lo)
            hi = jnp.where(here, rl(v, at - 64 + DEPTH[f]), hi)
    zlo[plane(3), :] = lo
    zhi[plane(3), :] = hi


def span(x, count):
    if isinstance(x, int):
        return pl.ds(x * YR, count * YR)
    return pl.ds(pl.multiple_of(x * YR, 8), count * YR)


def nb_sum(x, count, cx, cy_ref, cz, v, step):
    at = span(x, count)
    here = v[at, :]
    cz = cz[span(x, count), :]
    total = cx[span(x, count), :] * v[span(x + 1, count), :]
    total = total + cx[span(x - 1, count), :] * v[span(x - 1, count), :]
    cy = cy_ref[at, :]
    total = total + (cy * ry(here, -1) + ry(cy * here, 1))
    return total + (cz * rl(here, -step) + rl(cz * here, step))


def steps(count):
    def run(step):
        for k in range(count):
            step(k)

    return run


def even_lane(rows):
    return (lane_of(rows) & 1) == 0


def red_rows(planes):
    row = lax.broadcasted_iota(jnp.int32, (YR, 128), 0)
    first = (row + lane_of(YR)) & 1
    return jnp.concatenate([first, 1 - first] * (planes // 2), axis=0) == 0


FC = 4
FS = 4
STEPS = 68 // FS


def zpair(s):
    return s + jnp.where(even_lane(s.shape[0]), rl(s, -1), rl(s, 1))


def halves(w):
    w = w.reshape(FC // 2, 2, YR, 128)
    return w[:, 0].reshape(FC // 2 * YR, 128), w[:, 1].reshape(FC // 2 * YR, 128)


def both(w):
    first, second = halves(w)
    return first + second


def coefficient_kernel(
    rh0, aa0, bb0, xlo, xhi, zlo, zhi, f, fx, fy, fz, ir, ib, dg, v, c1, slo, shi, a, b, ta, tx, ty, tz
):
    lane = lane_of(YR)
    for x in range(FXN):
        group, base = z_slot(x - 3 if 3 <= x < 67 else (64 + x if x < 3 else x))
        for n, (src, dst) in enumerate(((rh0, f), (aa0, a), (bb0, b))):
            d = DEPTH[n]
            if 3 <= x < 67:
                w = src[plane(x), :]
            elif 3 - d <= x < 3:
                w = x_plane(n, x - 3 + d, xlo)
            elif 67 <= x < 67 + d:
                w = x_plane(n, x - 67, xhi)
            else:
                dst[plane(x), :] = jnp.zeros((YR, 128), F32)
                continue
            at = base + FIRST[n]
            w = jnp.where(lane >= 128 - d, rl(zlo[group, :], -d - at), w)
            above = (lane >= 64) & (lane < 64 + d)
            dst[plane(x), :] = jnp.where(above, rl(zhi[group, :], 64 - at), w)

    def faces(x, count):
        here = b[span(x, count), :]
        fx[span(x, count), :] = 0.5 * (here + b[span(x + 1, count), :])
        fy[span(x, count), :] = 0.5 * (here + ry(here, -1))
        fz[span(x, count), :] = 0.5 * (here + rl(here, -1))

    faces(0, 1)

    @steps(STEPS)
    def _(k):
        faces(1 + k * FS, FS)

    nothing = jnp.zeros((YR, 128), F32)
    for ref in (fx, fy, fz):
        ref[plane(FXN - 1), :] = nothing
    for ref in (ir, ib, dg, v):
        ref[plane(0), :] = nothing
        ref[plane(FXN - 1), :] = nothing

    red = red_rows(FS)

    @steps(STEPS)
    def _(k):
        x = 1 + k * FS
        at = span(x, FS)
        py = fy[at, :]
        pz = fz[at, :]
        ax = a[at, :]
        total = fx[at, :] + fx[span(x - 1, FS), :] + py + ry(py, 1) + pz + rl(pz, 1)
        diag = ax + total
        inside = ax > 0.0
        one = jnp.where(inside, 1.0 / jnp.where(inside, diag, 1.0), 0.0)
        dg[at, :] = diag
        ir[at, :] = jnp.where(red, one, 0.0)
        ib[at, :] = jnp.where(red, 0.0, one)
        v[at, :] = jnp.where(red, f[at, :] * one, 0.0)

    edge = fx[plane(2), :]
    edge = edge + jnp.where(even_lane(YR), rl(edge, -1), rl(edge, 1))
    tx[plane(0), :] = edge

    @steps(64 // FC)
    def _(k):
        at = span(3 + k * FC, FC)
        to = span(k * (FC // 2), FC // 2)
        ta[to, :] = zpair(both(a[at, :]))
        tx[span(k * (FC // 2) + 1, FC // 2), :] = zpair(halves(fx[at, :])[1])
        ty[to, :] = zpair(both(fy[at, :]))
        tz[to, :] = both(fz[at, :])

    @steps(8)
    def _(k):
        base = k * 4 * YR
        even = even_lane(80)

        def rows(ref, first, planes=0):
            return ref[every(base + planes * YR + first, 80, 2), :]

        acoef = 0.125 * (rows(ta, 0) + rows(ta, 1))
        fxp = 0.25 * (rows(tx, 0, 1) + rows(tx, 1, 1))
        fxm = 0.25 * (rows(tx, 0) + rows(tx, 1))
        fyp = 0.25 * rows(ty, 1)
        s = 0.25 * (rows(tz, 0) + rows(tz, 1))
        fzp = jnp.where(even, rl(s, -1), s)
        diag = acoef + 0.25 * (fxp + fxm + fyp + ry(fyp, 1) + fzp + rl(fzp, 2))
        pa = jnp.where(even, fxp, fyp)
        pb = jnp.where(even, fzp, diag)
        c1[pl.ds(k * 80, 80), :] = jnp.where(lane_of(80) < 64, pa, rl(pb, 64))

    for dst, y0 in ((slo, 2), (shi, 9)):
        for r in range(9):
            dst[plane(r, 32), :] = c1[every(y0 + r, 32, 20), :]


def presmooth_kernel(f, fx, fy, fz, ib, dg, v0, v, rc, slo, shi, tr):
    for x in (0, FXN - 1):
        v[plane(x), :] = v0[plane(x), :]

    @steps(STEPS)
    def _(k):
        x = 1 + k * FS
        at = span(x, FS)
        new = (f[at, :] + nb_sum(x, FS, fx, fy, fz, v0, 1)) * ib[at, :]
        v[at, :] = v0[at, :] + new

    @steps(64 // FC)
    def _(k):
        x = 3 + k * FC
        at = span(x, FC)
        miss = f[at, :] - (dg[at, :] * v[at, :] - nb_sum(x, FC, fx, fy, fz, v, 1))
        tr[span(k * (FC // 2), FC // 2), :] = zpair(both(miss))

    @steps(8)
    def _(k):
        base = k * 4 * YR
        rhs = tr[every(base, 80, 2), :] + tr[every(base + 1, 80, 2), :]
        rc[pl.ds(k * 80, 80), :] = jnp.where(lane_of(80) < 64, 0.125 * rhs, 0.0)

    lane32 = lane_of(32)
    for dst, y0, fine0 in ((slo, 2, 0), (shi, 9, 29)):
        for r in range(9):
            w = rc[every(y0 + r, 32, 20), :]
            if r < 6:
                start = (3 + 32 * (r // 3)) * YR + FY0 + fine0 + r % 3
                w = jnp.where(lane32 < 64, w, rl(v[every(start, 32, YR), :], 64))
            dst[plane(r, 32), :] = w


def coarse_own(dst, src):
    dst[...] = jnp.zeros_like(dst)
    for i in range(32):
        dst[pl.ds((i + 9) * YR + CY0, 16), :] = src[pl.ds(i * 20 + 2, 16), :]


def coef_x_kernel(c1, ylo, yhi, ec, slo, shi):
    coarse_own(ec, c1)
    for src, crow in ((ylo, CY0 - 9), (yhi, CY0 + 16)):
        for r in range(9):
            ec[every(9 * YR + crow + r, 32, YR), :] = src[plane(r, 32), :]
    slo[...] = ec[pl.ds(9 * YR, 9 * YR), :]
    shi[...] = ec[pl.ds(32 * YR, 9 * YR), :]


def rhs_x_kernel(rc, v, ylo, yhi, er, vs, slo, shi):
    lane = lane_of(YR)
    coarse_own(er, rc)
    vs[...] = v[...]
    for src, crow, frow in ((ylo, CY0 - 9, FY0 - 3), (yhi, CY0 + 16, FY0 + 32)):
        for r in range(9):
            w = src[plane(r, 32), :]
            er[every(9 * YR + crow + r, 32, YR), :] = w
            if r < 6:
                start = (3 + 32 * (r // 3)) * YR + frow + r % 3
                vs[every(start, 32, YR), :] = own_lanes(rl(w, 64))
    for dst, first, fine in ((slo, 9, 3), (shi, 32, 64)):
        for i in range(9):
            w = er[plane(first + i), :]
            if i < 3:
                w = jnp.where(lane < 64, w, rl(own_lanes(vs[plane(fine + i), :]), 64))
            dst[plane(i), :] = w


def coef_slot(which, x):
    n = which * 50 + x
    return plane(n // 7), 18 * (n % 7)


def coef_z_kernel(ec0, xlo, xhi, ec, zlo, zhi):
    lane = lane_of(YR)
    ec[...] = ec0[...]
    ec[pl.ds(0, 9 * YR), :] = xlo[...]
    ec[pl.ds(41 * YR, 9 * YR), :] = xhi[...]
    lo = hi = None
    for n in range(100):
        at = 18 * (n % 7)
        if at == 0:
            lo = jnp.zeros((YR, 128), F32)
            hi = lo
        w = ec[plane(n % 50), :]
        base = 64 * (n // 50)
        here = (lane >= at) & (lane < at + 18)
        lo = jnp.where(here, rl(w, at - base), lo)
        hi = jnp.where(here, rl(w, at - base - 46), hi)
        if at == 108 or n == 99:
            zlo[plane(n // 7), :] = lo
            zhi[plane(n // 7), :] = hi


def smooth_slot(n):
    return plane(n // 12), 27 * (n // 3 % 4) + 18 + 3 * (n % 3)


def smooth_z_kernel(vs, zlo, zhi):
    lane = lane_of(YR)
    lo = hi = jnp.zeros((YR, 128), F32)
    zlo[plane(6), :] = lo
    zhi[plane(6), :] = lo
    for n in range(3, 67):
        group, to = smooth_slot(n)
        if n % 12 == 0:
            lo = hi = jnp.zeros((YR, 128), F32)
        w = vs[plane(n), :]
        here = (lane >= to) & (lane < to + 3)
        lo = jnp.where(here, rl(w, to), lo)
        hi = jnp.where(here, rl(w, to - 61), hi)
        if n % 12 == 11 or n == 66:
            zlo[group, :] = lo
            zhi[group, :] = hi


def rhs_z_kernel(er, xlo, xhi, plo, phi, rm, zlo, zhi):
    lane = lane_of(YR)
    even = even_lane(YR)
    own = lane < 64
    lo = hi = None
    for n in range(25):
        at = 27 * (n % 4)
        if at == 0:
            lo = plo[plane(n // 4), :]
            hi = phi[plane(n // 4), :]
        first = xlo[plane(n), :] if n < 9 else er[plane(n), :]
        second = xhi[plane(n - 16), :] if n >= 16 else er[plane(n + 25), :]
        w = jnp.where(even, first, second)
        rm[plane(n), :] = jnp.where(own, w, 0.0)
        here = (lane >= at) & (lane < at + 18)
        lo = jnp.where(here, rl(w, at), lo)
        hi = jnp.where(here, rl(w, at - 46), hi)
        for m in range(3 * n, 3 * n + 3):
            if m < 3 or 67 <= m < FXN:
                w = rl((xlo if m < 3 else xhi)[plane(m if m < 3 else m - 67), :], 64)
                to = smooth_slot(m)[1]
                here = (lane >= to) & (lane < to + 3)
                lo = jnp.where(here, rl(w, to), lo)
                hi = jnp.where(here, rl(w, to - 61), hi)
        if at == 81 or n == 24:
            zlo[plane(n // 4), :] = lo
            zhi[plane(n // 4), :] = hi


MXN = 28
CC = 1


def merge_kernel(ec, zlo, zhi, cx, cy, cz, jr, jb):
    lane = lane_of(YR)
    even = even_lane(YR)
    own = lane < 64
    below = lane >= 110
    above = (lane >= 64) & (lane < 82)
    nothing = jnp.zeros((YR, 128), F32)
    row = lax.broadcasted_iota(jnp.int32, (YR, 128), 0)
    reds = ((row + (lane >> 1) + jnp.where(even, 0, 1)) & 1) == 0

    def load(which, x):
        if not 0 <= x < CXN:
            return nothing
        group, at = coef_slot(which, x)
        w = jnp.where(own, rl(ec[plane(x), :], 64 * which), 0.0)
        w = jnp.where(below, rl(zlo[group, :], -18 - at), w)
        return jnp.where(above, rl(zhi[group, :], 64 - at), w)

    for p in range(27):
        first, second = load(0, p - 1), load(0, p + 24)
        cx[plane(p), :] = 0.25 * jnp.where(even, first, rl(second, 1))
        cy[plane(p), :] = 0.25 * jnp.where(even, rl(first, -1), second)
        first, second = load(1, p - 1), load(1, p + 24)
        cz[plane(p), :] = 0.25 * jnp.where(even, first, rl(second, 1))
        diag = jnp.where(even, rl(first, -1), second)
        inside = diag > 0.0
        one = jnp.where(inside, 1.0 / jnp.where(inside, diag, 1.0), 0.0)
        mine, other = (jr, jb) if p % 2 == 0 else (jb, jr)
        mine[plane(p), :] = jnp.where(reds, one, 0.0)
        other[plane(p), :] = jnp.where(reds, 0.0, one)
    for ref in (cx, cy, cz, jr, jb):
        ref[plane(27), :] = nothing


def finish_kernel(
    rm, vs, xlo, xhi, zlo, zhi, cx, cy, cz, jr, jb, f, fx, fy, fz, ir, ib, dg, out, res, cf, red, blk, v, w0, tmp
):
    lane = lane_of(YR)
    even = even_lane(YR)
    below = lane >= 110
    above = (lane >= 64) & (lane < 82)
    nothing = jnp.zeros((YR, 128), F32)
    for ref in (cf, red, blk):
        for p in (0, 26, 27):
            ref[plane(p), :] = nothing
    for n in range(25):
        at = 27 * (n % 4)
        w = jnp.where(below, rl(zlo[plane(n // 4), :], -18 - at), rm[plane(n), :])
        w = jnp.where(above, rl(zhi[plane(n // 4), :], 64 - at), w)
        cf[plane(n + 1), :] = w
        red[plane(n + 1), :] = w * jr[plane(n + 1), :]
    for n in range(FXN):
        group, at = smooth_slot(n)
        if n < 3:
            w = rl(xlo[plane(n), :], 64)
        elif n >= 67:
            w = rl(xhi[plane(n - 67), :], 64)
        else:
            w = vs[plane(n), :]
        w = own_lanes(w)
        low = rl(zlo[group, :], -3 - at)
        high = rl(zhi[group, :], 64 - at)
        w = jnp.where(lane >= 125, low, w)
        v[plane(n), :] = jnp.where((lane >= 64) & (lane < 67), high, w)

    def seam(ref):
        ref[plane(26), :] = jnp.where(even, rl(ref[plane(1), :], -1), 0.0)
        ref[plane(0), :] = jnp.where(even, 0.0, rl(ref[plane(25), :], 1))

    seam(red)

    for half in range(1, 8):
        src, dst, inv = (red, blk, jb) if half % 2 else (blk, red, jr)

        @steps(26 // CC)
        def _(k):
            x = 1 + k * CC
            at = span(x, CC)
            dst[at, :] = (cf[at, :] + nb_sum(x, CC, cx, cy, cz, src, 2)) * inv[at, :]

        seam(dst)

    for i in range(-2, 34):
        p = i + 10 if i + 9 < 25 else i + 9 - 24
        c = red[plane(p), :] + blk[plane(p), :]
        c = jnp.where(even, c, rl(c, 1)) if i + 9 < 25 else jnp.where(even, rl(c, -1), c)
        c = c[CY0 - 2 : CY0 + 18]
        slot = (i % 8) * YR
        tmp[every(slot, 20, 2), :] = c
        tmp[every(slot + 1, 20, 2), :] = c
        spread = tmp[pl.ds(slot, YR), :]
        for x in (2 * i + 3, 2 * i + 4):
            if 0 <= x < FXN:
                v[plane(x), :] = v[plane(x), :] + spread

    w0[plane(0), :] = nothing
    w0[plane(FXN - 1), :] = nothing

    @steps(STEPS)
    def _(k):
        x = 1 + k * FS
        at = span(x, FS)
        w0[at, :] = (f[at, :] + nb_sum(x, FS, fx, fy, fz, v, 1)) * ir[at, :]

    @steps(STEPS)
    def _(k):
        x = 1 + k * FS
        at = span(x, FS)
        new = (f[at, :] + nb_sum(x, FS, fx, fy, fz, w0, 1)) * ib[at, :]
        v[at, :] = new + w0[at, :]

    def crop(w):
        return w.reshape(FC, YR, 128)[:, FY0 : FY0 + 32, :64]

    @steps(64 // FC)
    def _(k):
        x = 3 + k * FC
        at = span(x, FC)
        w = v[at, :]
        r = f[at, :] - (dg[at, :] * w - nb_sum(x, FC, fx, fy, fz, v, 1))
        out[pl.ds(k * FC, FC)] = crop(w)
        res[pl.ds(k * FC, FC)] = crop(r)


def swap(low, high, axis):
    count = lax.axis_size(axis)
    up = [(i, i + 1) for i in range(count - 1)]
    down = [(i + 1, i) for i in range(count - 1)]
    return lax.ppermute(high, axis, up), lax.ppermute(low, axis, down)


def body(rhs_boxes, a_boxes, b_boxes, new_place):
    exchange = functools.partial(
        lax.all_to_all, axis_name=LAYER, split_axis=0, concat_axis=0, tiled=True
    )
    hbm = pl.BlockSpec(memory_space=pltpu.HBM)
    spread = pl.pallas_call(
        spread_kernel,
        out_shape=jax.ShapeDtypeStruct((32, 104, 128), F32),
        in_specs=[hbm] * 4,
        out_specs=pl.BlockSpec(memory_space=pltpu.VMEM),
        scratch_shapes=[
            pltpu.VMEM((3, 4, 32768), F32),
            pltpu.SMEM((1, 4), jnp.int32),
            pltpu.SemaphoreType.DMA((13,)),
        ],
        compiler_params=pltpu.CompilerParams(vmem_limit_bytes=8 << 20),
    )(
        *(
            pltpu.with_memory_space_constraint(w, pltpu.HBM)
            for w in (new_place, rhs_boxes, a_boxes, b_boxes)
        )
    )
    got = exchange(spread)
    place = got[:, 96, :4].astype(jnp.int32)
    (routed,) = call(route_kernel, [(32, 12, 8, 128)], smem=1)(place, got)
    got = exchange(routed)

    fine = (FXN * YR, 128)
    coarse = (CXN * YR, 128)
    ylo, yhi = call(strip_kernel, [(7 * 32, 128)] * 2, us=1)(got.reshape(3072, 128))
    ylo, yhi = swap(ylo, yhi, "gy")
    rh, aa, bb, xlo, xhi = call(brick_kernel, [fine] * 3 + [(7 * YR, 128)] * 2, us=4)(got)
    xlo, xhi = call(fine_x_kernel, [(4 * YR, 128)] * 2, [(7 * YR, 128)] * 2, us=1)(
        xlo, xhi, ylo, yhi
    )
    xlo, xhi = swap(xlo, xhi, "gx")
    rh, aa, bb, zlo, zhi = call(fine_y_kernel, [fine] * 3 + [(4 * YR, 128)] * 2)(
        rh, aa, bb, ylo, yhi
    )
    zlo, zhi = call(fine_z_kernel, [(4 * YR, 128)] * 2, us=1)(zlo, zhi, xlo, xhi)
    zlo, zhi = swap(zlo, zhi, "gz")
    f, fx, fy, fz, ir, ib, dg, v, c1, cylo, cyhi = call(
        coefficient_kernel,
        [fine] * 8 + [(640, 128)] + [(9 * 32, 128)] * 2,
        [fine, fine] + [(33 * YR, 128)] * 4,
        us=8,
    )(rh, aa, bb, xlo, xhi, zlo, zhi)
    cylo, cyhi = swap(cylo, cyhi, "gy")
    v, rc, ylo, yhi = call(
        presmooth_kernel,
        [fine, (640, 128)] + [(9 * 32, 128)] * 2,
        [(32 * YR, 128)],
        us=6,
    )(f, fx, fy, fz, ib, dg, v)
    cylo, cyhi, rc = lax.optimization_barrier((cylo, cyhi, rc))
    ylo, yhi = swap(ylo, yhi, "gy")
    ec, cxlo, cxhi = call(coef_x_kernel, [coarse] + [(9 * YR, 128)] * 2, us=1)(c1, cylo, cyhi)
    cxlo, cxhi = swap(cxlo, cxhi, "gx")
    er, vs, xlo, xhi = call(rhs_x_kernel, [coarse, fine] + [(9 * YR, 128)] * 2, us=1)(
        rc, v, ylo, yhi
    )
    xlo, xhi = swap(xlo, xhi, "gx")
    ec, czlo, czhi = call(coef_z_kernel, [coarse] + [(15 * YR, 128)] * 2)(ec, cxlo, cxhi)
    czlo, czhi = swap(czlo, czhi, "gz")
    plo, phi = call(smooth_z_kernel, [(7 * YR, 128)] * 2)(vs)
    rm, zlo, zhi = call(rhs_z_kernel, [(25 * YR, 128)] + [(7 * YR, 128)] * 2, us=1)(
        er, xlo, xhi, plo, phi
    )
    rxlo, rxhi = xlo, xhi
    zlo, zhi = swap(zlo, zhi, "gz")
    merged = (MXN * YR, 128)
    coefs = call(merge_kernel, [merged] * 5, us=5)(ec, czlo, czhi)
    return tuple(
        call(
            finish_kernel,
            [(64, 32, 64)] * 2,
            [merged] * 3 + [fine, fine, (8 * YR, 128)],
            us=8,
        )(rm, vs, rxlo, rxhi, zlo, zhi, *coefs, f, fx, fy, fz, ir, ib, dg)
    )


def solution(mesh):
    return jax.shard_map(
        body,
        mesh=mesh,
        in_specs=(
            P("gz", ("gx", "gy"), None),
            P("gz", ("gx", "gy"), None),
            P("gz", ("gx", "gy"), None),
            P("gz", ("gx", "gy")),
        ),
        out_specs=(P("gx", "gy", "gz"), P("gx", "gy", "gz")),
        check_vma=False,
    )
```

```python
import functools

import jax
import jax.numpy as jnp
from jax import lax
from jax.experimental import pallas as pl
from jax.experimental.pallas import tpu as pltpu
from jax.sharding import PartitionSpec as P

LAYER = ("gx", "gy")
F32 = jnp.float32
YR = 40
FXN = 70
CXN = 50
FY0 = 4
CY0 = 12


def lane_of(rows):
    return lax.broadcasted_iota(jnp.int32, (rows, 128), 1)


def rl(v, shift):
    shift = shift % 128
    return v if shift == 0 else pltpu.roll(v, shift, 1)


def ry(v, shift):
    return pltpu.roll(v, shift % v.shape[0], 0)


def plane(index, rows=YR):
    if isinstance(index, int):
        return pl.ds(index * rows, rows)
    return pl.ds(pl.multiple_of(index * rows, 8), rows)


def every(start, count, stride):
    return pl.ds(start, count, stride=stride)


def own_lanes(v):
    lane = lane_of(v.shape[0])
    return jnp.where(lane < 64, v, 0.0)


def call(kernel, outs, scratch=(), limit=24, us=2):
    def run(*args):
        return pl.pallas_call(
            kernel,
            out_shape=[jax.ShapeDtypeStruct(s, F32) for s in outs],
            in_specs=[pl.BlockSpec(memory_space=pltpu.VMEM)] * len(args),
            out_specs=[pl.BlockSpec(memory_space=pltpu.VMEM)] * len(outs),
            scratch_shapes=[pltpu.VMEM(s, F32) for s in scratch],
            cost_estimate=pl.CostEstimate(
                flops=0, transcendentals=0, bytes_accessed=us * 3_000_000
            ),
            compiler_params=pltpu.CompilerParams(vmem_limit_bytes=limit << 20),
        )(*args)

    return run


def spread_kernel(place_hbm, rhs, a, b, out, buf, place, sem):
    first = pltpu.make_async_copy(place_hbm, place, sem.at[12])
    first.start()
    copies = []
    for f, src in enumerate((rhs, a, b)):
        for part in range(4):
            at = pl.ds(part * 8192, 8192)
            copy = pltpu.make_async_copy(
                src.at[0, :, at], buf.at[f, :, at], sem.at[f * 4 + part]
            )
            copy.start()
            copies.append(copy)
    first.wait()
    lane = lane_of(1)
    mark = jnp.zeros((1, 128), F32)
    for k in range(4):
        mark = jnp.where(lane == k, place[0, k].astype(F32), mark)
    for j in range(32):
        out[j * 97 + 96 : j * 97 + 97, :] = mark
    for f in range(3):
        for part in range(4):
            copies[f * 4 + part].wait()
            for j in range(part * 8, part * 8 + 8):
                for m in range(8):
                    at = j * 97 + f * 32 + m * 4
                    out[at : at + 4, :] = buf[f, :, j * 1024 + m * 128 : j * 1024 + m * 128 + 128]


def route_kernel(got, out, ints, place, sem):
    ints[...] = got[every(96, 32, 97), :].astype(jnp.int32)
    copy = pltpu.make_async_copy(ints, place, sem.at[0])
    copy.start()
    copy.wait()

    @pl.loop(0, 32)
    def _(s):
        for k in range(4):
            p = place[s, k]
            t = lax.shift_right_logical(p, 2)
            q = lax.bitwise_and(p, 3)
            for f in range(3):
                out[t, f * 4 + q] = got[every(s * 97 + f * 32 + k, 8, 4), :]


DEPTH = (2, 2, 3)
FIRST = (0, 2, 4)
ITEMS = tuple((f, r) for f in range(3) for r in range(DEPTH[f]))


def strip_kernel(got, ylo, yhi):
    quarter = lane_of(32) // 32
    for f in range(3):
        for dst, row, first in ((ylo, 0, 0), (yhi, 7, 4 - DEPTH[f])):
            parts = [got[every((f * 4 + q) * 8 + row, 32, 96), :] for q in range(4)]
            for r in range(DEPTH[f]):
                w = rl(parts[0], -32 * (first + r))
                for q in range(1, 4):
                    w = jnp.where(quarter == q, rl(parts[q], 32 * (q - first - r)), w)
                dst[plane(FIRST[f] + r, 32), :] = w


def brick_kernel(got, rh, aa, bb, xlo, xhi):
    lane8 = lane_of(8)
    bricks = (rh, aa, bb)
    for br in bricks:
        br[...] = jnp.zeros_like(br)

    @pl.loop(0, 16)
    def _(k):
        for half in range(2):
            j = 2 * k + half
            for f, br in enumerate(bricks):
                for qx in range(2):
                    low = got[j, f * 4 + qx * 2]
                    high = got[j, f * 4 + qx * 2 + 1]
                    for c in range(4):
                        w = jnp.where(lane8 < 32, rl(low, -32 * c), rl(high, 32 - 32 * c))
                        start = (j + (qx * 32 + 3)) * YR + (FY0 + c)
                        br[every(start, 8, 4), :] = own_lanes(w)

    for f, br in enumerate(bricks):
        size = DEPTH[f] * YR
        xlo[pl.ds(FIRST[f] * YR, size), :] = br[pl.ds(3 * YR, size), :]
        xhi[pl.ds(FIRST[f] * YR, size), :] = br[pl.ds(67 * YR - size, size), :]


def fine_x_kernel(xlo, xhi, ylo, yhi, slo, shi, tlo, thi):
    lane = lane_of(YR)
    for own, out, tmp, upper in ((xlo, slo, tlo, False), (xhi, shi, thi, True)):
        tmp[...] = own[...]
        for n, (f, r) in enumerate(ITEMS):
            d = DEPTH[f]
            at = pl.ds(n * 32 + (32 - d if upper else 0), d)
            shift = 64 if upper else 0
            for src, row in ((ylo, FY0 - d + r), (yhi, FY0 + 32 + r)):
                tmp[every(FIRST[f] * YR + row, d, YR), :] = own_lanes(rl(src[at, :], shift))
        for m in range(4):
            v = tmp[plane(2 * m), :]
            w = rl(tmp[plane(2 * m + 1), :], 64) if m < 3 else jnp.zeros_like(v)
            out[plane(m), :] = jnp.where(lane < 64, v, w)


def z_slot(n):
    return plane(n // 18), 7 * (n % 18)


def fine_y_kernel(rh0, aa0, bb0, ylo, yhi, rh, aa, bb, zlo, zhi):
    lane = lane_of(YR)
    bricks = (rh, aa, bb)
    for br0, br in zip((rh0, aa0, bb0), bricks):
        br[...] = br0[...]
    for n, (f, r) in enumerate(ITEMS):
        for src, row in ((ylo, FY0 - DEPTH[f] + r), (yhi, FY0 + 32 + r)):
            v = src[plane(n, 32), :]
            bricks[f][every(3 * YR + row, 32, YR), :] = own_lanes(v)
            bricks[f][every(35 * YR + row, 32, YR), :] = own_lanes(rl(v, 64))
    lo = hi = None
    for n in range(64):
        group, base = z_slot(n)
        if base == 0:
            lo = jnp.zeros((YR, 128), F32)
            hi = lo
        for f, br in enumerate(bricks):
            v = br[plane(n + 3), :]
            at = base + FIRST[f]
            here = (lane >= at) & (lane < at + DEPTH[f])
            lo = jnp.where(here, rl(v, at), lo)
            hi = jnp.where(here, rl(v, at - 64 + DEPTH[f]), hi)
        if n % 18 == 17 or n == 63:
            zlo[group, :] = lo
            zhi[group, :] = hi


def x_plane(f, r, src):
    n = FIRST[f] + r
    return own_lanes(rl(src[plane(n // 2), :], 64 * (n % 2)))


def fine_z_kernel(zlo0, zhi0, xlo, xhi, zlo, zhi):
    lane = lane_of(YR)
    zlo[...] = zlo0[...]
    zhi[...] = zhi0[...]
    lo = zlo0[plane(3), :]
    hi = zhi0[plane(3), :]
    for f, r in ITEMS:
        for src, n in ((xlo, 64 + 3 - DEPTH[f] + r), (xhi, 67 + r)):
            v = x_plane(f, r, src)
            at = z_slot(n)[1] + FIRST[f]
            here = (lane >= at) & (lane < at + DEPTH[f])
            lo = jnp.where(here, rl(v, at), lo)
            hi = jnp.where(here, rl(v, at - 64 + DEPTH[f]), hi)
    zlo[plane(3), :] = lo
    zhi[plane(3), :] = hi


def span(x, count):
    if isinstance(x, int):
        return pl.ds(x * YR, count * YR)
    return pl.ds(pl.multiple_of(x * YR, 8), count * YR)


def nb_sum(x, count, cx, cy_ref, cz, v, step):
    at = span(x, count)
    here = v[at, :]
    cz = cz[span(x, count), :]
    total = cx[span(x, count), :] * v[span(x + 1, count), :]
    total = total + cx[span(x - 1, count), :] * v[span(x - 1, count), :]
    cy = cy_ref[at, :]
    total = total + (cy * ry(here, -1) + ry(cy * here, 1))
    return total + (cz * rl(here, -step) + rl(cz * here, step))


def steps(count):
    def run(step):
        for k in range(count):
            step(k)

    return run


def even_lane(rows):
    return (lane_of(rows) & 1) == 0


def red_rows(planes):
    row = lax.broadcasted_iota(jnp.int32, (YR, 128), 0)
    first = (row + lane_of(YR)) & 1
    return jnp.concatenate([first, 1 - first] * (planes // 2), axis=0) == 0


FC = 4
FS = 4
STEPS = 68 // FS


def zpair(s):
    return s + jnp.where(even_lane(s.shape[0]), rl(s, -1), rl(s, 1))


def halves(w):
    w = w.reshape(FC // 2, 2, YR, 128)
    return w[:, 0].reshape(FC // 2 * YR, 128), w[:, 1].reshape(FC // 2 * YR, 128)


def both(w):
    first, second = halves(w)
    return first + second


def coefficient_kernel(
    rh0, aa0, bb0, xlo, xhi, zlo, zhi, f, fx, fy, fz, ir, ib, dg, v, c1, slo, shi, a, b, ta, tx, ty, tz
):
    lane = lane_of(YR)
    for x in range(FXN):
        group, base = z_slot(x - 3 if 3 <= x < 67 else (64 + x if x < 3 else x))
        for n, (src, dst) in enumerate(((rh0, f), (aa0, a), (bb0, b))):
            d = DEPTH[n]
            if 3 <= x < 67:
                w = src[plane(x), :]
            elif 3 - d <= x < 3:
                w = x_plane(n, x - 3 + d, xlo)
            elif 67 <= x < 67 + d:
                w = x_plane(n, x - 67, xhi)
            else:
                dst[plane(x), :] = jnp.zeros((YR, 128), F32)
                continue
            at = base + FIRST[n]
            w = jnp.where(lane >= 128 - d, rl(zlo[group, :], -d - at), w)
            above = (lane >= 64) & (lane < 64 + d)
            dst[plane(x), :] = jnp.where(above, rl(zhi[group, :], 64 - at), w)

    def faces(x, count):
        here = b[span(x, count), :]
        fx[span(x, count), :] = 0.5 * (here + b[span(x + 1, count), :])
        fy[span(x, count), :] = 0.5 * (here + ry(here, -1))
        fz[span(x, count), :] = 0.5 * (here + rl(here, -1))

    faces(0, 1)

    @steps(STEPS)
    def _(k):
        faces(1 + k * FS, FS)

    nothing = jnp.zeros((YR, 128), F32)
    for ref in (fx, fy, fz):
        ref[plane(FXN - 1), :] = nothing
    for ref in (ir, ib, dg, v):
        ref[plane(0), :] = nothing
        ref[plane(FXN - 1), :] = nothing

    red = red_rows(FS)

    @steps(STEPS)
    def _(k):
        x = 1 + k * FS
        at = span(x, FS)
        py = fy[at, :]
        pz = fz[at, :]
        ax = a[at, :]
        total = fx[at, :] + fx[span(x - 1, FS), :] + py + ry(py, 1) + pz + rl(pz, 1)
        diag = ax + total
        inside = ax > 0.0
        one = jnp.where(inside, 1.0 / jnp.where(inside, diag, 1.0), 0.0)
        dg[at, :] = diag
        ir[at, :] = jnp.where(red, one, 0.0)
        ib[at, :] = jnp.where(red, 0.0, one)
        v[at, :] = jnp.where(red, f[at, :] * one, 0.0)

    edge = fx[plane(2), :]
    edge = edge + jnp.where(even_lane(YR), rl(edge, -1), rl(edge, 1))
    tx[plane(0), :] = edge

    @steps(64 // FC)
    def _(k):
        at = span(3 + k * FC, FC)
        to = span(k * (FC // 2), FC // 2)
        ta[to, :] = zpair(both(a[at, :]))
        tx[span(k * (FC // 2) + 1, FC // 2), :] = zpair(halves(fx[at, :])[1])
        ty[to, :] = zpair(both(fy[at, :]))
        tz[to, :] = both(fz[at, :])

    @steps(8)
    def _(k):
        base = k * 4 * YR
        even = even_lane(80)

        def rows(ref, first, planes=0):
            return ref[every(base + planes * YR + first, 80, 2), :]

        acoef = 0.125 * (rows(ta, 0) + rows(ta, 1))
        fxp = 0.25 * (rows(tx, 0, 1) + rows(tx, 1, 1))
        fxm = 0.25 * (rows(tx, 0) + rows(tx, 1))
        fyp = 0.25 * rows(ty, 1)
        s = 0.25 * (rows(tz, 0) + rows(tz, 1))
        fzp = jnp.where(even, rl(s, -1), s)
        diag = acoef + 0.25 * (fxp + fxm + fyp + ry(fyp, 1) + fzp + rl(fzp, 2))
        pa = jnp.where(even, fxp, fyp)
        pb = jnp.where(even, fzp, diag)
        c1[pl.ds(k * 80, 80), :] = jnp.where(lane_of(80) < 64, pa, rl(pb, 64))

    for dst, y0 in ((slo, 2), (shi, 9)):
        for r in range(9):
            dst[plane(r, 32), :] = c1[every(y0 + r, 32, 20), :]


def presmooth_kernel(f, fx, fy, fz, ib, dg, v0, v, rc, slo, shi, tr):
    for x in (0, FXN - 1):
        v[plane(x), :] = v0[plane(x), :]

    @steps(STEPS)
    def _(k):
        x = 1 + k * FS
        at = span(x, FS)
        new = (f[at, :] + nb_sum(x, FS, fx, fy, fz, v0, 1)) * ib[at, :]
        v[at, :] = v0[at, :] + new

    @steps(64 // FC)
    def _(k):
        x = 3 + k * FC
        at = span(x, FC)
        miss = f[at, :] - (dg[at, :] * v[at, :] - nb_sum(x, FC, fx, fy, fz, v, 1))
        tr[span(k * (FC // 2), FC // 2), :] = zpair(both(miss))

    @steps(8)
    def _(k):
        base = k * 4 * YR
        rhs = tr[every(base, 80, 2), :] + tr[every(base + 1, 80, 2), :]
        rc[pl.ds(k * 80, 80), :] = jnp.where(lane_of(80) < 64, 0.125 * rhs, 0.0)

    lane32 = lane_of(32)
    for dst, y0, fine0 in ((slo, 2, 0), (shi, 9, 29)):
        for r in range(9):
            w = rc[every(y0 + r, 32, 20), :]
            if r < 6:
                start = (3 + 32 * (r // 3)) * YR + FY0 + fine0 + r % 3
                w = jnp.where(lane32 < 64, w, rl(v[every(start, 32, YR), :], 64))
            dst[plane(r, 32), :] = w


def coarse_own(dst, src):
    dst[...] = jnp.zeros_like(dst)
    for i in range(32):
        dst[pl.ds((i + 9) * YR + CY0, 16), :] = src[pl.ds(i * 20 + 2, 16), :]


def coef_x_kernel(c1, ylo, yhi, ec, slo, shi):
    coarse_own(ec, c1)
    for src, crow in ((ylo, CY0 - 9), (yhi, CY0 + 16)):
        for r in range(9):
            ec[every(9 * YR + crow + r, 32, YR), :] = src[plane(r, 32), :]
    slo[...] = ec[pl.ds(9 * YR, 9 * YR), :]
    shi[...] = ec[pl.ds(32 * YR, 9 * YR), :]


def rhs_x_kernel(rc, v, ylo, yhi, er, vs, slo, shi):
    lane = lane_of(YR)
    coarse_own(er, rc)
    vs[...] = v[...]
    for src, crow, frow in ((ylo, CY0 - 9, FY0 - 3), (yhi, CY0 + 16, FY0 + 32)):
        for r in range(9):
            w = src[plane(r, 32), :]
            er[every(9 * YR + crow + r, 32, YR), :] = w
            if r < 6:
                start = (3 + 32 * (r // 3)) * YR + frow + r % 3
                vs[every(start, 32, YR), :] = own_lanes(rl(w, 64))
    for dst, first, fine in ((slo, 9, 3), (shi, 32, 64)):
        for i in range(9):
            w = er[plane(first + i), :]
            if i < 3:
                w = jnp.where(lane < 64, w, rl(own_lanes(vs[plane(fine + i), :]), 64))
            dst[plane(i), :] = w


def coef_slot(which, x):
    n = which * 50 + x
    return plane(n // 7), 18 * (n % 7)


def coef_z_kernel(ec0, xlo, xhi, ec, zlo, zhi):
    lane = lane_of(YR)
    ec[...] = ec0[...]
    ec[pl.ds(0, 9 * YR), :] = xlo[...]
    ec[pl.ds(41 * YR, 9 * YR), :] = xhi[...]
    lo = hi = None
    for n in range(100):
        at = 18 * (n % 7)
        if at == 0:
            lo = jnp.zeros((YR, 128), F32)
            hi = lo
        w = ec[plane(n % 50), :]
        base = 64 * (n // 50)
        here = (lane >= at) & (lane < at + 18)
        lo = jnp.where(here, rl(w, at - base), lo)
        hi = jnp.where(here, rl(w, at - base - 46), hi)
        if at == 108 or n == 99:
            zlo[plane(n // 7), :] = lo
            zhi[plane(n // 7), :] = hi


def smooth_slot(n):
    return plane(n // 12), 27 * (n // 3 % 4) + 18 + 3 * (n % 3)


def smooth_z_kernel(vs, zlo, zhi):
    lane = lane_of(YR)
    lo = hi = jnp.zeros((YR, 128), F32)
    zlo[plane(6), :] = lo
    zhi[plane(6), :] = lo
    for n in range(3, 67):
        group, to = smooth_slot(n)
        if n % 12 == 0:
            lo = hi = jnp.zeros((YR, 128), F32)
        w = vs[plane(n), :]
        here = (lane >= to) & (lane < to + 3)
        lo = jnp.where(here, rl(w, to), lo)
        hi = jnp.where(here, rl(w, to - 61), hi)
        if n % 12 == 11 or n == 66:
            zlo[group, :] = lo
            zhi[group, :] = hi


def rhs_z_kernel(er, xlo, xhi, plo, phi, rm, zlo, zhi):
    lane = lane_of(YR)
    even = even_lane(YR)
    own = lane < 64
    lo = hi = None
    for n in range(25):
        at = 27 * (n % 4)
        if at == 0:
            lo = plo[plane(n // 4), :]
            hi = phi[plane(n // 4), :]
        first = xlo[plane(n), :] if n < 9 else er[plane(n), :]
        second = xhi[plane(n - 16), :] if n >= 16 else er[plane(n + 25), :]
        w = jnp.where(even, first, second)
        rm[plane(n), :] = jnp.where(own, w, 0.0)
        here = (lane >= at) & (lane < at + 18)
        lo = jnp.where(here, rl(w, at), lo)
        hi = jnp.where(here, rl(w, at - 46), hi)
        for m in range(3 * n, 3 * n + 3):
            if m < 3 or 67 <= m < FXN:
                w = rl((xlo if m < 3 else xhi)[plane(m if m < 3 else m - 67), :], 64)
                to = smooth_slot(m)[1]
                here = (lane >= to) & (lane < to + 3)
                lo = jnp.where(here, rl(w, to), lo)
                hi = jnp.where(here, rl(w, to - 61), hi)
        if at == 81 or n == 24:
            zlo[plane(n // 4), :] = lo
            zhi[plane(n // 4), :] = hi


MXN = 28
CC = 1


def merge_kernel(ec, zlo, zhi, cx, cy, cz, jr, jb):
    lane = lane_of(YR)
    even = even_lane(YR)
    own = lane < 64
    below = lane >= 110
    above = (lane >= 64) & (lane < 82)
    nothing = jnp.zeros((YR, 128), F32)
    row = lax.broadcasted_iota(jnp.int32, (YR, 128), 0)
    reds = ((row + (lane >> 1) + jnp.where(even, 0, 1)) & 1) == 0

    def load(which, x):
        if not 0 <= x < CXN:
            return nothing
        group, at = coef_slot(which, x)
        w = jnp.where(own, rl(ec[plane(x), :], 64 * which), 0.0)
        w = jnp.where(below, rl(zlo[group, :], -18 - at), w)
        return jnp.where(above, rl(zhi[group, :], 64 - at), w)

    for p in range(27):
        first, second = load(0, p - 1), load(0, p + 24)
        cx[plane(p), :] = 0.25 * jnp.where(even, first, rl(second, 1))
        cy[plane(p), :] = 0.25 * jnp.where(even, rl(first, -1), second)
        first, second = load(1, p - 1), load(1, p + 24)
        cz[plane(p), :] = 0.25 * jnp.where(even, first, rl(second, 1))
        diag = jnp.where(even, rl(first, -1), second)
        inside = diag > 0.0
        one = jnp.where(inside, 1.0 / jnp.where(inside, diag, 1.0), 0.0)
        mine, other = (jr, jb) if p % 2 == 0 else (jb, jr)
        mine[plane(p), :] = jnp.where(reds, one, 0.0)
        other[plane(p), :] = jnp.where(reds, 0.0, one)
    for ref in (cx, cy, cz, jr, jb):
        ref[plane(27), :] = nothing


def finish_kernel(
    rm, vs, xlo, xhi, zlo, zhi, cx, cy, cz, jr, jb, f, fx, fy, fz, ir, ib, dg, out, res, cf, red, blk, v, w0, tmp
):
    lane = lane_of(YR)
    even = even_lane(YR)
    below = lane >= 110
    above = (lane >= 64) & (lane < 82)
    nothing = jnp.zeros((YR, 128), F32)
    for ref in (cf, red, blk):
        for p in (0, 26, 27):
            ref[plane(p), :] = nothing
    for n in range(25):
        at = 27 * (n % 4)
        w = jnp.where(below, rl(zlo[plane(n // 4), :], -18 - at), rm[plane(n), :])
        w = jnp.where(above, rl(zhi[plane(n // 4), :], 64 - at), w)
        cf[plane(n + 1), :] = w
        red[plane(n + 1), :] = w * jr[plane(n + 1), :]
    for n in range(FXN):
        group, at = smooth_slot(n)
        if n < 3:
            w = rl(xlo[plane(n), :], 64)
        elif n >= 67:
            w = rl(xhi[plane(n - 67), :], 64)
        else:
            w = vs[plane(n), :]
        w = own_lanes(w)
        low = rl(zlo[group, :], -3 - at)
        high = rl(zhi[group, :], 64 - at)
        w = jnp.where(lane >= 125, low, w)
        v[plane(n), :] = jnp.where((lane >= 64) & (lane < 67), high, w)

    def seam(ref):
        ref[plane(26), :] = jnp.where(even, rl(ref[plane(1), :], -1), 0.0)
        ref[plane(0), :] = jnp.where(even, 0.0, rl(ref[plane(25), :], 1))

    seam(red)

    for half in range(1, 8):
        src, dst, inv = (red, blk, jb) if half % 2 else (blk, red, jr)

        @steps(26 // CC)
        def _(k):
            x = 1 + k * CC
            at = span(x, CC)
            dst[at, :] = (cf[at, :] + nb_sum(x, CC, cx, cy, cz, src, 2)) * inv[at, :]

        seam(dst)

    for i in range(-2, 34):
        p = i + 10 if i + 9 < 25 else i + 9 - 24
        c = red[plane(p), :] + blk[plane(p), :]
        c = jnp.where(even, c, rl(c, 1)) if i + 9 < 25 else jnp.where(even, rl(c, -1), c)
        c = c[CY0 - 2 : CY0 + 18]
        slot = (i % 8) * YR
        tmp[every(slot, 20, 2), :] = c
        tmp[every(slot + 1, 20, 2), :] = c
        spread = tmp[pl.ds(slot, YR), :]
        for x in (2 * i + 3, 2 * i + 4):
            if 0 <= x < FXN:
                v[plane(x), :] = v[plane(x), :] + spread

    w0[plane(0), :] = nothing
    w0[plane(FXN - 1), :] = nothing

    @steps(STEPS)
    def _(k):
        x = 1 + k * FS
        at = span(x, FS)
        w0[at, :] = (f[at, :] + nb_sum(x, FS, fx, fy, fz, v, 1)) * ir[at, :]

    @steps(STEPS)
    def _(k):
        x = 1 + k * FS
        at = span(x, FS)
        new = (f[at, :] + nb_sum(x, FS, fx, fy, fz, w0, 1)) * ib[at, :]
        v[at, :] = new + w0[at, :]

    def crop(w):
        return w.reshape(FC, YR, 128)[:, FY0 : FY0 + 32, :64]

    @steps(64 // FC)
    def _(k):
        x = 3 + k * FC
        at = span(x, FC)
        w = v[at, :]
        r = f[at, :] - (dg[at, :] * w - nb_sum(x, FC, fx, fy, fz, v, 1))
        out[pl.ds(k * FC, FC)] = crop(w)
        res[pl.ds(k * FC, FC)] = crop(r)


def swap(low, high, axis):
    count = lax.axis_size(axis)
    up = [(i, i + 1) for i in range(count - 1)]
    down = [(i + 1, i) for i in range(count - 1)]
    return lax.ppermute(high, axis, up), lax.ppermute(low, axis, down)


def body(rhs_boxes, a_boxes, b_boxes, new_place):
    exchange = functools.partial(
        lax.all_to_all, axis_name=LAYER, split_axis=0, concat_axis=0, tiled=True
    )
    hbm = pl.BlockSpec(memory_space=pltpu.HBM)
    spread = pl.pallas_call(
        spread_kernel,
        out_shape=jax.ShapeDtypeStruct((32 * 97, 128), F32),
        in_specs=[hbm] * 4,
        out_specs=pl.BlockSpec(memory_space=pltpu.VMEM),
        scratch_shapes=[
            pltpu.VMEM((3, 4, 32768), F32),
            pltpu.SMEM((1, 4), jnp.int32),
            pltpu.SemaphoreType.DMA((13,)),
        ],
        compiler_params=pltpu.CompilerParams(vmem_limit_bytes=8 << 20),
    )(
        *(
            pltpu.with_memory_space_constraint(w, pltpu.HBM)
            for w in (new_place, rhs_boxes, a_boxes, b_boxes)
        )
    )
    got = exchange(spread.reshape(32, 1, 97 * 128)).reshape(32 * 97, 128)
    vmem = pl.BlockSpec(memory_space=pltpu.VMEM)
    routed = pl.pallas_call(
        route_kernel,
        out_shape=jax.ShapeDtypeStruct((32, 12, 8, 128), F32),
        in_specs=[vmem],
        out_specs=vmem,
        scratch_shapes=[
            pltpu.VMEM((32, 128), jnp.int32),
            pltpu.SMEM((32, 128), jnp.int32),
            pltpu.SemaphoreType.DMA((1,)),
        ],
        compiler_params=pltpu.CompilerParams(vmem_limit_bytes=8 << 20),
    )(got)
    got = exchange(routed)

    fine = (FXN * YR, 128)
    coarse = (CXN * YR, 128)
    ylo, yhi = call(strip_kernel, [(7 * 32, 128)] * 2, us=1)(got.reshape(3072, 128))
    ylo, yhi = swap(ylo, yhi, "gy")
    rh, aa, bb, xlo, xhi = call(brick_kernel, [fine] * 3 + [(7 * YR, 128)] * 2, us=4)(got)
    xlo, xhi = call(fine_x_kernel, [(4 * YR, 128)] * 2, [(7 * YR, 128)] * 2, us=1)(
        xlo, xhi, ylo, yhi
    )
    xlo, xhi = swap(xlo, xhi, "gx")
    rh, aa, bb, zlo, zhi = call(fine_y_kernel, [fine] * 3 + [(4 * YR, 128)] * 2)(
        rh, aa, bb, ylo, yhi
    )
    zlo, zhi = call(fine_z_kernel, [(4 * YR, 128)] * 2, us=1)(zlo, zhi, xlo, xhi)
    zlo, zhi = swap(zlo, zhi, "gz")
    f, fx, fy, fz, ir, ib, dg, v, c1, cylo, cyhi = call(
        coefficient_kernel,
        [fine] * 8 + [(640, 128)] + [(9 * 32, 128)] * 2,
        [fine, fine] + [(33 * YR, 128)] * 4,
        us=8,
    )(rh, aa, bb, xlo, xhi, zlo, zhi)
    cylo, cyhi = swap(cylo, cyhi, "gy")
    v, rc, ylo, yhi = call(
        presmooth_kernel,
        [fine, (640, 128)] + [(9 * 32, 128)] * 2,
        [(32 * YR, 128)],
        us=6,
    )(f, fx, fy, fz, ib, dg, v)
    cylo, cyhi, rc = lax.optimization_barrier((cylo, cyhi, rc))
    ylo, yhi = swap(ylo, yhi, "gy")
    ec, cxlo, cxhi = call(coef_x_kernel, [coarse] + [(9 * YR, 128)] * 2, us=1)(c1, cylo, cyhi)
    cxlo, cxhi = swap(cxlo, cxhi, "gx")
    er, vs, xlo, xhi = call(rhs_x_kernel, [coarse, fine] + [(9 * YR, 128)] * 2, us=1)(
        rc, v, ylo, yhi
    )
    xlo, xhi = swap(xlo, xhi, "gx")
    ec, czlo, czhi = call(coef_z_kernel, [coarse] + [(15 * YR, 128)] * 2)(ec, cxlo, cxhi)
    czlo, czhi = swap(czlo, czhi, "gz")
    plo, phi = call(smooth_z_kernel, [(7 * YR, 128)] * 2)(vs)
    rm, zlo, zhi = call(rhs_z_kernel, [(25 * YR, 128)] + [(7 * YR, 128)] * 2, us=1)(
        er, xlo, xhi, plo, phi
    )
    rxlo, rxhi = xlo, xhi
    zlo, zhi = swap(zlo, zhi, "gz")
    merged = (MXN * YR, 128)
    coefs = call(merge_kernel, [merged] * 5, us=5)(ec, czlo, czhi)
    return tuple(
        call(
            finish_kernel,
            [(64, 32, 64)] * 2,
            [merged] * 3 + [fine, fine, (8 * YR, 128)],
            us=8,
        )(rm, vs, rxlo, rxhi, zlo, zhi, *coefs, f, fx, fy, fz, ir, ib, dg)
    )


def solution(mesh):
    return jax.shard_map(
        body,
        mesh=mesh,
        in_specs=(
            P("gz", ("gx", "gy"), None),
            P("gz", ("gx", "gy"), None),
            P("gz", ("gx", "gy"), None),
            P("gz", ("gx", "gy")),
        ),
        out_specs=(P("gx", "gy", "gz"), P("gx", "gy", "gz")),
        check_vma=False,
    )
```

```python
import functools

import jax
import jax.numpy as jnp
from jax import lax
from jax.experimental import pallas as pl
from jax.experimental.pallas import tpu as pltpu
from jax.sharding import PartitionSpec as P

LAYER = ("gx", "gy")
F32 = jnp.float32
YR = 40
FXN = 70
CXN = 50
FY0 = 4
CY0 = 12


def lane_of(rows):
    return lax.broadcasted_iota(jnp.int32, (rows, 128), 1)


def rl(v, shift):
    shift = shift % 128
    return v if shift == 0 else pltpu.roll(v, shift, 1)


def ry(v, shift):
    return pltpu.roll(v, shift % v.shape[0], 0)


def plane(index, rows=YR):
    if isinstance(index, int):
        return pl.ds(index * rows, rows)
    return pl.ds(pl.multiple_of(index * rows, 8), rows)


def every(start, count, stride):
    return pl.ds(start, count, stride=stride)


def own_lanes(v):
    lane = lane_of(v.shape[0])
    return jnp.where(lane < 64, v, 0.0)


def call(kernel, outs, scratch=(), limit=24, us=2):
    def run(*args):
        return pl.pallas_call(
            kernel,
            out_shape=[jax.ShapeDtypeStruct(s, F32) for s in outs],
            in_specs=[pl.BlockSpec(memory_space=pltpu.VMEM)] * len(args),
            out_specs=[pl.BlockSpec(memory_space=pltpu.VMEM)] * len(outs),
            scratch_shapes=[pltpu.VMEM(s, F32) for s in scratch],
            cost_estimate=pl.CostEstimate(
                flops=0, transcendentals=0, bytes_accessed=us * 3_000_000
            ),
            compiler_params=pltpu.CompilerParams(vmem_limit_bytes=limit << 20),
        )(*args)

    return run


def spread_kernel(place_hbm, rhs, a, b, out, buf, place, sem):
    first = pltpu.make_async_copy(place_hbm, place, sem.at[12])
    first.start()
    copies = []
    for f, src in enumerate((rhs, a, b)):
        for part in range(4):
            at = pl.ds(part * 8192, 8192)
            copy = pltpu.make_async_copy(
                src.at[0, :, at], buf.at[f, :, at], sem.at[f * 4 + part]
            )
            copy.start()
            copies.append(copy)
    first.wait()
    lane = lane_of(1)
    mark = jnp.zeros((1, 128), F32)
    for k in range(4):
        mark = jnp.where(lane == k, place[0, k].astype(F32), mark)
    for j in range(32):
        out[j * 97 + 96 : j * 97 + 97, :] = mark
    for f in range(3):
        for part in range(4):
            copies[f * 4 + part].wait()
            for j in range(part * 8, part * 8 + 8):
                for m in range(8):
                    at = j * 97 + f * 32 + m * 4
                    out[at : at + 4, :] = buf[f, :, j * 1024 + m * 128 : j * 1024 + m * 128 + 128]


def route_kernel(got, out, ints, place, sem):
    ints[...] = got[every(96, 32, 97), :].astype(jnp.int32)
    copy = pltpu.make_async_copy(ints, place, sem.at[0])
    copy.start()
    copy.wait()

    @pl.loop(0, 32)
    def _(s):
        for k in range(4):
            p = place[s, k]
            t = lax.shift_right_logical(p, 2)
            q = lax.bitwise_and(p, 3)
            for f in range(3):
                out[t, f * 4 + q] = got[every(s * 97 + f * 32 + k, 8, 4), :]


DEPTH = (2, 2, 3)
FIRST = (0, 2, 4)
ITEMS = tuple((f, r) for f in range(3) for r in range(DEPTH[f]))


def strip_kernel(got, ylo, yhi):
    quarter = lane_of(32) // 32
    for f in range(3):
        for dst, row, first in ((ylo, 0, 0), (yhi, 7, 4 - DEPTH[f])):
            parts = [got[every((f * 4 + q) * 8 + row, 32, 96), :] for q in range(4)]
            for r in range(DEPTH[f]):
                w = rl(parts[0], -32 * (first + r))
                for q in range(1, 4):
                    w = jnp.where(quarter == q, rl(parts[q], 32 * (q - first - r)), w)
                dst[plane(FIRST[f] + r, 32), :] = w


def brick_kernel(got, rh, aa, bb, xlo, xhi):
    lane8 = lane_of(8)
    bricks = (rh, aa, bb)
    for br in bricks:
        br[...] = jnp.zeros_like(br)

    @pl.loop(0, 16)
    def _(k):
        for half in range(2):
            j = 2 * k + half
            for f, br in enumerate(bricks):
                for qx in range(2):
                    low = got[j, f * 4 + qx * 2]
                    high = got[j, f * 4 + qx * 2 + 1]
                    for c in range(4):
                        w = jnp.where(lane8 < 32, rl(low, -32 * c), rl(high, 32 - 32 * c))
                        start = (j + (qx * 32 + 3)) * YR + (FY0 + c)
                        br[every(start, 8, 4), :] = own_lanes(w)

    for f, br in enumerate(bricks):
        size = DEPTH[f] * YR
        xlo[pl.ds(FIRST[f] * YR, size), :] = br[pl.ds(3 * YR, size), :]
        xhi[pl.ds(FIRST[f] * YR, size), :] = br[pl.ds(67 * YR - size, size), :]


def fine_x_kernel(xlo, xhi, ylo, yhi, slo, shi, tlo, thi):
    lane = lane_of(YR)
    for own, out, tmp, upper in ((xlo, slo, tlo, False), (xhi, shi, thi, True)):
        tmp[...] = own[...]
        for n, (f, r) in enumerate(ITEMS):
            d = DEPTH[f]
            at = pl.ds(n * 32 + (32 - d if upper else 0), d)
            shift = 64 if upper else 0
            for src, row in ((ylo, FY0 - d + r), (yhi, FY0 + 32 + r)):
                tmp[every(FIRST[f] * YR + row, d, YR), :] = own_lanes(rl(src[at, :], shift))
        for m in range(4):
            v = tmp[plane(2 * m), :]
            w = rl(tmp[plane(2 * m + 1), :], 64) if m < 3 else jnp.zeros_like(v)
            out[plane(m), :] = jnp.where(lane < 64, v, w)


def z_slot(n):
    return plane(n // 18), 7 * (n % 18)


def fine_y_kernel(rh0, aa0, bb0, ylo, yhi, rh, aa, bb, zlo, zhi):
    lane = lane_of(YR)
    bricks = (rh, aa, bb)
    for br0, br in zip((rh0, aa0, bb0), bricks):
        br[...] = br0[...]
    for n, (f, r) in enumerate(ITEMS):
        for src, row in ((ylo, FY0 - DEPTH[f] + r), (yhi, FY0 + 32 + r)):
            v = src[plane(n, 32), :]
            bricks[f][every(3 * YR + row, 32, YR), :] = own_lanes(v)
            bricks[f][every(35 * YR + row, 32, YR), :] = own_lanes(rl(v, 64))
    lo = hi = None
    for n in range(64):
        group, base = z_slot(n)
        if base == 0:
            lo = jnp.zeros((YR, 128), F32)
            hi = lo
        for f, br in enumerate(bricks):
            v = br[plane(n + 3), :]
            at = base + FIRST[f]
            here = (lane >= at) & (lane < at + DEPTH[f])
            lo = jnp.where(here, rl(v, at), lo)
            hi = jnp.where(here, rl(v, at - 64 + DEPTH[f]), hi)
        if n % 18 == 17 or n == 63:
            zlo[group, :] = lo
            zhi[group, :] = hi


def x_plane(f, r, src):
    n = FIRST[f] + r
    return own_lanes(rl(src[plane(n // 2), :], 64 * (n % 2)))


def fine_z_kernel(zlo0, zhi0, xlo, xhi, zlo, zhi):
    lane = lane_of(YR)
    zlo[...] = zlo0[...]
    zhi[...] = zhi0[...]
    lo = zlo0[plane(3), :]
    hi = zhi0[plane(3), :]
    for f, r in ITEMS:
        for src, n in ((xlo, 64 + 3 - DEPTH[f] + r), (xhi, 67 + r)):
            v = x_plane(f, r, src)
            at = z_slot(n)[1] + FIRST[f]
            here = (lane >= at) & (lane < at + DEPTH[f])
            lo = jnp.where(here, rl(v, at), lo)
            hi = jnp.where(here, rl(v, at - 64 + DEPTH[f]), hi)
    zlo[plane(3), :] = lo
    zhi[plane(3), :] = hi


def span(x, count):
    if isinstance(x, int):
        return pl.ds(x * YR, count * YR)
    return pl.ds(pl.multiple_of(x * YR, 8), count * YR)


def nb_sum(x, count, cx, cy_ref, cz, v, step):
    at = span(x, count)
    here = v[at, :]
    cz = cz[span(x, count), :]
    total = cx[span(x, count), :] * v[span(x + 1, count), :]
    total = total + cx[span(x - 1, count), :] * v[span(x - 1, count), :]
    cy = cy_ref[at, :]
    total = total + (cy * ry(here, -1) + ry(cy * here, 1))
    return total + (cz * rl(here, -step) + rl(cz * here, step))


def steps(count):
    def run(step):
        for k in range(count):
            step(k)

    return run


def even_lane(rows):
    return (lane_of(rows) & 1) == 0


def red_rows(planes):
    row = lax.broadcasted_iota(jnp.int32, (YR, 128), 0)
    first = (row + lane_of(YR)) & 1
    return jnp.concatenate([first, 1 - first] * (planes // 2), axis=0) == 0


FC = 4
FS = 4
STEPS = 68 // FS


def zpair(s):
    return s + jnp.where(even_lane(s.shape[0]), rl(s, -1), rl(s, 1))


def halves(w):
    w = w.reshape(FC // 2, 2, YR, 128)
    return w[:, 0].reshape(FC // 2 * YR, 128), w[:, 1].reshape(FC // 2 * YR, 128)


def both(w):
    first, second = halves(w)
    return first + second


def mean_kernel(aa, bb, xlo, xhi, ta, tx, ty):
    tx[plane(0), :] = zpair(0.5 * (x_plane(2, 2, xlo) + bb[plane(3), :]))
    for i in range(32):
        x = 2 * i + 3
        first = bb[plane(x), :]
        second = bb[plane(x + 1), :]
        third = bb[plane(x + 2), :] if i < 31 else x_plane(2, 0, xhi)
        ta[plane(i), :] = zpair(aa[plane(x), :] + aa[plane(x + 1), :])
        tx[plane(i + 1), :] = zpair(0.5 * (second + third))
        ty[plane(i), :] = zpair(0.5 * (first + ry(first, -1)) + 0.5 * (second + ry(second, -1)))


def coefficient_kernel(
    rh0, aa0, bb0, xlo, xhi, zlo, zhi, ta, tx, ty, f, a, fx, fy, fz, c1, slo, shi, b, tz
):
    lane = lane_of(YR)
    for x in range(FXN):
        group, base = z_slot(x - 3 if 3 <= x < 67 else (64 + x if x < 3 else x))
        for n, (src, dst) in enumerate(((rh0, f), (aa0, a), (bb0, b))):
            d = DEPTH[n]
            if 3 <= x < 67:
                w = src[plane(x), :]
            elif 3 - d <= x < 3:
                w = x_plane(n, x - 3 + d, xlo)
            elif 67 <= x < 67 + d:
                w = x_plane(n, x - 67, xhi)
            else:
                dst[plane(x), :] = jnp.zeros((YR, 128), F32)
                continue
            at = base + FIRST[n]
            w = jnp.where(lane >= 128 - d, rl(zlo[group, :], -d - at), w)
            above = (lane >= 64) & (lane < 64 + d)
            dst[plane(x), :] = jnp.where(above, rl(zhi[group, :], 64 - at), w)

    def faces(x, count):
        here = b[span(x, count), :]
        fx[span(x, count), :] = 0.5 * (here + b[span(x + 1, count), :])
        fy[span(x, count), :] = 0.5 * (here + ry(here, -1))
        fz[span(x, count), :] = 0.5 * (here + rl(here, -1))

    faces(0, 1)

    @steps(STEPS)
    def _(k):
        faces(1 + k * FS, FS)

    nothing = jnp.zeros((YR, 128), F32)
    for ref in (fx, fy, fz):
        ref[plane(FXN - 1), :] = nothing
    @steps(64 // FC)
    def _(k):
        tz[span(k * (FC // 2), FC // 2), :] = both(fz[span(3 + k * FC, FC), :])

    @steps(8)
    def _(k):
        base = k * 4 * YR
        even = even_lane(80)

        def rows(ref, first, planes=0):
            return ref[every(base + planes * YR + first, 80, 2), :]

        acoef = 0.125 * (rows(ta, 0) + rows(ta, 1))
        fxp = 0.25 * (rows(tx, 0, 1) + rows(tx, 1, 1))
        fxm = 0.25 * (rows(tx, 0) + rows(tx, 1))
        fyp = 0.25 * rows(ty, 1)
        s = 0.25 * (rows(tz, 0) + rows(tz, 1))
        fzp = jnp.where(even, rl(s, -1), s)
        diag = acoef + 0.25 * (fxp + fxm + fyp + ry(fyp, 1) + fzp + rl(fzp, 2))
        pa = jnp.where(even, fxp, fyp)
        pb = jnp.where(even, fzp, diag)
        c1[pl.ds(k * 80, 80), :] = jnp.where(lane_of(80) < 64, pa, rl(pb, 64))

    for dst, y0 in ((slo, 2), (shi, 9)):
        for r in range(9):
            dst[plane(r, 32), :] = c1[every(y0 + r, 32, 20), :]


def presmooth_kernel(f, a, fx, fy, fz, ir, ib, dg, v, rc, slo, shi, tr, v0):
    for ref in (ir, ib, dg, v0):
        ref[plane(0), :] = jnp.zeros((YR, 128), F32)
        ref[plane(FXN - 1), :] = jnp.zeros((YR, 128), F32)

    red = red_rows(FS)

    @steps(STEPS)
    def _(k):
        x = 1 + k * FS
        at = span(x, FS)
        py = fy[at, :]
        pz = fz[at, :]
        ax = a[at, :]
        total = fx[at, :] + fx[span(x - 1, FS), :] + py + ry(py, 1) + pz + rl(pz, 1)
        diag = ax + total
        inside = ax > 0.0
        one = jnp.where(inside, 1.0 / jnp.where(inside, diag, 1.0), 0.0)
        dg[at, :] = diag
        ir[at, :] = jnp.where(red, one, 0.0)
        ib[at, :] = jnp.where(red, 0.0, one)
        v0[at, :] = jnp.where(red, f[at, :] * one, 0.0)

    for x in (0, FXN - 1):
        v[plane(x), :] = v0[plane(x), :]

    @steps(STEPS)
    def _(k):
        x = 1 + k * FS
        at = span(x, FS)
        new = (f[at, :] + nb_sum(x, FS, fx, fy, fz, v0, 1)) * ib[at, :]
        v[at, :] = v0[at, :] + new

    @steps(64 // FC)
    def _(k):
        x = 3 + k * FC
        at = span(x, FC)
        miss = f[at, :] - (dg[at, :] * v[at, :] - nb_sum(x, FC, fx, fy, fz, v, 1))
        tr[span(k * (FC // 2), FC // 2), :] = zpair(both(miss))

    @steps(8)
    def _(k):
        base = k * 4 * YR
        rhs = tr[every(base, 80, 2), :] + tr[every(base + 1, 80, 2), :]
        rc[pl.ds(k * 80, 80), :] = jnp.where(lane_of(80) < 64, 0.125 * rhs, 0.0)

    lane32 = lane_of(32)
    for dst, y0, fine0 in ((slo, 2, 0), (shi, 9, 29)):
        for r in range(9):
            w = rc[every(y0 + r, 32, 20), :]
            if r < 6:
                start = (3 + 32 * (r // 3)) * YR + FY0 + fine0 + r % 3
                w = jnp.where(lane32 < 64, w, rl(v[every(start, 32, YR), :], 64))
            dst[plane(r, 32), :] = w


def coarse_own(dst, src):
    dst[...] = jnp.zeros_like(dst)
    for i in range(32):
        dst[pl.ds((i + 9) * YR + CY0, 16), :] = src[pl.ds(i * 20 + 2, 16), :]


def coef_x_kernel(c1, ylo, yhi, ec, slo, shi):
    coarse_own(ec, c1)
    for src, crow in ((ylo, CY0 - 9), (yhi, CY0 + 16)):
        for r in range(9):
            ec[every(9 * YR + crow + r, 32, YR), :] = src[plane(r, 32), :]
    slo[...] = ec[pl.ds(9 * YR, 9 * YR), :]
    shi[...] = ec[pl.ds(32 * YR, 9 * YR), :]


def rhs_x_kernel(rc, v, ylo, yhi, er, vs, slo, shi):
    lane = lane_of(YR)
    coarse_own(er, rc)
    vs[...] = v[...]
    for src, crow, frow in ((ylo, CY0 - 9, FY0 - 3), (yhi, CY0 + 16, FY0 + 32)):
        for r in range(9):
            w = src[plane(r, 32), :]
            er[every(9 * YR + crow + r, 32, YR), :] = w
            if r < 6:
                start = (3 + 32 * (r // 3)) * YR + frow + r % 3
                vs[every(start, 32, YR), :] = own_lanes(rl(w, 64))
    for dst, first, fine in ((slo, 9, 3), (shi, 32, 64)):
        for i in range(9):
            w = er[plane(first + i), :]
            if i < 3:
                w = jnp.where(lane < 64, w, rl(own_lanes(vs[plane(fine + i), :]), 64))
            dst[plane(i), :] = w


def coef_slot(which, x):
    n = which * 50 + x
    return plane(n // 7), 18 * (n % 7)


def coef_z_kernel(ec0, xlo, xhi, ec, zlo, zhi):
    lane = lane_of(YR)
    ec[...] = ec0[...]
    ec[pl.ds(0, 9 * YR), :] = xlo[...]
    ec[pl.ds(41 * YR, 9 * YR), :] = xhi[...]
    lo = hi = None
    for n in range(100):
        at = 18 * (n % 7)
        if at == 0:
            lo = jnp.zeros((YR, 128), F32)
            hi = lo
        w = ec[plane(n % 50), :]
        base = 64 * (n // 50)
        here = (lane >= at) & (lane < at + 18)
        lo = jnp.where(here, rl(w, at - base), lo)
        hi = jnp.where(here, rl(w, at - base - 46), hi)
        if at == 108 or n == 99:
            zlo[plane(n // 7), :] = lo
            zhi[plane(n // 7), :] = hi


def smooth_slot(n):
    return plane(n // 12), 27 * (n // 3 % 4) + 18 + 3 * (n % 3)


def smooth_z_kernel(vs, zlo, zhi):
    lane = lane_of(YR)
    lo = hi = jnp.zeros((YR, 128), F32)
    zlo[plane(6), :] = lo
    zhi[plane(6), :] = lo
    for n in range(3, 67):
        group, to = smooth_slot(n)
        if n % 12 == 0:
            lo = hi = jnp.zeros((YR, 128), F32)
        w = vs[plane(n), :]
        here = (lane >= to) & (lane < to + 3)
        lo = jnp.where(here, rl(w, to), lo)
        hi = jnp.where(here, rl(w, to - 61), hi)
        if n % 12 == 11 or n == 66:
            zlo[group, :] = lo
            zhi[group, :] = hi


def rhs_z_kernel(er, xlo, xhi, plo, phi, rm, zlo, zhi):
    lane = lane_of(YR)
    even = even_lane(YR)
    own = lane < 64
    lo = hi = None
    for n in range(25):
        at = 27 * (n % 4)
        if at == 0:
            lo = plo[plane(n // 4), :]
            hi = phi[plane(n // 4), :]
        first = xlo[plane(n), :] if n < 9 else er[plane(n), :]
        second = xhi[plane(n - 16), :] if n >= 16 else er[plane(n + 25), :]
        w = jnp.where(even, first, second)
        rm[plane(n), :] = jnp.where(own, w, 0.0)
        here = (lane >= at) & (lane < at + 18)
        lo = jnp.where(here, rl(w, at), lo)
        hi = jnp.where(here, rl(w, at - 46), hi)
        for m in range(3 * n, 3 * n + 3):
            if m < 3 or 67 <= m < FXN:
                w = rl((xlo if m < 3 else xhi)[plane(m if m < 3 else m - 67), :], 64)
                to = smooth_slot(m)[1]
                here = (lane >= to) & (lane < to + 3)
                lo = jnp.where(here, rl(w, to), lo)
                hi = jnp.where(here, rl(w, to - 61), hi)
        if at == 81 or n == 24:
            zlo[plane(n // 4), :] = lo
            zhi[plane(n // 4), :] = hi


MXN = 28
CC = 1


def merge_kernel(ec, zlo, zhi, cx, cy, cz, jr, jb):
    lane = lane_of(YR)
    even = even_lane(YR)
    own = lane < 64
    below = lane >= 110
    above = (lane >= 64) & (lane < 82)
    nothing = jnp.zeros((YR, 128), F32)
    row = lax.broadcasted_iota(jnp.int32, (YR, 128), 0)
    reds = ((row + (lane >> 1) + jnp.where(even, 0, 1)) & 1) == 0

    def load(which, x):
        if not 0 <= x < CXN:
            return nothing
        group, at = coef_slot(which, x)
        w = jnp.where(own, rl(ec[plane(x), :], 64 * which), 0.0)
        w = jnp.where(below, rl(zlo[group, :], -18 - at), w)
        return jnp.where(above, rl(zhi[group, :], 64 - at), w)

    for p in range(27):
        first, second = load(0, p - 1), load(0, p + 24)
        cx[plane(p), :] = 0.25 * jnp.where(even, first, rl(second, 1))
        cy[plane(p), :] = 0.25 * jnp.where(even, rl(first, -1), second)
        first, second = load(1, p - 1), load(1, p + 24)
        cz[plane(p), :] = 0.25 * jnp.where(even, first, rl(second, 1))
        diag = jnp.where(even, rl(first, -1), second)
        inside = diag > 0.0
        one = jnp.where(inside, 1.0 / jnp.where(inside, diag, 1.0), 0.0)
        mine, other = (jr, jb) if p % 2 == 0 else (jb, jr)
        mine[plane(p), :] = jnp.where(reds, one, 0.0)
        other[plane(p), :] = jnp.where(reds, 0.0, one)
    for ref in (cx, cy, cz, jr, jb):
        ref[plane(27), :] = nothing


def finish_kernel(
    rm, vs, xlo, xhi, zlo, zhi, cx, cy, cz, jr, jb, f, fx, fy, fz, ir, ib, dg, out, res, cf, red, blk, v, w0, tmp
):
    lane = lane_of(YR)
    even = even_lane(YR)
    below = lane >= 110
    above = (lane >= 64) & (lane < 82)
    nothing = jnp.zeros((YR, 128), F32)
    for ref in (cf, red, blk):
        for p in (0, 26, 27):
            ref[plane(p), :] = nothing
    for n in range(25):
        at = 27 * (n % 4)
        w = jnp.where(below, rl(zlo[plane(n // 4), :], -18 - at), rm[plane(n), :])
        w = jnp.where(above, rl(zhi[plane(n // 4), :], 64 - at), w)
        cf[plane(n + 1), :] = w
        red[plane(n + 1), :] = w * jr[plane(n + 1), :]
    for n in range(FXN):
        group, at = smooth_slot(n)
        if n < 3:
            w = rl(xlo[plane(n), :], 64)
        elif n >= 67:
            w = rl(xhi[plane(n - 67), :], 64)
        else:
            w = vs[plane(n), :]
        w = own_lanes(w)
        low = rl(zlo[group, :], -3 - at)
        high = rl(zhi[group, :], 64 - at)
        w = jnp.where(lane >= 125, low, w)
        v[plane(n), :] = jnp.where((lane >= 64) & (lane < 67), high, w)

    def seam(ref):
        ref[plane(26), :] = jnp.where(even, rl(ref[plane(1), :], -1), 0.0)
        ref[plane(0), :] = jnp.where(even, 0.0, rl(ref[plane(25), :], 1))

    seam(red)

    for half in range(1, 8):
        src, dst, inv = (red, blk, jb) if half % 2 else (blk, red, jr)

        @steps(26 // CC)
        def _(k):
            x = 1 + k * CC
            at = span(x, CC)
            dst[at, :] = (cf[at, :] + nb_sum(x, CC, cx, cy, cz, src, 2)) * inv[at, :]

        seam(dst)

    for i in range(-2, 34):
        p = i + 10 if i + 9 < 25 else i + 9 - 24
        c = red[plane(p), :] + blk[plane(p), :]
        c = jnp.where(even, c, rl(c, 1)) if i + 9 < 25 else jnp.where(even, rl(c, -1), c)
        c = c[CY0 - 2 : CY0 + 18]
        slot = (i % 8) * YR
        tmp[every(slot, 20, 2), :] = c
        tmp[every(slot + 1, 20, 2), :] = c
        spread = tmp[pl.ds(slot, YR), :]
        for x in (2 * i + 3, 2 * i + 4):
            if 0 <= x < FXN:
                v[plane(x), :] = v[plane(x), :] + spread

    w0[plane(0), :] = nothing
    w0[plane(FXN - 1), :] = nothing

    @steps(STEPS)
    def _(k):
        x = 1 + k * FS
        at = span(x, FS)
        w0[at, :] = (f[at, :] + nb_sum(x, FS, fx, fy, fz, v, 1)) * ir[at, :]

    @steps(STEPS)
    def _(k):
        x = 1 + k * FS
        at = span(x, FS)
        new = (f[at, :] + nb_sum(x, FS, fx, fy, fz, w0, 1)) * ib[at, :]
        v[at, :] = new + w0[at, :]

    def crop(w):
        return w.reshape(FC, YR, 128)[:, FY0 : FY0 + 32, :64]

    @steps(64 // FC)
    def _(k):
        x = 3 + k * FC
        at = span(x, FC)
        w = v[at, :]
        r = f[at, :] - (dg[at, :] * w - nb_sum(x, FC, fx, fy, fz, v, 1))
        out[pl.ds(k * FC, FC)] = crop(w)
        res[pl.ds(k * FC, FC)] = crop(r)


def swap(low, high, axis):
    count = lax.axis_size(axis)
    up = [(i, i + 1) for i in range(count - 1)]
    down = [(i + 1, i) for i in range(count - 1)]
    return lax.ppermute(high, axis, up), lax.ppermute(low, axis, down)


def body(rhs_boxes, a_boxes, b_boxes, new_place):
    exchange = functools.partial(
        lax.all_to_all, axis_name=LAYER, split_axis=0, concat_axis=0, tiled=True
    )
    hbm = pl.BlockSpec(memory_space=pltpu.HBM)
    spread = pl.pallas_call(
        spread_kernel,
        out_shape=jax.ShapeDtypeStruct((32 * 97, 128), F32),
        in_specs=[hbm] * 4,
        out_specs=pl.BlockSpec(memory_space=pltpu.VMEM),
        scratch_shapes=[
            pltpu.VMEM((3, 4, 32768), F32),
            pltpu.SMEM((1, 4), jnp.int32),
            pltpu.SemaphoreType.DMA((13,)),
        ],
        compiler_params=pltpu.CompilerParams(vmem_limit_bytes=8 << 20),
    )(
        *(
            pltpu.with_memory_space_constraint(w, pltpu.HBM)
            for w in (new_place, rhs_boxes, a_boxes, b_boxes)
        )
    )
    got = exchange(spread.reshape(32, 1, 97 * 128)).reshape(32 * 97, 128)
    vmem = pl.BlockSpec(memory_space=pltpu.VMEM)
    routed = pl.pallas_call(
        route_kernel,
        out_shape=jax.ShapeDtypeStruct((32, 12, 8, 128), F32),
        in_specs=[vmem],
        out_specs=vmem,
        scratch_shapes=[
            pltpu.VMEM((32, 128), jnp.int32),
            pltpu.SMEM((32, 128), jnp.int32),
            pltpu.SemaphoreType.DMA((1,)),
        ],
        compiler_params=pltpu.CompilerParams(vmem_limit_bytes=8 << 20),
    )(got)
    got = exchange(routed)

    fine = (FXN * YR, 128)
    coarse = (CXN * YR, 128)
    ylo, yhi = call(strip_kernel, [(7 * 32, 128)] * 2, us=1)(got.reshape(3072, 128))
    ylo, yhi = swap(ylo, yhi, "gy")
    rh, aa, bb, xlo, xhi = call(brick_kernel, [fine] * 3 + [(7 * YR, 128)] * 2, us=4)(got)
    xlo, xhi = call(fine_x_kernel, [(4 * YR, 128)] * 2, [(7 * YR, 128)] * 2, us=1)(
        xlo, xhi, ylo, yhi
    )
    xlo, xhi = swap(xlo, xhi, "gx")
    rh, aa, bb, zlo, zhi = call(fine_y_kernel, [fine] * 3 + [(4 * YR, 128)] * 2)(
        rh, aa, bb, ylo, yhi
    )
    zlo, zhi = call(fine_z_kernel, [(4 * YR, 128)] * 2, us=1)(zlo, zhi, xlo, xhi)
    zlo, zhi = swap(zlo, zhi, "gz")
    means = call(mean_kernel, [(33 * YR, 128)] * 3)(aa, bb, xlo, xhi)
    f, a, fx, fy, fz, c1, cylo, cyhi = call(
        coefficient_kernel,
        [fine] * 5 + [(640, 128)] + [(9 * 32, 128)] * 2,
        [fine, (33 * YR, 128)],
        us=4,
    )(rh, aa, bb, xlo, xhi, zlo, zhi, *means)
    cylo, cyhi = swap(cylo, cyhi, "gy")
    ir, ib, dg, v, rc, ylo, yhi = call(
        presmooth_kernel,
        [fine] * 4 + [(640, 128)] + [(9 * 32, 128)] * 2,
        [(32 * YR, 128), fine],
        us=6,
    )(f, a, fx, fy, fz)
    cylo, cyhi, rc = lax.optimization_barrier((cylo, cyhi, rc))
    ylo, yhi = swap(ylo, yhi, "gy")
    ec, cxlo, cxhi = call(coef_x_kernel, [coarse] + [(9 * YR, 128)] * 2, us=1)(c1, cylo, cyhi)
    cxlo, cxhi = swap(cxlo, cxhi, "gx")
    er, vs, xlo, xhi = call(rhs_x_kernel, [coarse, fine] + [(9 * YR, 128)] * 2, us=1)(
        rc, v, ylo, yhi
    )
    xlo, xhi = swap(xlo, xhi, "gx")
    ec, czlo, czhi = call(coef_z_kernel, [coarse] + [(15 * YR, 128)] * 2)(ec, cxlo, cxhi)
    czlo, czhi = swap(czlo, czhi, "gz")
    plo, phi = call(smooth_z_kernel, [(7 * YR, 128)] * 2)(vs)
    rm, zlo, zhi = call(rhs_z_kernel, [(25 * YR, 128)] + [(7 * YR, 128)] * 2, us=1)(
        er, xlo, xhi, plo, phi
    )
    rxlo, rxhi = xlo, xhi
    zlo, zhi = swap(zlo, zhi, "gz")
    merged = (MXN * YR, 128)
    coefs = call(merge_kernel, [merged] * 5, us=5)(ec, czlo, czhi)
    return tuple(
        call(
            finish_kernel,
            [(64, 32, 64)] * 2,
            [merged] * 3 + [fine, fine, (8 * YR, 128)],
            us=8,
        )(rm, vs, rxlo, rxhi, zlo, zhi, *coefs, f, fx, fy, fz, ir, ib, dg)
    )


def solution(mesh):
    return jax.shard_map(
        body,
        mesh=mesh,
        in_specs=(
            P("gz", ("gx", "gy"), None),
            P("gz", ("gx", "gy"), None),
            P("gz", ("gx", "gy"), None),
            P("gz", ("gx", "gy")),
        ),
        out_specs=(P("gx", "gy", "gz"), P("gx", "gy", "gz")),
        check_vma=False,
    )
```

```python
import functools

import jax
import jax.numpy as jnp
from jax import lax
from jax.experimental import pallas as pl
from jax.experimental.pallas import tpu as pltpu
from jax.sharding import PartitionSpec as P

LAYER = ("gx", "gy")
F32 = jnp.float32
YR = 40
FXN = 70
CXN = 50
FY0 = 4
CY0 = 12


def lane_of(rows):
    return lax.broadcasted_iota(jnp.int32, (rows, 128), 1)


def rl(v, shift):
    shift = shift % 128
    return v if shift == 0 else pltpu.roll(v, shift, 1)


def ry(v, shift):
    return pltpu.roll(v, shift % v.shape[0], 0)


def plane(index, rows=YR):
    if isinstance(index, int):
        return pl.ds(index * rows, rows)
    return pl.ds(pl.multiple_of(index * rows, 8), rows)


def every(start, count, stride):
    return pl.ds(start, count, stride=stride)


def own_lanes(v):
    lane = lane_of(v.shape[0])
    return jnp.where(lane < 64, v, 0.0)


def call(kernel, outs, scratch=(), limit=24, us=2):
    def run(*args):
        return pl.pallas_call(
            kernel,
            out_shape=[jax.ShapeDtypeStruct(s, F32) for s in outs],
            in_specs=[pl.BlockSpec(memory_space=pltpu.VMEM)] * len(args),
            out_specs=[pl.BlockSpec(memory_space=pltpu.VMEM)] * len(outs),
            scratch_shapes=[pltpu.VMEM(s, F32) for s in scratch],
            cost_estimate=pl.CostEstimate(
                flops=0, transcendentals=0, bytes_accessed=us * 3_000_000
            ),
            compiler_params=pltpu.CompilerParams(vmem_limit_bytes=limit << 20),
        )(*args)

    return run


def spread_kernel(place_hbm, rhs, a, b, out, buf, place, sem):
    first = pltpu.make_async_copy(place_hbm, place, sem.at[12])
    first.start()
    copies = []
    for f, src in enumerate((rhs, a, b)):
        for part in range(4):
            at = pl.ds(part * 8192, 8192)
            copy = pltpu.make_async_copy(
                src.at[0, :, at], buf.at[f, :, at], sem.at[f * 4 + part]
            )
            copy.start()
            copies.append(copy)
    first.wait()
    lane = lane_of(1)
    mark = jnp.zeros((1, 128), F32)
    for k in range(4):
        mark = jnp.where(lane == k, place[0, k].astype(F32), mark)
    for j in range(32):
        out[j * 97 + 96 : j * 97 + 97, :] = mark
    for f in range(3):
        for part in range(4):
            copies[f * 4 + part].wait()
            for j in range(part * 8, part * 8 + 8):
                for m in range(8):
                    at = j * 97 + f * 32 + m * 4
                    out[at : at + 4, :] = buf[f, :, j * 1024 + m * 128 : j * 1024 + m * 128 + 128]


def route_kernel(got, out, ints, place, sem):
    ints[...] = got[every(96, 32, 97), :].astype(jnp.int32)
    copy = pltpu.make_async_copy(ints, place, sem.at[0])
    copy.start()
    copy.wait()

    @pl.loop(0, 32)
    def _(s):
        for k in range(4):
            p = place[s, k]
            t = lax.shift_right_logical(p, 2)
            q = lax.bitwise_and(p, 3)
            for f in range(3):
                out[t, f * 4 + q] = got[every(s * 97 + f * 32 + k, 8, 4), :]


DEPTH = (2, 2, 3)
FIRST = (0, 2, 4)
ITEMS = tuple((f, r) for f in range(3) for r in range(DEPTH[f]))


def strip_kernel(got, ylo, yhi):
    quarter = lane_of(32) // 32
    for f in range(3):
        for dst, row, first in ((ylo, 0, 0), (yhi, 7, 4 - DEPTH[f])):
            parts = [got[every((f * 4 + q) * 8 + row, 32, 96), :] for q in range(4)]
            for r in range(DEPTH[f]):
                w = rl(parts[0], -32 * (first + r))
                for q in range(1, 4):
                    w = jnp.where(quarter == q, rl(parts[q], 32 * (q - first - r)), w)
                dst[plane(FIRST[f] + r, 32), :] = w


def brick_kernel(got, rh, aa, bb, xlo, xhi):
    lane8 = lane_of(8)
    bricks = (rh, aa, bb)
    for br in bricks:
        br[...] = jnp.zeros_like(br)

    @pl.loop(0, 16)
    def _(k):
        for half in range(2):
            j = 2 * k + half
            for f, br in enumerate(bricks):
                for qx in range(2):
                    low = got[j, f * 4 + qx * 2]
                    high = got[j, f * 4 + qx * 2 + 1]
                    for c in range(4):
                        w = jnp.where(lane8 < 32, rl(low, -32 * c), rl(high, 32 - 32 * c))
                        start = (j + (qx * 32 + 3)) * YR + (FY0 + c)
                        br[every(start, 8, 4), :] = own_lanes(w)

    for f, br in enumerate(bricks):
        size = DEPTH[f] * YR
        xlo[pl.ds(FIRST[f] * YR, size), :] = br[pl.ds(3 * YR, size), :]
        xhi[pl.ds(FIRST[f] * YR, size), :] = br[pl.ds(67 * YR - size, size), :]


def fine_x_kernel(xlo, xhi, ylo, yhi, slo, shi, tlo, thi):
    lane = lane_of(YR)
    for own, out, tmp, upper in ((xlo, slo, tlo, False), (xhi, shi, thi, True)):
        tmp[...] = own[...]
        for n, (f, r) in enumerate(ITEMS):
            d = DEPTH[f]
            at = pl.ds(n * 32 + (32 - d if upper else 0), d)
            shift = 64 if upper else 0
            for src, row in ((ylo, FY0 - d + r), (yhi, FY0 + 32 + r)):
                tmp[every(FIRST[f] * YR + row, d, YR), :] = own_lanes(rl(src[at, :], shift))
        for m in range(4):
            v = tmp[plane(2 * m), :]
            w = rl(tmp[plane(2 * m + 1), :], 64) if m < 3 else jnp.zeros_like(v)
            out[plane(m), :] = jnp.where(lane < 64, v, w)


def z_slot(n):
    return plane(n // 18), 7 * (n % 18)


def fine_y_kernel(rh0, aa0, bb0, ylo, yhi, rh, aa, bb, zlo, zhi):
    lane = lane_of(YR)
    bricks = (rh, aa, bb)
    for br0, br in zip((rh0, aa0, bb0), bricks):
        br[...] = br0[...]
    for n, (f, r) in enumerate(ITEMS):
        for src, row in ((ylo, FY0 - DEPTH[f] + r), (yhi, FY0 + 32 + r)):
            v = src[plane(n, 32), :]
            bricks[f][every(3 * YR + row, 32, YR), :] = own_lanes(v)
            bricks[f][every(35 * YR + row, 32, YR), :] = own_lanes(rl(v, 64))
    lo = hi = None
    for n in range(64):
        group, base = z_slot(n)
        if base == 0:
            lo = jnp.zeros((YR, 128), F32)
            hi = lo
        for f, br in enumerate(bricks):
            v = br[plane(n + 3), :]
            at = base + FIRST[f]
            here = (lane >= at) & (lane < at + DEPTH[f])
            lo = jnp.where(here, rl(v, at), lo)
            hi = jnp.where(here, rl(v, at - 64 + DEPTH[f]), hi)
        if n % 18 == 17 or n == 63:
            zlo[group, :] = lo
            zhi[group, :] = hi


def x_plane(f, r, src):
    n = FIRST[f] + r
    return own_lanes(rl(src[plane(n // 2), :], 64 * (n % 2)))


def fine_z_kernel(zlo0, zhi0, xlo, xhi, zlo, zhi):
    lane = lane_of(YR)
    zlo[...] = zlo0[...]
    zhi[...] = zhi0[...]
    lo = zlo0[plane(3), :]
    hi = zhi0[plane(3), :]
    for f, r in ITEMS:
        for src, n in ((xlo, 64 + 3 - DEPTH[f] + r), (xhi, 67 + r)):
            v = x_plane(f, r, src)
            at = z_slot(n)[1] + FIRST[f]
            here = (lane >= at) & (lane < at + DEPTH[f])
            lo = jnp.where(here, rl(v, at), lo)
            hi = jnp.where(here, rl(v, at - 64 + DEPTH[f]), hi)
    zlo[plane(3), :] = lo
    zhi[plane(3), :] = hi


def span(x, count):
    if isinstance(x, int):
        return pl.ds(x * YR, count * YR)
    return pl.ds(pl.multiple_of(x * YR, 8), count * YR)


def nb_sum(x, count, cx, cy_ref, cz, v, step):
    at = span(x, count)
    here = v[at, :]
    cz = cz[span(x, count), :]
    total = cx[span(x, count), :] * v[span(x + 1, count), :]
    total = total + cx[span(x - 1, count), :] * v[span(x - 1, count), :]
    cy = cy_ref[at, :]
    total = total + (cy * ry(here, -1) + ry(cy * here, 1))
    return total + (cz * rl(here, -step) + rl(cz * here, step))


def steps(count):
    def run(step):
        for k in range(count):
            step(k)

    return run


def even_lane(rows):
    return (lane_of(rows) & 1) == 0


def red_rows(planes):
    row = lax.broadcasted_iota(jnp.int32, (YR, 128), 0)
    first = (row + lane_of(YR)) & 1
    return jnp.concatenate([first, 1 - first] * (planes // 2), axis=0) == 0


FC = 4
FS = 4
STEPS = 68 // FS


def zpair(s):
    return s + jnp.where(even_lane(s.shape[0]), rl(s, -1), rl(s, 1))


def halves(w):
    w = w.reshape(FC // 2, 2, YR, 128)
    return w[:, 0].reshape(FC // 2 * YR, 128), w[:, 1].reshape(FC // 2 * YR, 128)


def both(w):
    first, second = halves(w)
    return first + second


def mean_kernel(aa, bb, xlo, xhi, ta, tx, ty):
    tx[plane(0), :] = zpair(0.5 * (x_plane(2, 2, xlo) + bb[plane(3), :]))
    for i in range(32):
        x = 2 * i + 3
        first = bb[plane(x), :]
        second = bb[plane(x + 1), :]
        third = bb[plane(x + 2), :] if i < 31 else x_plane(2, 0, xhi)
        ta[plane(i), :] = zpair(aa[plane(x), :] + aa[plane(x + 1), :])
        tx[plane(i + 1), :] = zpair(0.5 * (second + third))
        ty[plane(i), :] = zpair(0.5 * (first + ry(first, -1)) + 0.5 * (second + ry(second, -1)))


def coefficient_kernel(
    rh0, aa0, bb0, xlo, xhi, zlo, zhi, ta, tx, ty, f, a, fx, fy, fz, c1, slo, shi, b, tz
):
    lane = lane_of(YR)
    for x in range(FXN):
        group, base = z_slot(x - 3 if 3 <= x < 67 else (64 + x if x < 3 else x))
        for n, (src, dst) in enumerate(((rh0, f), (aa0, a), (bb0, b))):
            d = DEPTH[n]
            if 3 <= x < 67:
                w = src[plane(x), :]
            elif 3 - d <= x < 3:
                w = x_plane(n, x - 3 + d, xlo)
            elif 67 <= x < 67 + d:
                w = x_plane(n, x - 67, xhi)
            else:
                dst[plane(x), :] = jnp.zeros((YR, 128), F32)
                continue
            at = base + FIRST[n]
            w = jnp.where(lane >= 128 - d, rl(zlo[group, :], -d - at), w)
            above = (lane >= 64) & (lane < 64 + d)
            dst[plane(x), :] = jnp.where(above, rl(zhi[group, :], 64 - at), w)

    def faces(x, count):
        here = b[span(x, count), :]
        fx[span(x, count), :] = 0.5 * (here + b[span(x + 1, count), :])
        fy[span(x, count), :] = 0.5 * (here + ry(here, -1))
        fz[span(x, count), :] = 0.5 * (here + rl(here, -1))

    faces(0, 1)

    @steps(STEPS)
    def _(k):
        faces(1 + k * FS, FS)

    nothing = jnp.zeros((YR, 128), F32)
    for ref in (fx, fy, fz):
        ref[plane(FXN - 1), :] = nothing
    @steps(64 // FC)
    def _(k):
        tz[span(k * (FC // 2), FC // 2), :] = both(fz[span(3 + k * FC, FC), :])

    @steps(8)
    def _(k):
        base = k * 4 * YR
        even = even_lane(80)

        def rows(ref, first, planes=0):
            return ref[every(base + planes * YR + first, 80, 2), :]

        acoef = 0.125 * (rows(ta, 0) + rows(ta, 1))
        fxp = 0.25 * (rows(tx, 0, 1) + rows(tx, 1, 1))
        fxm = 0.25 * (rows(tx, 0) + rows(tx, 1))
        fyp = 0.25 * rows(ty, 1)
        s = 0.25 * (rows(tz, 0) + rows(tz, 1))
        fzp = jnp.where(even, rl(s, -1), s)
        diag = acoef + 0.25 * (fxp + fxm + fyp + ry(fyp, 1) + fzp + rl(fzp, 2))
        pa = jnp.where(even, fxp, fyp)
        pb = jnp.where(even, fzp, diag)
        c1[pl.ds(k * 80, 80), :] = jnp.where(lane_of(80) < 64, pa, rl(pb, 64))

    for dst, y0 in ((slo, 2), (shi, 9)):
        for r in range(9):
            dst[plane(r, 32), :] = c1[every(y0 + r, 32, 20), :]


def presmooth_kernel(f, a, fx, fy, fz, ir, ib, dg, v, rc, slo, shi, tr, v0):
    for ref in (ir, ib, dg, v0):
        ref[plane(0), :] = jnp.zeros((YR, 128), F32)
        ref[plane(FXN - 1), :] = jnp.zeros((YR, 128), F32)

    red = red_rows(FS)

    @steps(STEPS)
    def _(k):
        x = 1 + k * FS
        at = span(x, FS)
        py = fy[at, :]
        pz = fz[at, :]
        ax = a[at, :]
        total = fx[at, :] + fx[span(x - 1, FS), :] + py + ry(py, 1) + pz + rl(pz, 1)
        diag = ax + total
        inside = ax > 0.0
        one = jnp.where(inside, 1.0 / jnp.where(inside, diag, 1.0), 0.0)
        dg[at, :] = diag
        ir[at, :] = jnp.where(red, one, 0.0)
        ib[at, :] = jnp.where(red, 0.0, one)
        v0[at, :] = jnp.where(red, f[at, :] * one, 0.0)

    for x in (0, FXN - 1):
        v[plane(x), :] = v0[plane(x), :]

    @steps(STEPS)
    def _(k):
        x = 1 + k * FS
        at = span(x, FS)
        new = (f[at, :] + nb_sum(x, FS, fx, fy, fz, v0, 1)) * ib[at, :]
        v[at, :] = v0[at, :] + new

    @steps(64 // FC)
    def _(k):
        x = 3 + k * FC
        at = span(x, FC)
        miss = f[at, :] - (dg[at, :] * v[at, :] - nb_sum(x, FC, fx, fy, fz, v, 1))
        tr[span(k * (FC // 2), FC // 2), :] = zpair(both(miss))

    @steps(8)
    def _(k):
        base = k * 4 * YR
        rhs = tr[every(base, 80, 2), :] + tr[every(base + 1, 80, 2), :]
        rc[pl.ds(k * 80, 80), :] = jnp.where(lane_of(80) < 64, 0.125 * rhs, 0.0)

    lane32 = lane_of(32)
    for dst, y0, fine0 in ((slo, 2, 0), (shi, 9, 29)):
        for r in range(9):
            w = rc[every(y0 + r, 32, 20), :]
            if r < 6:
                start = (3 + 32 * (r // 3)) * YR + FY0 + fine0 + r % 3
                w = jnp.where(lane32 < 64, w, rl(v[every(start, 32, YR), :], 64))
            dst[plane(r, 32), :] = w


def coarse_own(dst, src):
    dst[...] = jnp.zeros_like(dst)
    for i in range(32):
        dst[pl.ds((i + 9) * YR + CY0, 16), :] = src[pl.ds(i * 20 + 2, 16), :]


def coef_x_kernel(c1, ylo, yhi, ec, slo, shi):
    coarse_own(ec, c1)
    for src, crow in ((ylo, CY0 - 9), (yhi, CY0 + 16)):
        for r in range(9):
            ec[every(9 * YR + crow + r, 32, YR), :] = src[plane(r, 32), :]
    slo[...] = ec[pl.ds(9 * YR, 9 * YR), :]
    shi[...] = ec[pl.ds(32 * YR, 9 * YR), :]


def rhs_x_kernel(rc, v, ylo, yhi, er, vs, slo, shi):
    lane = lane_of(YR)
    coarse_own(er, rc)
    vs[...] = v[...]
    for src, crow, frow in ((ylo, CY0 - 9, FY0 - 3), (yhi, CY0 + 16, FY0 + 32)):
        for r in range(9):
            w = src[plane(r, 32), :]
            er[every(9 * YR + crow + r, 32, YR), :] = w
            if r < 6:
                start = (3 + 32 * (r // 3)) * YR + frow + r % 3
                vs[every(start, 32, YR), :] = own_lanes(rl(w, 64))
    for dst, first, fine in ((slo, 9, 3), (shi, 32, 64)):
        for i in range(9):
            w = er[plane(first + i), :]
            if i < 3:
                w = jnp.where(lane < 64, w, rl(own_lanes(vs[plane(fine + i), :]), 64))
            dst[plane(i), :] = w


def coef_slot(which, x):
    n = which * 50 + x
    return plane(n // 7), 18 * (n % 7)


def coef_z_kernel(ec0, xlo, xhi, ec, zlo, zhi):
    lane = lane_of(YR)
    ec[...] = ec0[...]
    ec[pl.ds(0, 9 * YR), :] = xlo[...]
    ec[pl.ds(41 * YR, 9 * YR), :] = xhi[...]
    lo = hi = None
    for n in range(100):
        at = 18 * (n % 7)
        if at == 0:
            lo = jnp.zeros((YR, 128), F32)
            hi = lo
        w = ec[plane(n % 50), :]
        base = 64 * (n // 50)
        here = (lane >= at) & (lane < at + 18)
        lo = jnp.where(here, rl(w, at - base), lo)
        hi = jnp.where(here, rl(w, at - base - 46), hi)
        if at == 108 or n == 99:
            zlo[plane(n // 7), :] = lo
            zhi[plane(n // 7), :] = hi


def smooth_slot(n):
    return plane(n // 12), 27 * (n // 3 % 4) + 18 + 3 * (n % 3)


def smooth_z_kernel(vs, zlo, zhi):
    lane = lane_of(YR)
    lo = hi = jnp.zeros((YR, 128), F32)
    zlo[plane(6), :] = lo
    zhi[plane(6), :] = lo
    for n in range(3, 67):
        group, to = smooth_slot(n)
        if n % 12 == 0:
            lo = hi = jnp.zeros((YR, 128), F32)
        w = vs[plane(n), :]
        here = (lane >= to) & (lane < to + 3)
        lo = jnp.where(here, rl(w, to), lo)
        hi = jnp.where(here, rl(w, to - 61), hi)
        if n % 12 == 11 or n == 66:
            zlo[group, :] = lo
            zhi[group, :] = hi


def rhs_z_kernel(er, xlo, xhi, plo, phi, rm, zlo, zhi):
    lane = lane_of(YR)
    even = even_lane(YR)
    own = lane < 64
    lo = hi = None
    for n in range(25):
        at = 27 * (n % 4)
        if at == 0:
            lo = plo[plane(n // 4), :]
            hi = phi[plane(n // 4), :]
        first = xlo[plane(n), :] if n < 9 else er[plane(n), :]
        second = xhi[plane(n - 16), :] if n >= 16 else er[plane(n + 25), :]
        w = jnp.where(even, first, second)
        rm[plane(n), :] = jnp.where(own, w, 0.0)
        here = (lane >= at) & (lane < at + 18)
        lo = jnp.where(here, rl(w, at), lo)
        hi = jnp.where(here, rl(w, at - 46), hi)
        for m in range(3 * n, 3 * n + 3):
            if m < 3 or 67 <= m < FXN:
                w = rl((xlo if m < 3 else xhi)[plane(m if m < 3 else m - 67), :], 64)
                to = smooth_slot(m)[1]
                here = (lane >= to) & (lane < to + 3)
                lo = jnp.where(here, rl(w, to), lo)
                hi = jnp.where(here, rl(w, to - 61), hi)
        if at == 81 or n == 24:
            zlo[plane(n // 4), :] = lo
            zhi[plane(n // 4), :] = hi


MXN = 28
CC = 1


def merge_own_kernel(ec, ox, oy, oz, od):
    even = even_lane(YR)

    def load(which, x):
        if not 0 <= x < CXN:
            return jnp.zeros((YR, 128), F32)
        return rl(ec[plane(x), :], 64 * which)

    for p in range(27):
        for which, (low, high) in enumerate(((ox, oy), (oz, od))):
            first, second = load(which, p - 1), load(which, p + 24)
            low[plane(p), :] = jnp.where(even, first, rl(second, 1))
            high[plane(p), :] = jnp.where(even, rl(first, -1), second)


def merge_kernel(ox, oy, oz, od, zlo, zhi, cx, cy, cz, jr, jb):
    lane = lane_of(YR)
    even = even_lane(YR)
    own = lane < 64
    below = lane >= 110
    above = (lane >= 64) & (lane < 82)
    nothing = jnp.zeros((YR, 128), F32)
    row = lax.broadcasted_iota(jnp.int32, (YR, 128), 0)
    reds = ((row + (lane >> 1) + jnp.where(even, 0, 1)) & 1) == 0

    def load(which, x):
        if not 0 <= x < CXN:
            return nothing
        group, at = coef_slot(which, x)
        w = jnp.where(below, rl(zlo[group, :], -18 - at), 0.0)
        return jnp.where(above, rl(zhi[group, :], 64 - at), w)

    for p in range(27):
        first, second = load(0, p - 1), load(0, p + 24)
        w = jnp.where(even, first, rl(second, 1))
        cx[plane(p), :] = 0.25 * jnp.where(own, ox[plane(p), :], w)
        w = jnp.where(even, rl(first, -1), second)
        cy[plane(p), :] = 0.25 * jnp.where(own, oy[plane(p), :], w)
        first, second = load(1, p - 1), load(1, p + 24)
        w = jnp.where(even, first, rl(second, 1))
        cz[plane(p), :] = 0.25 * jnp.where(own, oz[plane(p), :], w)
        diag = jnp.where(own, od[plane(p), :], jnp.where(even, rl(first, -1), second))
        inside = diag > 0.0
        one = jnp.where(inside, 1.0 / jnp.where(inside, diag, 1.0), 0.0)
        mine, other = (jr, jb) if p % 2 == 0 else (jb, jr)
        mine[plane(p), :] = jnp.where(reds, one, 0.0)
        other[plane(p), :] = jnp.where(reds, 0.0, one)
    for ref in (cx, cy, cz, jr, jb):
        ref[plane(27), :] = nothing


def finish_kernel(
    rm, vs, xlo, xhi, zlo, zhi, cx, cy, cz, jr, jb, f, fx, fy, fz, ir, ib, dg, out, res, cf, red, blk, v, w0, tmp
):
    lane = lane_of(YR)
    even = even_lane(YR)
    below = lane >= 110
    above = (lane >= 64) & (lane < 82)
    nothing = jnp.zeros((YR, 128), F32)
    for ref in (cf, red, blk):
        for p in (0, 26, 27):
            ref[plane(p), :] = nothing
    for n in range(25):
        at = 27 * (n % 4)
        w = jnp.where(below, rl(zlo[plane(n // 4), :], -18 - at), rm[plane(n), :])
        w = jnp.where(above, rl(zhi[plane(n // 4), :], 64 - at), w)
        cf[plane(n + 1), :] = w
        red[plane(n + 1), :] = w * jr[plane(n + 1), :]
    for n in range(FXN):
        group, at = smooth_slot(n)
        if n < 3:
            w = rl(xlo[plane(n), :], 64)
        elif n >= 67:
            w = rl(xhi[plane(n - 67), :], 64)
        else:
            w = vs[plane(n), :]
        w = own_lanes(w)
        low = rl(zlo[group, :], -3 - at)
        high = rl(zhi[group, :], 64 - at)
        w = jnp.where(lane >= 125, low, w)
        v[plane(n), :] = jnp.where((lane >= 64) & (lane < 67), high, w)

    def seam(ref):
        ref[plane(26), :] = jnp.where(even, rl(ref[plane(1), :], -1), 0.0)
        ref[plane(0), :] = jnp.where(even, 0.0, rl(ref[plane(25), :], 1))

    seam(red)

    for half in range(1, 8):
        src, dst, inv = (red, blk, jb) if half % 2 else (blk, red, jr)

        @steps(26 // CC)
        def _(k):
            x = 1 + k * CC
            at = span(x, CC)
            dst[at, :] = (cf[at, :] + nb_sum(x, CC, cx, cy, cz, src, 2)) * inv[at, :]

        seam(dst)

    for i in range(-2, 34):
        p = i + 10 if i + 9 < 25 else i + 9 - 24
        c = red[plane(p), :] + blk[plane(p), :]
        c = jnp.where(even, c, rl(c, 1)) if i + 9 < 25 else jnp.where(even, rl(c, -1), c)
        c = c[CY0 - 2 : CY0 + 18]
        slot = (i % 8) * YR
        tmp[every(slot, 20, 2), :] = c
        tmp[every(slot + 1, 20, 2), :] = c
        spread = tmp[pl.ds(slot, YR), :]
        for x in (2 * i + 3, 2 * i + 4):
            if 0 <= x < FXN:
                v[plane(x), :] = v[plane(x), :] + spread

    w0[plane(0), :] = nothing
    w0[plane(FXN - 1), :] = nothing

    @steps(STEPS)
    def _(k):
        x = 1 + k * FS
        at = span(x, FS)
        w0[at, :] = (f[at, :] + nb_sum(x, FS, fx, fy, fz, v, 1)) * ir[at, :]

    @steps(STEPS)
    def _(k):
        x = 1 + k * FS
        at = span(x, FS)
        new = (f[at, :] + nb_sum(x, FS, fx, fy, fz, w0, 1)) * ib[at, :]
        v[at, :] = new + w0[at, :]

    def crop(w):
        return w.reshape(FC, YR, 128)[:, FY0 : FY0 + 32, :64]

    @steps(64 // FC)
    def _(k):
        x = 3 + k * FC
        at = span(x, FC)
        w = v[at, :]
        r = f[at, :] - (dg[at, :] * w - nb_sum(x, FC, fx, fy, fz, v, 1))
        out[pl.ds(k * FC, FC)] = crop(w)
        res[pl.ds(k * FC, FC)] = crop(r)


def swap(low, high, axis):
    count = lax.axis_size(axis)
    up = [(i, i + 1) for i in range(count - 1)]
    down = [(i + 1, i) for i in range(count - 1)]
    return lax.ppermute(high, axis, up), lax.ppermute(low, axis, down)


def body(rhs_boxes, a_boxes, b_boxes, new_place):
    exchange = functools.partial(
        lax.all_to_all, axis_name=LAYER, split_axis=0, concat_axis=0, tiled=True
    )
    hbm = pl.BlockSpec(memory_space=pltpu.HBM)
    spread = pl.pallas_call(
        spread_kernel,
        out_shape=jax.ShapeDtypeStruct((32 * 97, 128), F32),
        in_specs=[hbm] * 4,
        out_specs=pl.BlockSpec(memory_space=pltpu.VMEM),
        scratch_shapes=[
            pltpu.VMEM((3, 4, 32768), F32),
            pltpu.SMEM((1, 4), jnp.int32),
            pltpu.SemaphoreType.DMA((13,)),
        ],
        compiler_params=pltpu.CompilerParams(vmem_limit_bytes=8 << 20),
    )(
        *(
            pltpu.with_memory_space_constraint(w, pltpu.HBM)
            for w in (new_place, rhs_boxes, a_boxes, b_boxes)
        )
    )
    got = exchange(spread.reshape(32, 1, 97 * 128)).reshape(32 * 97, 128)
    vmem = pl.BlockSpec(memory_space=pltpu.VMEM)
    routed = pl.pallas_call(
        route_kernel,
        out_shape=jax.ShapeDtypeStruct((32, 12, 8, 128), F32),
        in_specs=[vmem],
        out_specs=vmem,
        scratch_shapes=[
            pltpu.VMEM((32, 128), jnp.int32),
            pltpu.SMEM((32, 128), jnp.int32),
            pltpu.SemaphoreType.DMA((1,)),
        ],
        compiler_params=pltpu.CompilerParams(vmem_limit_bytes=8 << 20),
    )(got)
    got = exchange(routed)

    fine = (FXN * YR, 128)
    coarse = (CXN * YR, 128)
    ylo, yhi = call(strip_kernel, [(7 * 32, 128)] * 2, us=1)(got.reshape(3072, 128))
    ylo, yhi = swap(ylo, yhi, "gy")
    rh, aa, bb, xlo, xhi = call(brick_kernel, [fine] * 3 + [(7 * YR, 128)] * 2, us=4)(got)
    xlo, xhi = call(fine_x_kernel, [(4 * YR, 128)] * 2, [(7 * YR, 128)] * 2, us=1)(
        xlo, xhi, ylo, yhi
    )
    xlo, xhi = swap(xlo, xhi, "gx")
    rh, aa, bb, zlo, zhi = call(fine_y_kernel, [fine] * 3 + [(4 * YR, 128)] * 2)(
        rh, aa, bb, ylo, yhi
    )
    zlo, zhi = call(fine_z_kernel, [(4 * YR, 128)] * 2, us=1)(zlo, zhi, xlo, xhi)
    zlo, zhi = swap(zlo, zhi, "gz")
    means = call(mean_kernel, [(33 * YR, 128)] * 3)(aa, bb, xlo, xhi)
    f, a, fx, fy, fz, c1, cylo, cyhi = call(
        coefficient_kernel,
        [fine] * 5 + [(640, 128)] + [(9 * 32, 128)] * 2,
        [fine, (33 * YR, 128)],
        us=4,
    )(rh, aa, bb, xlo, xhi, zlo, zhi, *means)
    cylo, cyhi = swap(cylo, cyhi, "gy")
    ir, ib, dg, v, rc, ylo, yhi = call(
        presmooth_kernel,
        [fine] * 4 + [(640, 128)] + [(9 * 32, 128)] * 2,
        [(32 * YR, 128), fine],
        us=6,
    )(f, a, fx, fy, fz)
    cylo, cyhi, rc = lax.optimization_barrier((cylo, cyhi, rc))
    ylo, yhi = swap(ylo, yhi, "gy")
    ec, cxlo, cxhi = call(coef_x_kernel, [coarse] + [(9 * YR, 128)] * 2, us=1)(c1, cylo, cyhi)
    cxlo, cxhi = swap(cxlo, cxhi, "gx")
    er, vs, xlo, xhi = call(rhs_x_kernel, [coarse, fine] + [(9 * YR, 128)] * 2, us=1)(
        rc, v, ylo, yhi
    )
    xlo, xhi = swap(xlo, xhi, "gx")
    ec, czlo, czhi = call(coef_z_kernel, [coarse] + [(15 * YR, 128)] * 2)(ec, cxlo, cxhi)
    czlo, czhi = swap(czlo, czhi, "gz")
    owned = call(merge_own_kernel, [(MXN * YR, 128)] * 4)(ec)
    plo, phi = call(smooth_z_kernel, [(7 * YR, 128)] * 2)(vs)
    plo, *owned = lax.optimization_barrier((plo, *owned))
    rm, zlo, zhi = call(rhs_z_kernel, [(25 * YR, 128)] + [(7 * YR, 128)] * 2, us=1)(
        er, xlo, xhi, plo, phi
    )
    rxlo, rxhi = xlo, xhi
    zlo, zhi = swap(zlo, zhi, "gz")
    merged = (MXN * YR, 128)
    coefs = call(merge_kernel, [merged] * 5, us=5)(*owned, czlo, czhi)
    return tuple(
        call(
            finish_kernel,
            [(64, 32, 64)] * 2,
            [merged] * 3 + [fine, fine, (8 * YR, 128)],
            us=8,
        )(rm, vs, rxlo, rxhi, zlo, zhi, *coefs, f, fx, fy, fz, ir, ib, dg)
    )


def solution(mesh):
    return jax.shard_map(
        body,
        mesh=mesh,
        in_specs=(
            P("gz", ("gx", "gy"), None),
            P("gz", ("gx", "gy"), None),
            P("gz", ("gx", "gy"), None),
            P("gz", ("gx", "gy")),
        ),
        out_specs=(P("gx", "gy", "gz"), P("gx", "gy", "gz")),
        check_vma=False,
    )
```
